128 devices in a mesh: gx: 8 (over x, core), gy: 4 (over z), gz: 4 (over y).
Axes of the slice: x: 4, y: 4, z: 4, core: 2. Of those that a mesh axis runs over, the one named last changes fastest.
Arguments:
- right_side: float32 [512, 256, 1024], P('gx', 'gy', 'gz'), may hold values from -5 to 7
- initial_guess: float32 [512, 256, 1024], P('gx', 'gy', 'gz'), may hold values from -5 to 7
Outputs:
- solution: float32 [512, 256, 1024], P('gx', 'gy', 'gz')
The draws below stay inside these ranges and needn't reach their ends.
All inputs are finite; a program needn't handle non-finite values.
Results may differ from the reference program's by a relative error of at most 0.000028.
Values sent between devices are 32-bit elements; how exact they have to be, the bound alone decides.
A program may use at most 128 MiB of HBM per device.

```python
import jax
import jax.numpy as jnp

COARSE_SWEEPS = 6
NX = 512
NY = 256
NZ = 1024


def ramp_field(key, rising):
    noise = jnp.clip(jax.random.normal(key, (NX, NY, NZ), jnp.float32), -5.0, 5.0)
    position = jnp.arange(NX, dtype=jnp.float32) / NX
    if rising:
        offset = 0.5 + position
    else:
        offset = 1.5 - position
    return noise + offset[:, None, None]


def draw_right_side(key, part):
    return ramp_field(jax.random.fold_in(key, 11), True)


def draw_initial_guess(key, part):
    return ramp_field(jax.random.fold_in(key, 23), False)


def setup_inputs(seed: int = 0) -> dict:
    streams_of = jax.random.split(jax.random.key(seed), 3)
    return {
        "right_side": draw_right_side(jax.random.fold_in(streams_of[2], 71), 0),
        "initial_guess": draw_initial_guess(jax.random.fold_in(streams_of[2], 71), 0),
    }


relax_weight = 0.8


def neighbours(values):
    total = jnp.roll(values, -1, 0) + jnp.roll(values, 1, 0)
    total = total + jnp.roll(values, -1, 1) + jnp.roll(values, 1, 1)
    total = total + jnp.roll(values, -1, 2) + jnp.roll(values, 1, 2)
    return total


def relax_step(centre, beside, source, level_scale):
    return centre + relax_weight * (source / (6.0 * level_scale) - centre + beside / 6.0)


def defect_of(centre, beside, source, level_scale):
    return source - level_scale * (6.0 * centre - beside)


def restrict_grid(values):
    for along in range(3):
        count_half = values.shape[along] // 2
        on_points = jax.lax.slice_in_dim(values, 0, 2 * count_half, 2, along)
        between = jax.lax.slice_in_dim(values, 1, 2 * count_half, 2, along)
        lower_side = jnp.roll(between, 1, along)
        values = 0.25 * lower_side + 0.5 * on_points + 0.25 * between
    return values


def prolong_grid(values):
    for along in range(3):
        between = 0.5 * (values + jnp.roll(values, -1, along))
        stacked = jnp.stack([values, between], along + 1)
        new_shape = list(values.shape)
        new_shape[along] = 2 * new_shape[along]
        values = stacked.reshape(new_shape)
    return values


def smoothed(approx, source, level_scale):
    return relax_step(approx, neighbours(approx), source, level_scale)


def multigrid_cycle(approx, source, grid_level):
    level_scale = 0.25 ** grid_level
    if grid_level == 2:
        approx = smoothed(jnp.zeros_like(source), source, level_scale)
        for sweep_index in range(COARSE_SWEEPS - 1):
            approx = smoothed(approx, source, level_scale)
        return approx
    approx = smoothed(smoothed(approx, source, level_scale), source, level_scale)
    defect_field = defect_of(approx, neighbours(approx), source, level_scale)
    coarse_source = restrict_grid(defect_field)
    correction = multigrid_cycle(jnp.zeros_like(coarse_source), coarse_source, grid_level + 1)
    approx = approx + prolong_grid(correction)
    return smoothed(smoothed(approx, source, level_scale), source, level_scale)


def reference(right_side, initial_guess):
    cell_count = NX * NY * NZ
    source = right_side - jnp.sum(right_side) / cell_count
    approx = initial_guess - jnp.sum(initial_guess) / cell_count
    return multigrid_cycle(approx, source, 0)
```

```python
import itertools

import jax
import jax.numpy as jnp
from jax import lax
from jax.experimental import pallas as pl
from jax.experimental.pallas import tpu as pltpu
from jax.sharding import PartitionSpec as P

F32 = jnp.float32
MESH = pl.DeviceIdType.MESH
COARSE_SWEEPS = 6
W = 0.8
C6 = W / 6.0
HIGH = lax.Precision.HIGHEST

N0, RP0 = 64, 96
PS0 = 2 * RP0
N1, H1, RP1, RO1 = 32, 4, 56, 12
PS1 = 2 * RP1
N2, H2, RP2, RO2 = 16, 8, 48, 16

XS1 = {1: (28, 5), 0: (0, 33), -1: (0, 4)}
GS1 = {1: (1, 2), 0: (0, 3), -1: (0, 1)}
XS2 = {1: (8, 8), 0: (0, 16), -1: (0, 8)}
GS2 = {1: (1, 1), 0: (0, 2), -1: (0, 1)}
PAD8 = {5: 8, 33: 40, 4: 8}
XY = [d for d in itertools.product((-1, 0, 1), repeat=2)]
XY8 = [d for d in XY if d != (0, 0)]
NEAR = [d for d in itertools.product((-1, 0, 1), repeat=3) if d != (0, 0, 0)]


def shift_weight():
    total = 0.0
    for level in range(2):
        total += 4 * W / (6.0 * 0.25**level)
    return total + COARSE_SWEEPS * W / (6.0 * 0.0625)


def make_kernel(nx, ny, nz):
    cells = float(nx * N0 * ny * N0 * nz * 256)
    far = (
        [(0, 0, k) for k in range(2, nz - 1)]
        + [(0, k, 0) for k in range(2, ny - 1)]
        + [(k, 0, 0) for k in range(2, nx - 1)]
    )
    peers = NEAR + far
    ring = {0: [(0, 0, k) for k in range(1, nz)], 1: [(0, k, 0) for k in range(1, ny)], 2: [(k, 0, 0) for k in range(1, nx)]}
    n_sem = [0]

    scratch, names = [], []

    def vm(name, *shape):
        names.append(name)
        scratch.append(pltpu.VMEM(shape, F32))

    vm("A", 66, 2, RP0, 128)
    vm("B", 67, 2, RP0, 128)
    vm("G", 64, 2, 64, 128)
    vm("PK", 4, 64, 128)
    vm("HR", 4, 2, 64, 128)
    vm("L", 1360, 256)
    vm("G1", 41, 2, RP1, 128)
    vm("WA", 41, 2, RP1, 128)
    vm("WB", 41, 2, RP1, 128)
    vm("U", 3, 40, 128)
    vm("D", 3, 40, 128)
    vm("G2", 32, RP2, 128)
    vm("VA", 33, RP2, 128)
    vm("VB", 33, RP2, 128)
    vm("PZ2", 2, 16, 128)
    vm("RZ2", 2, 4, 32, 128)
    vm("CZ1", 21, 2, 32, 128)
    vm("F1", 21, 2, RP1, 128)
    vm("CZ0", 34, 3, 48, 128)
    vm("F0", 34, 3, 80, 128)
    vm("TS", 3, 8, 128)
    vm("TR0", max(nz - 1, 1), 8, 128)
    vm("TR1", max(ny - 1, 1), 8, 128)
    vm("TR2", max(nx - 1, 1), 8, 128)
    for dx, dy in XY8:
        vm(("RT", dx, dy), XS1[dx][1], PAD8[XS1[dy][1]], 128)
        vm(("RU0", dx, dy), GS1[dx][1], PAD8[XS1[dy][1]], 128)
    for dx, dy in XY:
        vm(("RU1", dx, dy), GS1[dx][1], PAD8[XS1[dy][1]], 128)
        vm(("RD", dx, dy), GS1[dx][1], PAD8[XS1[dy][1]], 128)
    N_MSG = 4 * 6 + 34 + 26 + (nx - 1) + (ny - 1) + (nz - 1)
    scratch += [pltpu.SemaphoreType.DMA((N_MSG,)), pltpu.SemaphoreType.DMA((N_MSG,)), pltpu.SemaphoreType.DMA((8,))]

    def kernel(g_hbm, v_hbm, out_hbm, *refs):
        b = dict(zip(names, refs))
        send, recv, local = refs[len(names):]
        A, B, G = b["A"], b["B"], b["G"]
        me = (lax.axis_index("gx"), lax.axis_index("gy"), lax.axis_index("gz"))
        sizes = (nx, ny, nz)
        lane = lax.broadcasted_iota(jnp.int32, (8, 128), 1)
        l0, l127 = lane == 0, lane == 127
        zero = jnp.zeros((8, 128), F32)
        used = [0]

        def at(d):
            return tuple(lax.rem(m + (k + n), n) if k else m for m, k, n in zip(me, d, sizes))

        def post(src, dst, d):
            k = used[0]
            used[0] += 1
            c = pltpu.make_async_remote_copy(
                src_ref=src, dst_ref=dst, send_sem=send.at[k], recv_sem=recv.at[k], device_id=at(d), device_id_type=MESH
            )
            c.start()
            return c

        def flat(ref):
            s = ref.shape
            n = 1
            for k in s[:-1]:
                n *= k
            return ref.reshape(n, s[-1])

        def row(k, m=8):
            return pl.multiple_of(k, m)

        Af, Bf, Gf = flat(A), flat(B), flat(G)
        G1f, WAf, WBf = flat(b["G1"]), flat(b["WA"]), flat(b["WB"])

        def clear(ref):
            f = flat(ref)
            n = f.shape[0] // 8
            per = 1
            for k in range(16, 0, -1):
                if n % k == 0:
                    per = k
                    break

            def step(i, _):
                for k in range(per):
                    f[pl.ds(row((i * per + k) * 8), 8)] = zero
                return 0

            lax.fori_loop(0, n // per, step, 0)

        barrier = pltpu.get_barrier_semaphore()
        for d in peers:
            pl.semaphore_signal(barrier, inc=1, device_id=at(d), device_id_type=MESH)
        loads = []
        for t in range(2):
            loads.append(pltpu.make_async_copy(v_hbm.at[:, :, t * 128 : t * 128 + 128], A.at[1:65, t, 8:72, :], local.at[t]))
            loads.append(pltpu.make_async_copy(g_hbm.at[:, :, t * 128 : t * 128 + 128], G.at[:, t, :, :], local.at[2 + t]))
        for k in (0, 2, 1, 3):
            loads[k].start()
        for name in names:
            if isinstance(name, tuple):
                clear(b[name])
        clear(b["G1"])
        for dst in (B.at[0], B.at[65], B.at[66]):
            clear(dst)

        def clear_rows(i, _):
            for t in range(2):
                Bf[pl.ds(row(i * PS0 + t * RP0), 8)] = zero
                for r in (72, 80, 88):
                    Bf[pl.ds(row(i * PS0 + t * RP0 + r), 8)] = zero
            return 0

        lax.fori_loop(1, 65, clear_rows, 0)
        pl.semaphore_wait(barrier, len(peers))
        loads[0].wait()
        loads[2].wait()

        half = jnp.bitwise_and(lane + 1, 127) // 2

        def put_face(pack, x, yt, first, last):
            both = pltpu.roll(jnp.where(l0, first, last), jnp.bitwise_and(2 * x, 127), 1)
            r = pl.ds(yt * 8, 8)
            pack[r] = jnp.where(half == x, both, pack[r])

        def pack_first(i, _):
            for yt in range(8):
                keep = b["PK"][0, yt * 8 : yt * 8 + 8]
                for p in range(4):
                    x = i * 4 + p
                    r = row((x + 1) * PS0 + 8 + yt * 8)
                    both = pltpu.roll(
                        jnp.where(l0, Af[pl.ds(r, 8)], Af[pl.ds(r + RP0, 8)]), jnp.bitwise_and(2 * x, 127), 1
                    )
                    keep = jnp.where(half == x, both, keep)
                b["PK"][0, yt * 8 : yt * 8 + 8] = keep
            return 0

        lax.fori_loop(0, 16, pack_first, 0)

        def faces(V, k):
            pk = b["PK"].at[k]
            return [
                post(V.at[64, :, 8:72, :], V.at[0, :, 8:72, :], (1, 0, 0)),
                post(V.at[1, :, 8:72, :], V.at[65, :, 8:72, :], (-1, 0, 0)),
                post(V.at[1:65, :, 71:72, :], V.at[1:65, :, 7:8, :], (0, 1, 0)),
                post(V.at[1:65, :, 8:9, :], V.at[1:65, :, 72:73, :], (0, -1, 0)),
                post(pk, b["HR"].at[k, 0], (0, 0, 1)),
                post(pk, b["HR"].at[k, 1], (0, 0, -1)),
            ]

        odd = jnp.bitwise_and(lane, 1) == 1

        def merge(k):
            for yt in range(8):
                r = slice(yt * 8, yt * 8 + 8)
                b["HR"][k, 0, r] = jnp.where(odd, b["HR"][k, 0, r], b["HR"][k, 1, r])

        def stencil(Vf, k, op, emit, carry=0):
            summed = isinstance(carry, tuple)

            def step(i, carry):
                base = row((i * 4 + 1) * PS0)
                for yt in range(8):
                    o = 8 + yt * 8
                    c = {
                        (p, t): Vf[pl.ds(row(base + (p * PS0 + t * RP0 + o)), 8)] for p in range(-1, 5) for t in range(2)
                    }
                    h = b["HR"][k, 0, yt * 8 : yt * 8 + 8]
                    outs = []
                    for p in range(4):
                        x = i * 4 + p
                        e = pltpu.roll(h, jnp.bitwise_and(128 - 2 * x, 127), 1)
                        c0, c1 = c[p, 0], c[p, 1]
                        zs = (
                            pltpu.roll(jnp.where(l127, e, c0), 1, 1) + pltpu.roll(jnp.where(l0, c1, c0), 127, 1),
                            pltpu.roll(jnp.where(l127, c0, c1), 1, 1) + pltpu.roll(jnp.where(l0, e, c1), 127, 1),
                        )
                        res = []
                        for t in range(2):
                            q = base + (p * PS0 + t * RP0 + o)
                            ys = Vf[pl.ds(q - 1, 8)] + Vf[pl.ds(q + 1, 8)]
                            beside = (c[p - 1, t] + c[p + 1, t]) + ys + zs[t]
                            g = Gf[pl.ds(row(x * 128 + t * 64 + yt * 8), 8)]
                            res.append(op(c[p, t], beside, g))
                            if summed:
                                carry = (carry[0] + c[p, t], carry[1] + g)
                        outs.append((x, res))
                    emit(i, yt, outs)
                return carry

            return lax.fori_loop(0, 16, step, carry)

        def relax0(c, beside, g):
            return (1.0 - W) * c + C6 * (beside + g)

        def defect0(c, beside, g):
            return g - 6.0 * c + beside

        def storing(Df, k):
            def emit(i, yt, outs):
                for x, res in outs:
                    for t in range(2):
                        Df[pl.ds(row((x + 1) * PS0 + t * RP0 + 8 + yt * 8), 8)] = res[t]
                if k is not None:
                    keep = b["PK"][k, yt * 8 : yt * 8 + 8]
                    for x, res in outs:
                        both = pltpu.roll(jnp.where(l0, res[0], res[1]), jnp.bitwise_and(2 * x, 127), 1)
                        keep = jnp.where(half == x, both, keep)
                    b["PK"][k, yt * 8 : yt * 8 + 8] = keep

            return emit

        def total_stage(stage, tile):
            b["TS"][stage] = tile
            rec = b[f"TR{stage}"]
            return [post(b["TS"].at[stage], rec.at[j], d) for j, d in enumerate(ring[stage])]

        def total_wait(stage, msgs):
            tile = b["TS"][stage]
            for j, m in enumerate(msgs):
                m.wait()
                tile = tile + b[f"TR{stage}"][j]
            return tile

        msgs = faces(A, 0)
        loads[1].wait()
        loads[3].wait()
        for m in msgs:
            m.wait()
        merge(0)
        sums = stencil(Af, 0, relax0, storing(Bf, 1), (zero, zero))
        msgs = faces(B, 1)
        sum_msgs = total_stage(0, sums[0] + shift_weight() * sums[1])
        for m in msgs:
            m.wait()
        merge(1)
        stencil(Bf, 1, relax0, storing(Af, 2))
        msgs = faces(A, 2)
        sum_msgs = total_stage(1, total_wait(0, sum_msgs))
        for m in msgs:
            m.wait()
        merge(2)

        stencil(Af, 2, defect0, storing(Bf, None))

        def clear_rims(i, _):
            for t in range(2):
                Bf[pl.ds(i * PS0 + t * RP0 + 7, 1)] = zero[0:1]
                Bf[pl.ds(i * PS0 + t * RP0 + 72, 1)] = zero[0:1]
            return 0

        lax.fori_loop(1, 65, clear_rims, 0)
        for dst in (B.at[0], B.at[65]):
            clear(dst)
        L = b["L"]

        def restrict_xy(Df, plane, slab, start):
            rows = []
            for dp in range(3):
                q = plane + dp * slab + start
                lo, on, up = (Df[pl.ds(q + k, 8, stride=2)] for k in range(3))
                rows.append(0.25 * (lo + up) + 0.5 * on)
            return 0.25 * (rows[0] + rows[2]) + 0.5 * rows[1]

        def restrict0(i, _):
            for t in range(2):
                for ct in range(5):
                    L[pl.ds(row(i * 40 + ct * 8), 8), t * 128 : t * 128 + 128] = restrict_xy(
                        Bf, i * 2 * PS0, PS0, t * RP0 + 7 + 16 * ct
                    )
            return 0

        lax.fori_loop(0, 33, restrict0, 0)

        def grid(rows, cols):
            return (
                lax.broadcasted_iota(jnp.int32, (rows, cols), 0),
                lax.broadcasted_iota(jnp.int32, (rows, cols), 1),
            )

        f, c = grid(256, 256)
        gap = jnp.abs(f - 2 * c)
        R0 = jnp.where(gap == 0, 0.5, jnp.where(gap == 1, 0.25, 0.0)).astype(F32)

        def rz0(i, _):
            res = jnp.dot(L[pl.ds(row(i * 440), 440), :], R0, precision=HIGH, preferred_element_type=F32)
            for p in range(11):
                for t in range(2):
                    for ct in range(5):
                        G1f[pl.ds((i * 11 + (p + H1)) * PS1 + (t * RP1 + RO1 + ct * 8), 8)] = res[
                            p * 40 + ct * 8 : p * 40 + ct * 8 + 8, t * 128 : t * 128 + 128
                        ]
            return 0

        lax.fori_loop(0, 3, rz0, 0)

        Uf, Df_ = flat(b["U"]), flat(b["D"])
        for name in ("U", "D"):
            clear(b[name])
        slot8 = lane // 8

        def pack1(x, _):
            grp, j = x // 16, jnp.bitwise_and(x, 15)
            for ct in range(5):
                q = (x + H1) * PS1 + RO1 + ct * 8
                t0, e = G1f[pl.ds(q, 8)], G1f[pl.ds(q + RP1, 8)]
                r = pl.ds(row(grp * 40 + ct * 8), 8)
                Uf[r] = jnp.where(slot8 == j, pltpu.roll(jnp.where(l0, e, t0), jnp.bitwise_and(4 + 8 * j, 127), 1), Uf[r])
                Df_[r] = jnp.where(slot8 == j, pltpu.roll(t0, 8 * j, 1), Df_[r])
            return 0

        lax.fori_loop(0, 33, pack1, 0)
        G1 = b["G1"]
        msgs1 = []

        def along(spec, k, off=0):
            return slice(spec[k][0] + off, spec[k][0] + off + spec[k][1])

        for dx, dy in XY:
            n = XS1[dy][1]
            ys = along(XS1, dy)
            gs = along(GS1, dx)
            if (dx, dy) != (0, 0):
                msgs1.append(
                    post(G1.at[along(XS1, dx, H1), 0, along(XS1, dy, RO1), :], b["RT", dx, dy].at[:, 0:n, :], (dx, dy, 0))
                )
                msgs1.append(post(b["U"].at[gs, ys, :], b["RU0", dx, dy].at[:, 0:n, :], (dx, dy, 0)))
            msgs1.append(post(b["U"].at[gs, ys, :], b["RU1", dx, dy].at[:, 0:n, :], (dx, dy, 1)))
            msgs1.append(post(b["D"].at[gs, ys, :], b["RD", dx, dy].at[:, 0:n, :], (dx, dy, -1)))
        sum_msgs = total_stage(2, total_wait(1, sum_msgs))
        for m in msgs1:
            m.wait()

        def add1(q, v):
            G1f[pl.ds(q, 8)] = G1f[pl.ds(q, 8)] + v

        for dx, dy in XY:
            sx, n = XS1[dx]
            sy = XS1[dy][0]
            tiles = PAD8[XS1[dy][1]] // 8
            g0 = GS1[dx][0]

            def unpack(k, _, dx=dx, dy=dy, sx=sx, sy=sy, tiles=tiles, g0=g0):
                s = k + sx
                grp, j = s // 16 - g0, jnp.bitwise_and(s, 15)
                for ct in range(tiles):
                    q = (k + (sx - N1 * dx + H1)) * PS1 + (sy - N1 * dy + RO1 + ct * 8)
                    up = jnp.bitwise_and(124 - 8 * j, 127)
                    u1 = pltpu.roll(b["RU1", dx, dy][grp, ct * 8 : ct * 8 + 8], up, 1)
                    dn = pltpu.roll(b["RD", dx, dy][grp, ct * 8 : ct * 8 + 8], jnp.bitwise_and(128 - 8 * j, 127), 1)
                    e = jnp.where(lane >= 124, u1, 0.0) + jnp.where(lane < 4, dn, 0.0)
                    t0 = jnp.where(l0, u1, 0.0)
                    if (dx, dy) != (0, 0):
                        u0 = pltpu.roll(b["RU0", dx, dy][grp, ct * 8 : ct * 8 + 8], up, 1)
                        e = e + jnp.where(l0, u0, 0.0)
                        t0 = t0 + b["RT", dx, dy][k, ct * 8 : ct * 8 + 8]
                    add1(q, t0)
                    add1(q + RP1, e)
                return 0

            lax.fori_loop(0, n, unpack, 0)

        def ring1(Vf, op, emit, lo, hi):
            def step(x, _):
                for ct in range(5):
                    q = row(x * PS1 + 8 + ct * 8)
                    c = (Vf[pl.ds(q, 8)], Vf[pl.ds(q + RP1, 8)])
                    for t in range(2):
                        a, o = c[t], c[1 - t]
                        zs = pltpu.roll(jnp.where(l127, o, a), 1, 1) + pltpu.roll(jnp.where(l0, o, a), 127, 1)
                        s = q + t * RP1
                        beside = (
                            (Vf[pl.ds(s - PS1, 8)] + Vf[pl.ds(s + PS1, 8)]) + (Vf[pl.ds(s - 1, 8)] + Vf[pl.ds(s + 1, 8)]) + zs
                        )
                        emit(x, t, ct, s, op(a, beside, G1f[pl.ds(s, 8)]))
                return 0

            lax.fori_loop(lo + H1, hi + H1, step, 0)

        first = W / (6.0 * 0.25)

        def put1(Df):
            def emit(x, t, ct, s, v):
                Df[pl.ds(s, 8)] = v

            return emit

        ring1(G1f, lambda a, beside, g: ((2.0 - W) * first) * a + (C6 * first) * beside, put1(WAf), -3, 35)
        ring1(WAf, lambda a, beside, g: g - 0.25 * (6.0 * a - beside), put1(WBf), -1, 32)

        def restrict1(i, _):
            for t in range(2):
                for ct in range(2):
                    L[pl.ds(row(i * 16 + ct * 8), 8), t * 128 : t * 128 + 128] = restrict_xy(
                        WBf, (2 * i + (H1 - 1)) * PS1, PS1, t * RP1 + RO1 - 1 + 16 * ct
                    )
            return 0

        lax.fori_loop(0, 16, restrict1, 0)
        f, c = grid(256, 128)
        gap = jnp.abs(jnp.where(f < 192, f, f - 256) - 2 * c)
        R1 = jnp.where(c < 64, jnp.where(gap == 0, 0.5, jnp.where(gap == 1, 0.25, 0.0)), 0.0).astype(F32)
        G2, VA, VB = b["G2"], b["VA"], b["VB"]
        G2f, VAf, VBf = flat(G2), flat(VA), flat(VB)
        res = jnp.dot(L[0:256, :], R1, precision=HIGH, preferred_element_type=F32)
        slot16 = lane // 16
        for x in range(16):
            for ct in range(2):
                G2[x + H2, RO2 + ct * 8 : RO2 + ct * 8 + 8] = res[x * 16 + ct * 8 : x * 16 + ct * 8 + 8]
        for grp in range(2):
            for ct in range(2):
                acc = zero
                for j in range(8):
                    v = res[(grp * 8 + j) * 16 + ct * 8 : (grp * 8 + j) * 16 + ct * 8 + 8]
                    v = jnp.where(lane < 8, v, pltpu.roll(v, 128 - 48, 1))
                    acc = jnp.where(slot16 == j, pltpu.roll(v, 16 * j, 1) if j else v, acc)
                b["PZ2"][grp, ct * 8 : ct * 8 + 8] = acc
        msgs2 = []
        for dx, dy in XY:
            px, py = along(XS2, dx), along(XS2, dy)
            if (dx, dy) != (0, 0):
                msgs2.append(
                    post(
                        G2.at[along(XS2, dx, H2), along(XS2, dy, RO2), :],
                        G2.at[along(XS2, dx, H2 - N2 * dx), along(XS2, dy, RO2 - N2 * dy), :],
                        (dx, dy, 0),
                    )
                )
            gs = along(GS2, dx)
            gd = along(GS2, dx, 1 - 2 * dx)
            yd = along(XS2, dy, 8 - N2 * dy)
            for side, dz in ((0, 1), (1, -1)):
                msgs2.append(post(b["PZ2"].at[gs, py, :], b["RZ2"].at[side, gd, yd, :], (dx, dy, dz)))
        for m in msgs2:
            m.wait()

        first2 = W / (6.0 * 0.0625)

        def spread(grp, _):
            for ct in range(4):
                m = jnp.where(
                    jnp.bitwise_and(lane, 15) < 8,
                    b["RZ2"][1, grp, ct * 8 : ct * 8 + 8],
                    b["RZ2"][0, grp, ct * 8 : ct * 8 + 8],
                )
                for j in range(8):
                    hi = pltpu.roll(m, (64 - 16 * j) % 128, 1)
                    lo = pltpu.roll(m, 112 - 16 * j, 1) if j < 7 else m
                    r = pl.ds(row((grp * 8 + j) * RP2 + 8 + ct * 8), 8)
                    own = G2f[r]
                    v = jnp.where(lane < 64, own, jnp.where(lane < 72, hi, jnp.where(lane >= 120, lo, 0.0)))
                    G2f[r] = v
                    VAf[r] = first2 * v
            return 0

        lax.fori_loop(0, 4, spread, 0)

        def coarse(Sf, Tf, lo, hi):
            def step(k, _):
                for ct in range(4):
                    q = row(k * RP2 + 8 + ct * 8)
                    a = Sf[pl.ds(q, 8)]
                    beside = (
                        (Sf[pl.ds(q - RP2, 8)] + Sf[pl.ds(q + RP2, 8)])
                        + (Sf[pl.ds(q - 1, 8)] + Sf[pl.ds(q + 1, 8)])
                        + (pltpu.roll(a, 1, 1) + pltpu.roll(a, 127, 1))
                    )
                    Tf[pl.ds(q, 8)] = (1.0 - W) * a + (C6 * beside + first2 * G2f[pl.ds(q, 8)])
                return 0

            lax.fori_loop(lo, hi, step, 0)

        src, dst = VAf, VBf
        for k in range(COARSE_SWEEPS - 1):
            coarse(src, dst, 2 + k, 31 - k)
            src, dst = dst, src

        f, c = grid(128, 256)
        gap = jnp.abs(jnp.where(c < 192, c, c - 256) - 2 * jnp.where(f < 96, f, f - 128))
        P1 = jnp.where(gap == 0, 1.0, jnp.where(gap == 1, 0.5, 0.0)).astype(F32)
        CZ1f, F1f = flat(b["CZ1"]), flat(b["F1"])
        for k in range(20):
            L[k * 24 : k * 24 + 24, 0:128] = src[pl.ds((k + 6) * RP2 + 12, 24)]
        res = jnp.dot(L[0:480, 0:128], P1, precision=HIGH, preferred_element_type=F32)
        for k in range(20):
            for t in range(2):
                b["CZ1"][k, t, 0:24] = res[k * 24 : k * 24 + 24, t * 128 : t * 128 + 128]

        def widen1(k, _):
            for t in range(2):
                for ct in range(3):
                    q = k * 64 + (t * 32 + ct * 8)
                    v, n = CZ1f[pl.ds(q, 8)], CZ1f[pl.ds(q + 1, 8)]
                    o = k * PS1 + (t * RP1 + 4 + 16 * ct)
                    F1f[pl.ds(o, 8, stride=2)] = v
                    F1f[pl.ds(o + 1, 8, stride=2)] = 0.5 * (v + n)
            return 0

        lax.fori_loop(0, 20, widen1, 0)

        def correct1(k, _):
            for t in range(2):
                for ct in range(5):
                    o = t * RP1 + 8 + ct * 8
                    v = F1f[pl.ds(row(k * PS1 + o), 8)]
                    n = F1f[pl.ds(row((k + 1) * PS1 + o), 8)]
                    q = row(2 * k * PS1 + o)
                    WAf[pl.ds(q, 8)] = WAf[pl.ds(q, 8)] + v
                    q = row((2 * k + 1) * PS1 + o)
                    WAf[pl.ds(q, 8)] = WAf[pl.ds(q, 8)] + 0.5 * (v + n)
            return 0

        lax.fori_loop(0, 20, correct1, 0)

        def relax1(a, beside, g):
            return (1.0 - W) * a + (C6 * beside + first * g)

        def put_l(x, t, ct, s, v):
            L[pl.ds(row((x - (H1 - 1)) * 40 + ct * 8), 8), t * 128 : t * 128 + 128] = v

        ring1(WAf, relax1, put1(WBf), -2, 34)
        ring1(WBf, relax1, put_l, -1, 33)

        f, c = grid(256, 384)
        gap = jnp.abs(jnp.where(c <= 256, c, jnp.where(c == 383, -1, 9999)) - 2 * jnp.where(f < 192, f, f - 256))
        P0 = jnp.where(gap == 0, 1.0, jnp.where(gap == 1, 0.5, 0.0)).astype(F32)
        CZ0f, F0f = flat(b["CZ0"]), flat(b["F0"])

        def pz0(i, _):
            res = jnp.dot(L[pl.ds(row(i * 680), 680), :], P0, precision=HIGH, preferred_element_type=F32)
            for p in range(17):
                for t in range(3):
                    CZ0f[pl.ds(row((i * 17 + p) * 144 + t * 48), 40)] = res[p * 40 : p * 40 + 40, t * 128 : t * 128 + 128]
            return 0

        lax.fori_loop(0, 2, pz0, 0)

        def widen0(k, _):
            for t in range(3):
                for ct in range(5):
                    q = k * 144 + (t * 48 + ct * 8)
                    v, n = CZ0f[pl.ds(q, 8)], CZ0f[pl.ds(q + 1, 8)]
                    o = k * 240 + (t * 80 + 16 * ct)
                    F0f[pl.ds(o, 8, stride=2)] = v
                    F0f[pl.ds(o + 1, 8, stride=2)] = 0.5 * (v + n)
            return 0

        lax.fori_loop(0, 34, widen0, 0)

        def add0(plane, t, r, v):
            q = pl.ds(row(plane * PS0 + t * RP0 + r), 8)
            Af[q] = Af[q] + v

        def get0(k, t, r):
            return F0f[pl.ds(row(k * 240 + t * 80 + r), 8)]

        for t in range(2):
            for r in range(8, 72, 8):
                add0(0, t, r, 0.5 * (get0(0, t, r) + get0(1, t, r)))
                add0(65, t, r, get0(33, t, r))

        def correct0(i, _):
            for t in range(2):
                for r in range(0, 80, 8):
                    v, n = get0(i + 1, t, r), get0(i + 2, t, r)
                    add0(2 * i + 1, t, r, v)
                    add0(2 * i + 2, t, r, 0.5 * (v + n))
            for yt in range(8):
                v, n = get0(i + 1, 2, 8 + yt * 8), get0(i + 2, 2, 8 + yt * 8)
                h = b["HR"][2, 0, yt * 8 : yt * 8 + 8]
                for x, w in ((2 * i, v), (2 * i + 1, 0.5 * (v + n))):
                    h = h + jnp.where(half == x, pltpu.roll(w, jnp.bitwise_and(2 * x, 127), 1), 0.0)
                b["HR"][2, 0, yt * 8 : yt * 8 + 8] = h
            return 0

        lax.fori_loop(0, 32, correct0, 0)

        stencil(Af, 2, relax0, storing(Bf, 3))
        msgs = faces(B, 3)
        tile = total_wait(2, sum_msgs)
        mean = jnp.sum(tile, keepdims=True) / cells
        mean = jnp.broadcast_to(mean, (8, 128))
        for m in msgs:
            m.wait()
        merge(3)
        stencil(Bf, 3, lambda c, beside, g: relax0(c, beside, g) - mean, storing(Af, None))
        outs = []
        for t in range(2):
            outs.append(pltpu.make_async_copy(A.at[1:65, t, 8:72, :], out_hbm.at[:, :, t * 128 : t * 128 + 128], local.at[4 + t]))
        for o in outs:
            o.start()
        for o in outs:
            o.wait()

    return kernel, scratch


def solution(mesh):
    nx, ny, nz = (mesh.shape[a] for a in ("gx", "gy", "gz"))
    kernel, scratch = make_kernel(nx, ny, nz)

    def shards(right_side, initial_guess):
        assert right_side.shape == (64, 64, 256)
        return pl.pallas_call(
            kernel,
            out_shape=jax.ShapeDtypeStruct(right_side.shape, F32),
            in_specs=[pl.BlockSpec(memory_space=pl.ANY)] * 2,
            out_specs=pl.BlockSpec(memory_space=pl.ANY),
            scratch_shapes=scratch,
            compiler_params=pltpu.CompilerParams(collective_id=0, has_side_effects=True, vmem_limit_bytes=60 << 20),
        )(right_side, initial_guess)

    placed = P("gx", "gy", "gz")
    return jax.shard_map(shards, mesh=mesh, in_specs=(placed, placed), out_specs=placed, check_vma=False)
```

```python
import itertools

import jax
import jax.numpy as jnp
from jax import lax
from jax.experimental import pallas as pl
from jax.experimental.pallas import tpu as pltpu
from jax.sharding import PartitionSpec as P

F32 = jnp.float32
MESH = pl.DeviceIdType.MESH
COARSE_SWEEPS = 6
W = 0.8
C6 = W / 6.0
HIGH = lax.Precision.HIGHEST

N0, RP0 = 64, 96
PS0 = 2 * RP0
N1, H1, RP1, RO1 = 32, 4, 56, 12
PS1 = 2 * RP1
N2, H2, RP2, RO2 = 16, 8, 48, 16

XS1 = {1: (28, 5), 0: (0, 33), -1: (0, 4)}
GS1 = {1: (1, 2), 0: (0, 3), -1: (0, 1)}
XS2 = {1: (8, 8), 0: (0, 16), -1: (0, 8)}
GS2 = {1: (1, 1), 0: (0, 2), -1: (0, 1)}
PAD8 = {5: 8, 33: 40, 4: 8}
XY = [d for d in itertools.product((-1, 0, 1), repeat=2)]
XY8 = [d for d in XY if d != (0, 0)]
NEAR = [d for d in itertools.product((-1, 0, 1), repeat=3) if d != (0, 0, 0)]


def shift_weight():
    total = 0.0
    for level in range(2):
        total += 4 * W / (6.0 * 0.25**level)
    return total + COARSE_SWEEPS * W / (6.0 * 0.0625)


def make_kernel(nx, ny, nz):
    cells = float(nx * N0 * ny * N0 * nz * 256)
    far = (
        [(0, 0, k) for k in range(2, nz - 1)]
        + [(0, k, 0) for k in range(2, ny - 1)]
        + [(k, 0, 0) for k in range(2, nx - 1)]
    )
    peers = NEAR + far
    ring = {0: [(0, 0, k) for k in range(1, nz)], 1: [(0, k, 0) for k in range(1, ny)], 2: [(k, 0, 0) for k in range(1, nx)]}
    n_sem = [0]

    scratch, names = [], []

    def vm(name, *shape):
        names.append(name)
        scratch.append(pltpu.VMEM(shape, F32))

    vm("A", 66, 2, RP0, 128)
    vm("B", 67, 2, RP0, 128)
    vm("G", 64, 2, 64, 128)
    vm("PK", 4, 64, 128)
    vm("HR", 4, 2, 64, 128)
    vm("L", 1360, 256)
    vm("G1", 41, 2, RP1, 128)
    vm("WA", 41, 2, RP1, 128)
    vm("WB", 41, 2, RP1, 128)
    vm("U", 3, 40, 128)
    vm("D", 3, 40, 128)
    vm("G2", 32, RP2, 128)
    vm("VA", 33, RP2, 128)
    vm("VB", 33, RP2, 128)
    vm("PZ2", 2, 16, 128)
    vm("RZ2", 2, 4, 32, 128)
    vm("CZ1", 21, 2, 32, 128)
    vm("F1", 21, 2, RP1, 128)
    vm("CZ0", 34, 3, 48, 128)
    vm("F0", 34, 3, 80, 128)
    vm("TS", 3, 8, 128)
    vm("TR0", max(nz - 1, 1), 8, 128)
    vm("TR1", max(ny - 1, 1), 8, 128)
    vm("TR2", max(nx - 1, 1), 8, 128)
    for dx, dy in XY8:
        vm(("RT", dx, dy), XS1[dx][1], PAD8[XS1[dy][1]], 128)
        vm(("RU0", dx, dy), GS1[dx][1], PAD8[XS1[dy][1]], 128)
    for dx, dy in XY:
        vm(("RU1", dx, dy), GS1[dx][1], PAD8[XS1[dy][1]], 128)
        vm(("RD", dx, dy), GS1[dx][1], PAD8[XS1[dy][1]], 128)
    N_MSG = 4 * 6 + 34 + 26 + (nx - 1) + (ny - 1) + (nz - 1)
    scratch += [pltpu.SemaphoreType.DMA((N_MSG,)), pltpu.SemaphoreType.DMA((N_MSG,)), pltpu.SemaphoreType.DMA((8,))]

    def kernel(g_hbm, v_hbm, out_hbm, *refs):
        b = dict(zip(names, refs))
        send, recv, local = refs[len(names):]
        A, B, G = b["A"], b["B"], b["G"]
        me = (lax.axis_index("gx"), lax.axis_index("gy"), lax.axis_index("gz"))
        sizes = (nx, ny, nz)
        lane = lax.broadcasted_iota(jnp.int32, (8, 128), 1)
        l0, l127 = lane == 0, lane == 127
        zero = jnp.zeros((8, 128), F32)
        used = [0]

        def at(d):
            return tuple(lax.rem(m + (k + n), n) if k else m for m, k, n in zip(me, d, sizes))

        def post(src, dst, d):
            k = used[0]
            used[0] += 1
            c = pltpu.make_async_remote_copy(
                src_ref=src, dst_ref=dst, send_sem=send.at[k], recv_sem=recv.at[k], device_id=at(d), device_id_type=MESH
            )
            c.start()
            return c

        def flat(ref):
            s = ref.shape
            n = 1
            for k in s[:-1]:
                n *= k
            return ref.reshape(n, s[-1])

        def row(k, m=8):
            return pl.multiple_of(k, m)

        Af, Bf, Gf = flat(A), flat(B), flat(G)
        G1f, WAf, WBf = flat(b["G1"]), flat(b["WA"]), flat(b["WB"])

        def clear(ref):
            f = flat(ref)
            n = f.shape[0] // 8
            per = 1
            for k in range(16, 0, -1):
                if n % k == 0:
                    per = k
                    break

            def step(i, _):
                for k in range(per):
                    f[pl.ds(row((i * per + k) * 8), 8)] = zero
                return 0

            lax.fori_loop(0, n // per, step, 0)

        barrier = pltpu.get_barrier_semaphore()
        for d in peers:
            pl.semaphore_signal(barrier, inc=1, device_id=at(d), device_id_type=MESH)
        loads = []
        for t in range(2):
            loads.append(pltpu.make_async_copy(v_hbm.at[:, :, t * 128 : t * 128 + 128], A.at[1:65, t, 8:72, :], local.at[t]))
            loads.append(pltpu.make_async_copy(g_hbm.at[:, :, t * 128 : t * 128 + 128], G.at[:, t, :, :], local.at[2 + t]))
        for k in (0, 2, 1, 3):
            loads[k].start()
        for name in names:
            if isinstance(name, tuple):
                clear(b[name])
        clear(b["G1"])
        for dst in (B.at[0], B.at[65], B.at[66]):
            clear(dst)

        def clear_rows(i, _):
            for t in range(2):
                Bf[pl.ds(row(i * PS0 + t * RP0), 8)] = zero
                for r in (72, 80, 88):
                    Bf[pl.ds(row(i * PS0 + t * RP0 + r), 8)] = zero
            return 0

        lax.fori_loop(1, 65, clear_rows, 0)
        pl.semaphore_wait(barrier, len(peers))
        loads[0].wait()
        loads[2].wait()

        half = jnp.bitwise_and(lane + 1, 127) // 2

        def faces(V, k):
            pk = b["PK"].at[k]
            return [
                post(V.at[64, :, 8:72, :], V.at[0, :, 8:72, :], (1, 0, 0)),
                post(V.at[1, :, 8:72, :], V.at[65, :, 8:72, :], (-1, 0, 0)),
                post(V.at[1:65, :, 71:72, :], V.at[1:65, :, 7:8, :], (0, 1, 0)),
                post(V.at[1:65, :, 8:9, :], V.at[1:65, :, 72:73, :], (0, -1, 0)),
                post(pk, b["HR"].at[k, 0], (0, 0, 1)),
                post(pk, b["HR"].at[k, 1], (0, 0, -1)),
            ]

        odd = jnp.bitwise_and(lane, 1) == 1

        def merge(k):
            for yt in range(8):
                r = slice(yt * 8, yt * 8 + 8)
                b["HR"][k, 0, r] = jnp.where(odd, pltpu.roll(b["HR"][k, 1, r], 127, 1), pltpu.roll(b["HR"][k, 0, r], 1, 1))

        def put_faces(Df, k, i):
            for yt in range(8):
                keep = b["PK"][k, yt * 8 : yt * 8 + 8]
                for p in range(4):
                    x = i * 4 + p
                    r = row((i * 4 + 1) * PS0) + (p * PS0 + 8 + yt * 8)
                    both = jnp.where(l0, Df[pl.ds(r, 8)], Df[pl.ds(r + RP0, 8)])
                    both = pltpu.roll(both, jnp.bitwise_and(2 * x, 127), 1)
                    keep = jnp.where(half == x, both, keep)
                b["PK"][k, yt * 8 : yt * 8 + 8] = keep

        def stencil(Vf, Df, k, op, faces_to=None, carry=0):
            summed = isinstance(carry, tuple)

            def step(i, carry):
                base = row((i * 4 + 1) * PS0)
                if faces_to is not None:
                    put_faces(Df, faces_to, jnp.maximum(i - 1, 0))
                for yt in range(8):
                    o = 8 + yt * 8
                    c = {
                        (p, t): Vf[pl.ds(row(base + (p * PS0 + t * RP0 + o)), 8)] for p in range(-1, 5) for t in range(2)
                    }
                    h = b["HR"][k, 0, yt * 8 : yt * 8 + 8]
                    for p in range(4):
                        x = i * 4 + p
                        e = pltpu.roll(h, jnp.bitwise_and(128 - 2 * x, 127), 1)
                        c0, c1 = c[p, 0], c[p, 1]
                        up0, up1, dn0, dn1 = (pltpu.roll(v, n, 1) for n in (1, 127) for v in (c0, c1))
                        zs = (
                            jnp.where(l0, e, up0) + jnp.where(l127, dn1, dn0),
                            jnp.where(l0, up0, up1) + jnp.where(l127, e, dn1),
                        )
                        for t in range(2):
                            q = base + (p * PS0 + t * RP0 + o)
                            ys = Vf[pl.ds(q - 1, 8)] + Vf[pl.ds(q + 1, 8)]
                            beside = (c[p - 1, t] + c[p + 1, t]) + ys + zs[t]
                            g = Gf[pl.ds(row(x * 128 + t * 64 + yt * 8), 8)]
                            Df[pl.ds(row(q), 8)] = op(c[p, t], beside, g)
                            if summed:
                                carry = (carry[0] + c[p, t], carry[1] + g)
                return carry

            carry = lax.fori_loop(0, 16, step, carry)
            if faces_to is not None:
                put_faces(Df, faces_to, 15)
            return carry

        def relax0(c, beside, g):
            return (1.0 - W) * c + C6 * (beside + g)

        def defect0(c, beside, g):
            return g - 6.0 * c + beside

        def total_stage(stage, tile):
            b["TS"][stage] = tile
            rec = b[f"TR{stage}"]
            return [post(b["TS"].at[stage], rec.at[j], d) for j, d in enumerate(ring[stage])]

        def total_wait(stage, msgs):
            tile = b["TS"][stage]
            for j, m in enumerate(msgs):
                m.wait()
                tile = tile + b[f"TR{stage}"][j]
            return tile

        def pack_first(i, _):
            put_faces(Af, 0, 2 * i)
            put_faces(Af, 0, 2 * i + 1)
            return 0

        lax.fori_loop(0, 8, pack_first, 0)
        msgs = faces(A, 0)
        loads[1].wait()
        loads[3].wait()
        for m in msgs:
            m.wait()
        merge(0)
        sums = stencil(Af, Bf, 0, relax0, 1, (zero, zero))
        msgs = faces(B, 1)
        sum_msgs = total_stage(0, sums[0] + shift_weight() * sums[1])
        for m in msgs:
            m.wait()
        merge(1)
        stencil(Bf, Af, 1, relax0, 2)
        msgs = faces(A, 2)
        sum_msgs = total_stage(1, total_wait(0, sum_msgs))
        for m in msgs:
            m.wait()
        merge(2)

        stencil(Af, Bf, 2, defect0)

        def clear_rims(i, _):
            for t in range(2):
                Bf[pl.ds(i * PS0 + t * RP0 + 7, 1)] = zero[0:1]
                Bf[pl.ds(i * PS0 + t * RP0 + 72, 1)] = zero[0:1]
            return 0

        lax.fori_loop(1, 65, clear_rims, 0)
        for dst in (B.at[0], B.at[65]):
            clear(dst)
        L = b["L"]

        def restrict_xy(Df, plane, slab, start):
            rows = []
            for dp in range(3):
                q = plane + dp * slab + start
                lo, on, up = (Df[pl.ds(q + k, 8, stride=2)] for k in range(3))
                rows.append(0.25 * (lo + up) + 0.5 * on)
            return 0.25 * (rows[0] + rows[2]) + 0.5 * rows[1]

        def restrict0(i, _):
            for t in range(2):
                for ct in range(5):
                    L[pl.ds(row(i * 40 + ct * 8), 8), t * 128 : t * 128 + 128] = restrict_xy(
                        Bf, i * 2 * PS0, PS0, t * RP0 + 7 + 16 * ct
                    )
            return 0

        lax.fori_loop(0, 33, restrict0, 0)

        def grid(rows, cols):
            return (
                lax.broadcasted_iota(jnp.int32, (rows, cols), 0),
                lax.broadcasted_iota(jnp.int32, (rows, cols), 1),
            )

        f, c = grid(256, 256)
        gap = jnp.abs(f - 2 * c)
        R0 = jnp.where(gap == 0, 0.5, jnp.where(gap == 1, 0.25, 0.0)).astype(F32)

        def rz0(i, _):
            res = jnp.dot(L[pl.ds(row(i * 440), 440), :], R0, precision=HIGH, preferred_element_type=F32)
            for p in range(11):
                for t in range(2):
                    for ct in range(5):
                        G1f[pl.ds((i * 11 + (p + H1)) * PS1 + (t * RP1 + RO1 + ct * 8), 8)] = res[
                            p * 40 + ct * 8 : p * 40 + ct * 8 + 8, t * 128 : t * 128 + 128
                        ]
            return 0

        lax.fori_loop(0, 3, rz0, 0)

        slot8 = lane // 8
        for grp in range(3):
            for ct in range(5):
                up = dn = zero
                for j in range(16 if grp < 2 else 1):
                    q = (grp * 16 + j + H1) * PS1 + RO1 + ct * 8
                    t0, e = G1f[q : q + 8], G1f[q + RP1 : q + RP1 + 8]
                    up = jnp.where(slot8 == j, pltpu.roll(jnp.where(l0, e, t0), (4 + 8 * j) % 128, 1), up)
                    dn = jnp.where(slot8 == j, pltpu.roll(t0, 8 * j, 1) if j else t0, dn)
                b["U"][grp, ct * 8 : ct * 8 + 8] = up
                b["D"][grp, ct * 8 : ct * 8 + 8] = dn
        G1 = b["G1"]
        msgs1 = []

        def along(spec, k, off=0):
            return slice(spec[k][0] + off, spec[k][0] + off + spec[k][1])

        for dx, dy in XY:
            n = XS1[dy][1]
            ys = along(XS1, dy)
            gs = along(GS1, dx)
            if (dx, dy) != (0, 0):
                msgs1.append(
                    post(G1.at[along(XS1, dx, H1), 0, along(XS1, dy, RO1), :], b["RT", dx, dy].at[:, 0:n, :], (dx, dy, 0))
                )
                msgs1.append(post(b["U"].at[gs, ys, :], b["RU0", dx, dy].at[:, 0:n, :], (dx, dy, 0)))
            msgs1.append(post(b["U"].at[gs, ys, :], b["RU1", dx, dy].at[:, 0:n, :], (dx, dy, 1)))
            msgs1.append(post(b["D"].at[gs, ys, :], b["RD", dx, dy].at[:, 0:n, :], (dx, dy, -1)))
        sum_msgs = total_stage(2, total_wait(1, sum_msgs))
        for m in msgs1:
            m.wait()

        def add1(q, v):
            G1f[pl.ds(q, 8)] = G1f[pl.ds(q, 8)] + v

        for dx, dy in XY:
            sx, n = XS1[dx]
            sy = XS1[dy][0]
            tiles = PAD8[XS1[dy][1]] // 8
            g0 = GS1[dx][0]
            per = 11 if n == 33 else n

            def unpack(i, _, dx=dx, dy=dy, sx=sx, sy=sy, tiles=tiles, g0=g0, per=per):
                for p in range(per):
                    k = i * per + p
                    s = k + sx
                    grp, j = s // 16 - g0, s % 16 if isinstance(s, int) else jnp.bitwise_and(s, 15)
                    up = (124 - 8 * j) % 128 if isinstance(s, int) else jnp.bitwise_and(124 - 8 * j, 127)
                    down = (128 - 8 * j) % 128 if isinstance(s, int) else jnp.bitwise_and(128 - 8 * j, 127)
                    for ct in range(tiles):
                        q = i * per * PS1 + ((p + (sx - N1 * dx + H1)) * PS1 + (sy - N1 * dy + RO1 + ct * 8))
                        u1 = pltpu.roll(b["RU1", dx, dy][grp, ct * 8 : ct * 8 + 8], up, 1)
                        dn = pltpu.roll(b["RD", dx, dy][grp, ct * 8 : ct * 8 + 8], down, 1)
                        e = jnp.where(lane >= 124, u1, jnp.where(lane < 4, dn, 0.0))
                        t0 = jnp.where(l0, u1, 0.0)
                        if (dx, dy) != (0, 0):
                            u0 = pltpu.roll(b["RU0", dx, dy][grp, ct * 8 : ct * 8 + 8], up, 1)
                            e = e + jnp.where(l0, u0, 0.0)
                            t0 = t0 + b["RT", dx, dy][k, ct * 8 : ct * 8 + 8]
                        add1(q, t0)
                        add1(q + RP1, e)
                return 0

            if n == 33:
                lax.fori_loop(0, 3, unpack, 0)
            else:
                unpack(0, 0)

        def ring1(Vf, op, emit, lo, hi):
            per = 3 if (hi - lo) % 3 == 0 else 2

            def step(i, _):
                for p in range(per):
                    base = i * per * PS1
                    for ct in range(5):
                        q = row(base + ((p + lo + H1) * PS1 + 8 + ct * 8))
                        c = (Vf[pl.ds(q, 8)], Vf[pl.ds(q + RP1, 8)])
                        up = [pltpu.roll(v, 1, 1) for v in c]
                        dn = [pltpu.roll(v, 127, 1) for v in c]
                        for t in range(2):
                            zs = jnp.where(l0, up[1 - t], up[t]) + jnp.where(l127, dn[1 - t], dn[t])
                            s = q + t * RP1
                            beside = (
                                (Vf[pl.ds(s - PS1, 8)] + Vf[pl.ds(s + PS1, 8)])
                                + (Vf[pl.ds(s - 1, 8)] + Vf[pl.ds(s + 1, 8)])
                                + zs
                            )
                            emit(i * per * 40 + (p + lo + 1) * 40, t, ct, s, op(c[t], beside, G1f[pl.ds(s, 8)]))
                return 0

            lax.fori_loop(0, (hi - lo) // per, step, 0)

        first = W / (6.0 * 0.25)

        def put1(Df):
            def emit(x, t, ct, s, v):
                Df[pl.ds(s, 8)] = v

            return emit

        ring1(G1f, lambda a, beside, g: ((2.0 - W) * first) * a + (C6 * first) * beside, put1(WAf), -3, 35)
        ring1(WAf, lambda a, beside, g: g - 0.25 * (6.0 * a - beside), put1(WBf), -1, 32)

        def restrict1(i, _):
            for t in range(2):
                for ct in range(2):
                    L[pl.ds(row(i * 16 + ct * 8), 8), t * 128 : t * 128 + 128] = restrict_xy(
                        WBf, (2 * i + (H1 - 1)) * PS1, PS1, t * RP1 + RO1 - 1 + 16 * ct
                    )
            return 0

        lax.fori_loop(0, 16, restrict1, 0)
        f, c = grid(256, 128)
        gap = jnp.abs(jnp.where(f < 192, f, f - 256) - 2 * c)
        R1 = jnp.where(c < 64, jnp.where(gap == 0, 0.5, jnp.where(gap == 1, 0.25, 0.0)), 0.0).astype(F32)
        G2, VA, VB = b["G2"], b["VA"], b["VB"]
        G2f, VAf, VBf = flat(G2), flat(VA), flat(VB)
        res = jnp.dot(L[0:256, :], R1, precision=HIGH, preferred_element_type=F32)
        slot16 = lane // 16
        for x in range(16):
            for ct in range(2):
                G2[x + H2, RO2 + ct * 8 : RO2 + ct * 8 + 8] = res[x * 16 + ct * 8 : x * 16 + ct * 8 + 8]
        for grp in range(2):
            for ct in range(2):
                acc = zero
                for j in range(8):
                    v = res[(grp * 8 + j) * 16 + ct * 8 : (grp * 8 + j) * 16 + ct * 8 + 8]
                    v = jnp.where(lane < 8, v, pltpu.roll(v, 128 - 48, 1))
                    acc = jnp.where(slot16 == j, pltpu.roll(v, 16 * j, 1) if j else v, acc)
                b["PZ2"][grp, ct * 8 : ct * 8 + 8] = acc
        msgs2 = []
        for dx, dy in XY:
            px, py = along(XS2, dx), along(XS2, dy)
            if (dx, dy) != (0, 0):
                msgs2.append(
                    post(
                        G2.at[along(XS2, dx, H2), along(XS2, dy, RO2), :],
                        G2.at[along(XS2, dx, H2 - N2 * dx), along(XS2, dy, RO2 - N2 * dy), :],
                        (dx, dy, 0),
                    )
                )
            gs = along(GS2, dx)
            gd = along(GS2, dx, 1 - 2 * dx)
            yd = along(XS2, dy, 8 - N2 * dy)
            for side, dz in ((0, 1), (1, -1)):
                msgs2.append(post(b["PZ2"].at[gs, py, :], b["RZ2"].at[side, gd, yd, :], (dx, dy, dz)))
        for m in msgs2:
            m.wait()

        first2 = W / (6.0 * 0.0625)

        def spread(grp, _):
            for ct in range(4):
                m = jnp.where(
                    jnp.bitwise_and(lane, 15) < 8,
                    b["RZ2"][1, grp, ct * 8 : ct * 8 + 8],
                    b["RZ2"][0, grp, ct * 8 : ct * 8 + 8],
                )
                for j in range(8):
                    hi = pltpu.roll(m, (64 - 16 * j) % 128, 1)
                    lo = pltpu.roll(m, 112 - 16 * j, 1) if j < 7 else m
                    r = pl.ds(row((grp * 8 + j) * RP2 + 8 + ct * 8), 8)
                    own = G2f[r]
                    v = jnp.where(lane < 64, own, jnp.where(lane < 72, hi, jnp.where(lane >= 120, lo, 0.0)))
                    G2f[r] = v
                    VAf[r] = first2 * v
            return 0

        lax.fori_loop(0, 4, spread, 0)

        def coarse(Sf, Tf, lo, n, per):
            def step(i, _):
                for p in range(per):
                    for ct in range(4):
                        q = row(i * per * RP2 + ((lo + p) * RP2 + 8 + ct * 8))
                        a = Sf[pl.ds(q, 8)]
                        beside = (
                            (Sf[pl.ds(q - RP2, 8)] + Sf[pl.ds(q + RP2, 8)])
                            + (Sf[pl.ds(q - 1, 8)] + Sf[pl.ds(q + 1, 8)])
                            + (pltpu.roll(a, 1, 1) + pltpu.roll(a, 127, 1))
                        )
                        Tf[pl.ds(q, 8)] = (1.0 - W) * a + (C6 * beside + first2 * G2f[pl.ds(q, 8)])
                return 0

            lax.fori_loop(0, n // per, step, 0)

        src, dst = VAf, VBf
        for lo, n, per in ((2, 28, 7), (2, 28, 7), (4, 24, 8), (4, 24, 8), (6, 20, 10)):
            coarse(src, dst, lo, n, per)
            src, dst = dst, src

        f, c = grid(128, 256)
        gap = jnp.abs(jnp.where(c < 192, c, c - 256) - 2 * jnp.where(f < 96, f, f - 128))
        P1 = jnp.where(gap == 0, 1.0, jnp.where(gap == 1, 0.5, 0.0)).astype(F32)
        CZ1f, F1f = flat(b["CZ1"]), flat(b["F1"])
        for k in range(20):
            L[k * 24 : k * 24 + 24, 0:128] = src[pl.ds((k + 6) * RP2 + 12, 24)]
        res = jnp.dot(L[0:480, 0:128], P1, precision=HIGH, preferred_element_type=F32)
        for k in range(20):
            for t in range(2):
                b["CZ1"][k, t, 0:24] = res[k * 24 : k * 24 + 24, t * 128 : t * 128 + 128]

        def widen1(k, _):
            for t in range(2):
                for ct in range(3):
                    q = k * 64 + (t * 32 + ct * 8)
                    v, n = CZ1f[pl.ds(q, 8)], CZ1f[pl.ds(q + 1, 8)]
                    o = k * PS1 + (t * RP1 + 4 + 16 * ct)
                    F1f[pl.ds(o, 8, stride=2)] = v
                    F1f[pl.ds(o + 1, 8, stride=2)] = 0.5 * (v + n)
            return 0

        lax.fori_loop(0, 20, widen1, 0)

        def correct1(k, _):
            for t in range(2):
                for ct in range(5):
                    o = t * RP1 + 8 + ct * 8
                    v = F1f[pl.ds(row(k * PS1 + o), 8)]
                    n = F1f[pl.ds(row((k + 1) * PS1 + o), 8)]
                    q = row(2 * k * PS1 + o)
                    WAf[pl.ds(q, 8)] = WAf[pl.ds(q, 8)] + v
                    q = row((2 * k + 1) * PS1 + o)
                    WAf[pl.ds(q, 8)] = WAf[pl.ds(q, 8)] + 0.5 * (v + n)
            return 0

        lax.fori_loop(0, 20, correct1, 0)

        def relax1(a, beside, g):
            return (1.0 - W) * a + (C6 * beside + first * g)

        def put_l(r, t, ct, s, v):
            L[pl.ds(row(r + ct * 8), 8), t * 128 : t * 128 + 128] = v

        ring1(WAf, relax1, put1(WBf), -2, 34)
        ring1(WBf, relax1, put_l, -1, 33)

        f, c = grid(256, 384)
        gap = jnp.abs(jnp.where(c < 256, c, jnp.where(c == 383, 256, jnp.where(c == 256, -1, 9999))) - 2 * jnp.where(f < 192, f, f - 256))
        P0 = jnp.where(gap == 0, 1.0, jnp.where(gap == 1, 0.5, 0.0)).astype(F32)
        CZ0f, F0f = flat(b["CZ0"]), flat(b["F0"])

        def pz0(i, _):
            res = jnp.dot(L[pl.ds(row(i * 680), 680), :], P0, precision=HIGH, preferred_element_type=F32)
            for p in range(17):
                for t in range(3):
                    CZ0f[pl.ds(row((i * 17 + p) * 144 + t * 48), 40)] = res[p * 40 : p * 40 + 40, t * 128 : t * 128 + 128]
            return 0

        lax.fori_loop(0, 2, pz0, 0)

        def widen0(k, _):
            for t in range(3):
                for ct in range(5):
                    q = k * 144 + (t * 48 + ct * 8)
                    v, n = CZ0f[pl.ds(q, 8)], CZ0f[pl.ds(q + 1, 8)]
                    o = k * 240 + (t * 80 + 16 * ct)
                    F0f[pl.ds(o, 8, stride=2)] = v
                    F0f[pl.ds(o + 1, 8, stride=2)] = 0.5 * (v + n)
            return 0

        lax.fori_loop(0, 34, widen0, 0)

        def add0(plane, t, r, v):
            q = pl.ds(row(plane * PS0 + t * RP0 + r), 8)
            Af[q] = Af[q] + v

        def get0(k, t, r):
            return F0f[pl.ds(row(k * 240 + t * 80 + r), 8)]

        for t in range(2):
            for r in range(8, 72, 8):
                add0(0, t, r, 0.5 * (get0(0, t, r) + get0(1, t, r)))
                add0(65, t, r, get0(33, t, r))

        def correct0(k, _):
            for i in (2 * k, 2 * k + 1):
                for t in range(2):
                    for r in range(0, 80, 8):
                        v, n = get0(i + 1, t, r), get0(i + 2, t, r)
                        add0(2 * i + 1, t, r, v)
                        add0(2 * i + 2, t, r, 0.5 * (v + n))
            for yt in range(8):
                h = b["HR"][2, 0, yt * 8 : yt * 8 + 8]
                for i in (2 * k, 2 * k + 1):
                    v, n = get0(i + 1, 2, 8 + yt * 8), get0(i + 2, 2, 8 + yt * 8)
                    for x, w in ((2 * i, v), (2 * i + 1, 0.5 * (v + n))):
                        h = h + jnp.where(half == x, pltpu.roll(w, jnp.bitwise_and(2 * x, 127), 1), 0.0)
                b["HR"][2, 0, yt * 8 : yt * 8 + 8] = h
            return 0

        lax.fori_loop(0, 16, correct0, 0)

        stencil(Af, Bf, 2, relax0, 3)
        msgs = faces(B, 3)
        tile = total_wait(2, sum_msgs)
        mean = jnp.sum(tile, keepdims=True) / cells
        mean = jnp.broadcast_to(mean, (8, 128))
        for m in msgs:
            m.wait()
        merge(3)
        stencil(Bf, Af, 3, lambda c, beside, g: relax0(c, beside, g) - mean)
        outs = []
        for t in range(2):
            outs.append(pltpu.make_async_copy(A.at[1:65, t, 8:72, :], out_hbm.at[:, :, t * 128 : t * 128 + 128], local.at[4 + t]))
        for o in outs:
            o.start()
        for o in outs:
            o.wait()

    return kernel, scratch


def solution(mesh):
    nx, ny, nz = (mesh.shape[a] for a in ("gx", "gy", "gz"))
    kernel, scratch = make_kernel(nx, ny, nz)

    def shards(right_side, initial_guess):
        assert right_side.shape == (64, 64, 256)
        return pl.pallas_call(
            kernel,
            out_shape=jax.ShapeDtypeStruct(right_side.shape, F32),
            in_specs=[pl.BlockSpec(memory_space=pl.ANY)] * 2,
            out_specs=pl.BlockSpec(memory_space=pl.ANY),
            scratch_shapes=scratch,
            compiler_params=pltpu.CompilerParams(collective_id=0, has_side_effects=True, vmem_limit_bytes=60 << 20),
        )(right_side, initial_guess)

    placed = P("gx", "gy", "gz")
    return jax.shard_map(shards, mesh=mesh, in_specs=(placed, placed), out_specs=placed, check_vma=False)
```

```python
import itertools

import jax
import jax.numpy as jnp
from jax import lax
from jax.experimental import pallas as pl
from jax.experimental.pallas import tpu as pltpu
from jax.sharding import PartitionSpec as P

F32 = jnp.float32
MESH = pl.DeviceIdType.MESH
COARSE_SWEEPS = 6
W = 0.8
C6 = W / 6.0
HIGH = lax.Precision.HIGHEST

N0, RP0 = 64, 96
PS0 = 2 * RP0
N1, H1, RP1, RO1 = 32, 4, 56, 12
PS1 = 2 * RP1
N2, H2, RP2, RO2 = 16, 8, 48, 16

XS1 = {1: (28, 5), 0: (0, 33), -1: (0, 4)}
GS1 = {1: (1, 2), 0: (0, 3), -1: (0, 1)}
XS2 = {1: (8, 8), 0: (0, 16), -1: (0, 8)}
GS2 = {1: (1, 1), 0: (0, 2), -1: (0, 1)}
PAD8 = {5: 8, 33: 40, 4: 8}
XY = [d for d in itertools.product((-1, 0, 1), repeat=2)]
XY8 = [d for d in XY if d != (0, 0)]
NEAR = [d for d in itertools.product((-1, 0, 1), repeat=3) if d != (0, 0, 0)]


def shift_weight():
    total = 0.0
    for level in range(2):
        total += 4 * W / (6.0 * 0.25**level)
    return total + COARSE_SWEEPS * W / (6.0 * 0.0625)


def make_kernel(nx, ny, nz):
    cells = float(nx * N0 * ny * N0 * nz * 256)
    peers = [d for d in NEAR if sum(map(abs, d)) == 1]
    ring = {0: [(0, 0, k) for k in range(1, nz)], 1: [(0, k, 0) for k in range(1, ny)], 2: [(k, 0, 0) for k in range(1, nx)]}
    n_sem = [0]

    scratch, names = [], []

    def vm(name, *shape):
        names.append(name)
        scratch.append(pltpu.VMEM(shape, F32))

    vm("A", 66, 2, RP0, 128)
    vm("B", 67, 2, RP0, 128)
    vm("G", 64, 2, 64, 128)
    vm("PK", 4, 64, 128)
    vm("HR", 4, 2, 64, 128)
    vm("L", 1360, 256)
    vm("G1", 41, 2, RP1, 128)
    vm("WA", 41, 2, RP1, 128)
    vm("WB", 41, 2, RP1, 128)
    vm("U", 3, 40, 128)
    vm("D", 3, 40, 128)
    vm("G2", 32, RP2, 128)
    vm("VA", 33, RP2, 128)
    vm("VB", 33, RP2, 128)
    vm("PZ2", 2, 16, 128)
    vm("RZ2", 2, 4, 32, 128)
    vm("CZ1", 21, 2, 32, 128)
    vm("F1", 21, 2, RP1, 128)
    vm("CZ0", 34, 3, 48, 128)
    vm("F0", 34, 3, 80, 128)
    vm("TS", 3, 8, 128)
    vm("TR0", max(nz - 1, 1), 8, 128)
    vm("TR1", max(ny - 1, 1), 8, 128)
    vm("TR2", max(nx - 1, 1), 8, 128)
    for dx, dy in XY8:
        vm(("RT", dx, dy), XS1[dx][1], PAD8[XS1[dy][1]], 128)
        vm(("RU0", dx, dy), GS1[dx][1], PAD8[XS1[dy][1]], 128)
    for dx, dy in XY:
        vm(("RU1", dx, dy), GS1[dx][1], PAD8[XS1[dy][1]], 128)
        vm(("RD", dx, dy), GS1[dx][1], PAD8[XS1[dy][1]], 128)
    N_MSG = 4 * 6 + 34 + 26 + (nx - 1) + (ny - 1) + (nz - 1)
    scratch += [pltpu.SemaphoreType.DMA((N_MSG,)), pltpu.SemaphoreType.DMA((N_MSG,)), pltpu.SemaphoreType.DMA((8,))]

    def kernel(g_hbm, v_hbm, out_ref, *refs):
        b = dict(zip(names, refs))
        send, recv, local = refs[len(names):]
        A, B, G = b["A"], b["B"], b["G"]
        me = (lax.axis_index("gx"), lax.axis_index("gy"), lax.axis_index("gz"))
        sizes = (nx, ny, nz)
        lane = lax.broadcasted_iota(jnp.int32, (8, 128), 1)
        l0, l127 = lane == 0, lane == 127
        zero = jnp.zeros((8, 128), F32)
        used = [0]

        def at(d):
            return tuple(lax.rem(m + (k + n), n) if k else m for m, k, n in zip(me, d, sizes))

        def post(src, dst, d):
            k = used[0]
            used[0] += 1
            c = pltpu.make_async_remote_copy(
                src_ref=src, dst_ref=dst, send_sem=send.at[k], recv_sem=recv.at[k], device_id=at(d), device_id_type=MESH
            )
            c.start()
            return c

        def flat(ref):
            s = ref.shape
            n = 1
            for k in s[:-1]:
                n *= k
            return ref.reshape(n, s[-1])

        def row(k, m=8):
            return pl.multiple_of(k, m)

        Af, Bf, Gf = flat(A), flat(B), flat(G)
        G1f, WAf, WBf = flat(b["G1"]), flat(b["WA"]), flat(b["WB"])

        def clear(ref):
            f = flat(ref)
            n = f.shape[0] // 8
            per = 1
            for k in range(16, 0, -1):
                if n % k == 0:
                    per = k
                    break

            def step(i, _):
                for k in range(per):
                    f[pl.ds(row((i * per + k) * 8), 8)] = zero
                return 0

            lax.fori_loop(0, n // per, step, 0)

        barrier = pltpu.get_barrier_semaphore()
        for d in peers:
            pl.semaphore_signal(barrier, inc=1, device_id=at(d), device_id_type=MESH)
        loads = []
        for t in range(2):
            loads.append(pltpu.make_async_copy(v_hbm.at[:, :, t * 128 : t * 128 + 128], A.at[1:65, t, 8:72, :], local.at[t]))
            loads.append(pltpu.make_async_copy(g_hbm.at[:, :, t * 128 : t * 128 + 128], G.at[:, t, :, :], local.at[2 + t]))
        for k in (0, 2, 1, 3):
            loads[k].start()
        for name in names:
            if isinstance(name, tuple):
                clear(b[name])
        clear(b["G1"])
        for dst in (B.at[0], B.at[65], B.at[66]):
            clear(dst)

        def clear_rows(i, _):
            for t in range(2):
                Bf[pl.ds(row(i * PS0 + t * RP0), 8)] = zero
                for r in (72, 80, 88):
                    Bf[pl.ds(row(i * PS0 + t * RP0 + r), 8)] = zero
            return 0

        lax.fori_loop(1, 65, clear_rows, 0)
        loads[0].wait()
        loads[2].wait()

        half = jnp.bitwise_and(lane + 1, 127) // 2

        def faces(V, k):
            pk = b["PK"].at[k]
            return [
                post(V.at[64, :, 8:72, :], V.at[0, :, 8:72, :], (1, 0, 0)),
                post(V.at[1, :, 8:72, :], V.at[65, :, 8:72, :], (-1, 0, 0)),
                post(V.at[1:65, :, 71:72, :], V.at[1:65, :, 7:8, :], (0, 1, 0)),
                post(V.at[1:65, :, 8:9, :], V.at[1:65, :, 72:73, :], (0, -1, 0)),
                post(pk, b["HR"].at[k, 0], (0, 0, 1)),
                post(pk, b["HR"].at[k, 1], (0, 0, -1)),
            ]

        odd = jnp.bitwise_and(lane, 1) == 1

        def merge(k):
            for yt in range(8):
                r = slice(yt * 8, yt * 8 + 8)
                b["HR"][k, 0, r] = jnp.where(odd, pltpu.roll(b["HR"][k, 1, r], 127, 1), pltpu.roll(b["HR"][k, 0, r], 1, 1))

        def put_faces(Df, k, i):
            for yt in range(8):
                keep = b["PK"][k, yt * 8 : yt * 8 + 8]
                for p in range(4):
                    x = i * 4 + p
                    r = row((i * 4 + 1) * PS0) + (p * PS0 + 8 + yt * 8)
                    both = jnp.where(l0, Df[pl.ds(r, 8)], Df[pl.ds(r + RP0, 8)])
                    both = pltpu.roll(both, jnp.bitwise_and(2 * x, 127), 1)
                    keep = jnp.where(half == x, both, keep)
                b["PK"][k, yt * 8 : yt * 8 + 8] = keep

        def stencil(Vf, Df, k, op, faces_to=None, carry=0):
            summed = isinstance(carry, tuple)

            def step(i, carry):
                base = row((i * 4 + 1) * PS0)
                if faces_to is not None:
                    put_faces(Df, faces_to, jnp.maximum(i - 1, 0))
                for yt in range(8):
                    o = 8 + yt * 8
                    c = {
                        (p, t): Vf[pl.ds(row(base + (p * PS0 + t * RP0 + o)), 8)] for p in range(-1, 5) for t in range(2)
                    }
                    h = b["HR"][k, 0, yt * 8 : yt * 8 + 8]
                    for p in range(4):
                        x = i * 4 + p
                        e = pltpu.roll(h, jnp.bitwise_and(128 - 2 * x, 127), 1)
                        c0, c1 = c[p, 0], c[p, 1]
                        up0, up1, dn0, dn1 = (pltpu.roll(v, n, 1) for n in (1, 127) for v in (c0, c1))
                        zs = (
                            jnp.where(l0, e, up0) + jnp.where(l127, dn1, dn0),
                            jnp.where(l0, up0, up1) + jnp.where(l127, e, dn1),
                        )
                        for t in range(2):
                            q = base + (p * PS0 + t * RP0 + o)
                            ys = Vf[pl.ds(q - 1, 8)] + Vf[pl.ds(q + 1, 8)]
                            beside = (c[p - 1, t] + c[p + 1, t]) + ys + zs[t]
                            g = Gf[pl.ds(row(x * 128 + t * 64 + yt * 8), 8)]
                            v = op(c[p, t], beside, g)
                            if Df is None:
                                out_ref[x, yt * 8 : yt * 8 + 8, t * 128 : t * 128 + 128] = v
                            else:
                                Df[pl.ds(row(q), 8)] = v
                            if summed:
                                carry = (carry[0] + c[p, t], carry[1] + g)
                return carry

            carry = lax.fori_loop(0, 16, step, carry)
            if faces_to is not None:
                put_faces(Df, faces_to, 15)
            return carry

        def relax0(c, beside, g):
            return (1.0 - W) * c + C6 * (beside + g)

        def defect0(c, beside, g):
            return g - 6.0 * c + beside

        def total_stage(stage, tile):
            b["TS"][stage] = tile
            rec = b[f"TR{stage}"]
            return [post(b["TS"].at[stage], rec.at[j], d) for j, d in enumerate(ring[stage])]

        def total_wait(stage, msgs):
            tile = b["TS"][stage]
            for j, m in enumerate(msgs):
                m.wait()
                tile = tile + b[f"TR{stage}"][j]
            return tile

        def pack_first(i, _):
            put_faces(Af, 0, 2 * i)
            put_faces(Af, 0, 2 * i + 1)
            return 0

        lax.fori_loop(0, 8, pack_first, 0)
        pl.semaphore_wait(barrier, len(peers))
        msgs = faces(A, 0)
        loads[1].wait()
        loads[3].wait()
        for m in msgs:
            m.wait()
        merge(0)
        sums = stencil(Af, Bf, 0, relax0, 1, (zero, zero))
        msgs = faces(B, 1)
        sum_msgs = total_stage(0, sums[0] + shift_weight() * sums[1])
        for m in msgs:
            m.wait()
        merge(1)
        stencil(Bf, Af, 1, relax0, 2)
        msgs = faces(A, 2)
        sum_msgs = total_stage(1, total_wait(0, sum_msgs))
        for m in msgs:
            m.wait()
        merge(2)

        stencil(Af, Bf, 2, defect0)

        def clear_rims(i, _):
            for t in range(2):
                Bf[pl.ds(i * PS0 + t * RP0 + 7, 1)] = zero[0:1]
                Bf[pl.ds(i * PS0 + t * RP0 + 72, 1)] = zero[0:1]
            return 0

        lax.fori_loop(1, 65, clear_rims, 0)
        for dst in (B.at[0], B.at[65]):
            clear(dst)
        L = b["L"]

        def restrict_xy(Df, plane, slab, start):
            rows = []
            for dp in range(3):
                q = plane + dp * slab + start
                lo, on, up = (Df[pl.ds(q + k, 8, stride=2)] for k in range(3))
                rows.append(0.25 * (lo + up) + 0.5 * on)
            return 0.25 * (rows[0] + rows[2]) + 0.5 * rows[1]

        def restrict0(i, _):
            for t in range(2):
                for ct in range(5):
                    L[pl.ds(row(i * 40 + ct * 8), 8), t * 128 : t * 128 + 128] = restrict_xy(
                        Bf, i * 2 * PS0, PS0, t * RP0 + 7 + 16 * ct
                    )
            return 0

        lax.fori_loop(0, 33, restrict0, 0)

        def grid(rows, cols):
            return (
                lax.broadcasted_iota(jnp.int32, (rows, cols), 0),
                lax.broadcasted_iota(jnp.int32, (rows, cols), 1),
            )

        f, c = grid(256, 256)
        gap = jnp.abs(f - 2 * c)
        R0 = jnp.where(gap == 0, 0.5, jnp.where(gap == 1, 0.25, 0.0)).astype(F32)

        def rz0(i, _):
            res = jnp.dot(L[pl.ds(row(i * 440), 440), :], R0, precision=HIGH, preferred_element_type=F32)
            for p in range(11):
                for t in range(2):
                    for ct in range(5):
                        G1f[pl.ds((i * 11 + (p + H1)) * PS1 + (t * RP1 + RO1 + ct * 8), 8)] = res[
                            p * 40 + ct * 8 : p * 40 + ct * 8 + 8, t * 128 : t * 128 + 128
                        ]
            return 0

        lax.fori_loop(0, 3, rz0, 0)

        slot8 = lane // 8
        for grp in range(3):
            for ct in range(5):
                up = dn = zero
                for j in range(16 if grp < 2 else 1):
                    q = (grp * 16 + j + H1) * PS1 + RO1 + ct * 8
                    t0, e = G1f[q : q + 8], G1f[q + RP1 : q + RP1 + 8]
                    up = jnp.where(slot8 == j, pltpu.roll(jnp.where(l0, e, t0), (4 + 8 * j) % 128, 1), up)
                    dn = jnp.where(slot8 == j, pltpu.roll(t0, 8 * j, 1) if j else t0, dn)
                b["U"][grp, ct * 8 : ct * 8 + 8] = up
                b["D"][grp, ct * 8 : ct * 8 + 8] = dn
        G1 = b["G1"]
        msgs1 = []

        def along(spec, k, off=0):
            return slice(spec[k][0] + off, spec[k][0] + off + spec[k][1])

        for dx, dy in XY:
            n = XS1[dy][1]
            ys = along(XS1, dy)
            gs = along(GS1, dx)
            if (dx, dy) != (0, 0):
                msgs1.append(
                    post(G1.at[along(XS1, dx, H1), 0, along(XS1, dy, RO1), :], b["RT", dx, dy].at[:, 0:n, :], (dx, dy, 0))
                )
                msgs1.append(post(b["U"].at[gs, ys, :], b["RU0", dx, dy].at[:, 0:n, :], (dx, dy, 0)))
            msgs1.append(post(b["U"].at[gs, ys, :], b["RU1", dx, dy].at[:, 0:n, :], (dx, dy, 1)))
            msgs1.append(post(b["D"].at[gs, ys, :], b["RD", dx, dy].at[:, 0:n, :], (dx, dy, -1)))
        sum_msgs = total_stage(2, total_wait(1, sum_msgs))
        for m in msgs1:
            m.wait()

        def add1(q, v):
            G1f[pl.ds(q, 8)] = G1f[pl.ds(q, 8)] + v

        for dx, dy in XY:
            sx, n = XS1[dx]
            sy = XS1[dy][0]
            tiles = PAD8[XS1[dy][1]] // 8
            g0 = GS1[dx][0]
            per = 11 if n == 33 else n

            def unpack(i, _, dx=dx, dy=dy, sx=sx, sy=sy, tiles=tiles, g0=g0, per=per):
                for p in range(per):
                    k = i * per + p
                    s = k + sx
                    grp, j = s // 16 - g0, s % 16 if isinstance(s, int) else jnp.bitwise_and(s, 15)
                    up = (124 - 8 * j) % 128 if isinstance(s, int) else jnp.bitwise_and(124 - 8 * j, 127)
                    down = (128 - 8 * j) % 128 if isinstance(s, int) else jnp.bitwise_and(128 - 8 * j, 127)
                    for ct in range(tiles):
                        q = i * per * PS1 + ((p + (sx - N1 * dx + H1)) * PS1 + (sy - N1 * dy + RO1 + ct * 8))
                        u1 = pltpu.roll(b["RU1", dx, dy][grp, ct * 8 : ct * 8 + 8], up, 1)
                        dn = pltpu.roll(b["RD", dx, dy][grp, ct * 8 : ct * 8 + 8], down, 1)
                        e = jnp.where(lane >= 124, u1, jnp.where(lane < 4, dn, 0.0))
                        t0 = jnp.where(l0, u1, 0.0)
                        if (dx, dy) != (0, 0):
                            u0 = pltpu.roll(b["RU0", dx, dy][grp, ct * 8 : ct * 8 + 8], up, 1)
                            e = e + jnp.where(l0, u0, 0.0)
                            t0 = t0 + b["RT", dx, dy][k, ct * 8 : ct * 8 + 8]
                        add1(q, t0)
                        add1(q + RP1, e)
                return 0

            if n == 33:
                lax.fori_loop(0, 3, unpack, 0)
            else:
                unpack(0, 0)

        def ring1(Vf, op, emit, lo, hi):
            per = 3 if (hi - lo) % 3 == 0 else 2

            def step(i, _):
                for p in range(per):
                    base = i * per * PS1
                    for ct in range(5):
                        q = row(base + ((p + lo + H1) * PS1 + 8 + ct * 8))
                        c = (Vf[pl.ds(q, 8)], Vf[pl.ds(q + RP1, 8)])
                        up = [pltpu.roll(v, 1, 1) for v in c]
                        dn = [pltpu.roll(v, 127, 1) for v in c]
                        for t in range(2):
                            zs = jnp.where(l0, up[1 - t], up[t]) + jnp.where(l127, dn[1 - t], dn[t])
                            s = q + t * RP1
                            beside = (
                                (Vf[pl.ds(s - PS1, 8)] + Vf[pl.ds(s + PS1, 8)])
                                + (Vf[pl.ds(s - 1, 8)] + Vf[pl.ds(s + 1, 8)])
                                + zs
                            )
                            emit(i * per * 40 + (p + lo + 1) * 40, t, ct, s, op(c[t], beside, G1f[pl.ds(s, 8)]))
                return 0

            lax.fori_loop(0, (hi - lo) // per, step, 0)

        first = W / (6.0 * 0.25)

        def put1(Df):
            def emit(x, t, ct, s, v):
                Df[pl.ds(s, 8)] = v

            return emit

        ring1(G1f, lambda a, beside, g: ((2.0 - W) * first) * a + (C6 * first) * beside, put1(WAf), -3, 35)
        ring1(WAf, lambda a, beside, g: g - 0.25 * (6.0 * a - beside), put1(WBf), -1, 32)

        def restrict1(i, _):
            for t in range(2):
                for ct in range(2):
                    L[pl.ds(row(i * 16 + ct * 8), 8), t * 128 : t * 128 + 128] = restrict_xy(
                        WBf, (2 * i + (H1 - 1)) * PS1, PS1, t * RP1 + RO1 - 1 + 16 * ct
                    )
            return 0

        lax.fori_loop(0, 16, restrict1, 0)
        f, c = grid(256, 128)
        gap = jnp.abs(jnp.where(f < 192, f, f - 256) - 2 * c)
        R1 = jnp.where(c < 64, jnp.where(gap == 0, 0.5, jnp.where(gap == 1, 0.25, 0.0)), 0.0).astype(F32)
        G2, VA, VB = b["G2"], b["VA"], b["VB"]
        G2f, VAf, VBf = flat(G2), flat(VA), flat(VB)
        res = jnp.dot(L[0:256, :], R1, precision=HIGH, preferred_element_type=F32)
        slot16 = lane // 16
        for x in range(16):
            for ct in range(2):
                G2[x + H2, RO2 + ct * 8 : RO2 + ct * 8 + 8] = res[x * 16 + ct * 8 : x * 16 + ct * 8 + 8]
        for grp in range(2):
            for ct in range(2):
                acc = zero
                for j in range(8):
                    v = res[(grp * 8 + j) * 16 + ct * 8 : (grp * 8 + j) * 16 + ct * 8 + 8]
                    v = jnp.where(lane < 8, v, pltpu.roll(v, 128 - 48, 1))
                    acc = jnp.where(slot16 == j, pltpu.roll(v, 16 * j, 1) if j else v, acc)
                b["PZ2"][grp, ct * 8 : ct * 8 + 8] = acc
        msgs2 = []
        for dx, dy in XY:
            px, py = along(XS2, dx), along(XS2, dy)
            if (dx, dy) != (0, 0):
                msgs2.append(
                    post(
                        G2.at[along(XS2, dx, H2), along(XS2, dy, RO2), :],
                        G2.at[along(XS2, dx, H2 - N2 * dx), along(XS2, dy, RO2 - N2 * dy), :],
                        (dx, dy, 0),
                    )
                )
            gs = along(GS2, dx)
            gd = along(GS2, dx, 1 - 2 * dx)
            yd = along(XS2, dy, 8 - N2 * dy)
            for side, dz in ((0, 1), (1, -1)):
                msgs2.append(post(b["PZ2"].at[gs, py, :], b["RZ2"].at[side, gd, yd, :], (dx, dy, dz)))
        for m in msgs2:
            m.wait()

        first2 = W / (6.0 * 0.0625)

        def spread(grp, _):
            for ct in range(4):
                m = jnp.where(
                    jnp.bitwise_and(lane, 15) < 8,
                    b["RZ2"][1, grp, ct * 8 : ct * 8 + 8],
                    b["RZ2"][0, grp, ct * 8 : ct * 8 + 8],
                )
                for j in range(8):
                    hi = pltpu.roll(m, (64 - 16 * j) % 128, 1)
                    lo = pltpu.roll(m, 112 - 16 * j, 1) if j < 7 else m
                    r = pl.ds(row((grp * 8 + j) * RP2 + 8 + ct * 8), 8)
                    own = G2f[r]
                    v = jnp.where(lane < 64, own, jnp.where(lane < 72, hi, jnp.where(lane >= 120, lo, 0.0)))
                    G2f[r] = v
                    VAf[r] = first2 * v
            return 0

        lax.fori_loop(0, 4, spread, 0)

        def coarse(Sf, Tf, lo, n, per):
            def step(i, _):
                for p in range(per):
                    for ct in range(4):
                        q = row(i * per * RP2 + ((lo + p) * RP2 + 8 + ct * 8))
                        a = Sf[pl.ds(q, 8)]
                        beside = (
                            (Sf[pl.ds(q - RP2, 8)] + Sf[pl.ds(q + RP2, 8)])
                            + (Sf[pl.ds(q - 1, 8)] + Sf[pl.ds(q + 1, 8)])
                            + (pltpu.roll(a, 1, 1) + pltpu.roll(a, 127, 1))
                        )
                        Tf[pl.ds(q, 8)] = (1.0 - W) * a + (C6 * beside + first2 * G2f[pl.ds(q, 8)])
                return 0

            lax.fori_loop(0, n // per, step, 0)

        src, dst = VAf, VBf
        for lo, n, per in ((2, 28, 7), (2, 28, 7), (4, 24, 8), (4, 24, 8), (6, 20, 10)):
            coarse(src, dst, lo, n, per)
            src, dst = dst, src

        f, c = grid(128, 256)
        gap = jnp.abs(jnp.where(c < 192, c, c - 256) - 2 * jnp.where(f < 96, f, f - 128))
        P1 = jnp.where(gap == 0, 1.0, jnp.where(gap == 1, 0.5, 0.0)).astype(F32)
        CZ1f, F1f = flat(b["CZ1"]), flat(b["F1"])
        for k in range(20):
            L[k * 24 : k * 24 + 24, 0:128] = src[pl.ds((k + 6) * RP2 + 12, 24)]
        res = jnp.dot(L[0:480, 0:128], P1, precision=HIGH, preferred_element_type=F32)
        for k in range(20):
            for t in range(2):
                b["CZ1"][k, t, 0:24] = res[k * 24 : k * 24 + 24, t * 128 : t * 128 + 128]

        def widen1(k, _):
            for t in range(2):
                for ct in range(3):
                    q = k * 64 + (t * 32 + ct * 8)
                    v, n = CZ1f[pl.ds(q, 8)], CZ1f[pl.ds(q + 1, 8)]
                    o = k * PS1 + (t * RP1 + 4 + 16 * ct)
                    F1f[pl.ds(o, 8, stride=2)] = v
                    F1f[pl.ds(o + 1, 8, stride=2)] = 0.5 * (v + n)
            return 0

        lax.fori_loop(0, 20, widen1, 0)

        def correct1(k, _):
            for t in range(2):
                for ct in range(5):
                    o = t * RP1 + 8 + ct * 8
                    v = F1f[pl.ds(row(k * PS1 + o), 8)]
                    n = F1f[pl.ds(row((k + 1) * PS1 + o), 8)]
                    q = row(2 * k * PS1 + o)
                    WAf[pl.ds(q, 8)] = WAf[pl.ds(q, 8)] + v
                    q = row((2 * k + 1) * PS1 + o)
                    WAf[pl.ds(q, 8)] = WAf[pl.ds(q, 8)] + 0.5 * (v + n)
            return 0

        lax.fori_loop(0, 20, correct1, 0)

        def relax1(a, beside, g):
            return (1.0 - W) * a + (C6 * beside + first * g)

        def put_l(r, t, ct, s, v):
            L[pl.ds(row(r + ct * 8), 8), t * 128 : t * 128 + 128] = v

        ring1(WAf, relax1, put1(WBf), -2, 34)
        ring1(WBf, relax1, put_l, -1, 33)

        f, c = grid(256, 384)
        gap = jnp.abs(jnp.where(c < 256, c, jnp.where(c == 383, 256, jnp.where(c == 256, -1, 9999))) - 2 * jnp.where(f < 192, f, f - 256))
        P0 = jnp.where(gap == 0, 1.0, jnp.where(gap == 1, 0.5, 0.0)).astype(F32)
        CZ0f, F0f = flat(b["CZ0"]), flat(b["F0"])

        def pz0(i, _):
            res = jnp.dot(L[pl.ds(row(i * 680), 680), :], P0, precision=HIGH, preferred_element_type=F32)
            for p in range(17):
                for t in range(3):
                    CZ0f[pl.ds(row((i * 17 + p) * 144 + t * 48), 40)] = res[p * 40 : p * 40 + 40, t * 128 : t * 128 + 128]
            return 0

        lax.fori_loop(0, 2, pz0, 0)

        def widen0(k, _):
            for t in range(3):
                for ct in range(5):
                    q = k * 144 + (t * 48 + ct * 8)
                    v, n = CZ0f[pl.ds(q, 8)], CZ0f[pl.ds(q + 1, 8)]
                    o = k * 240 + (t * 80 + 16 * ct)
                    F0f[pl.ds(o, 8, stride=2)] = v
                    F0f[pl.ds(o + 1, 8, stride=2)] = 0.5 * (v + n)
            return 0

        lax.fori_loop(0, 34, widen0, 0)

        def add0(plane, t, r, v):
            q = pl.ds(row(plane * PS0 + t * RP0 + r), 8)
            Af[q] = Af[q] + v

        def get0(k, t, r):
            return F0f[pl.ds(row(k * 240 + t * 80 + r), 8)]

        for t in range(2):
            for r in range(8, 72, 8):
                add0(0, t, r, 0.5 * (get0(0, t, r) + get0(1, t, r)))
                add0(65, t, r, get0(33, t, r))

        def correct0(k, _):
            for i in (2 * k, 2 * k + 1):
                for t in range(2):
                    for r in range(0, 80, 8):
                        v, n = get0(i + 1, t, r), get0(i + 2, t, r)
                        add0(2 * i + 1, t, r, v)
                        add0(2 * i + 2, t, r, 0.5 * (v + n))
            for yt in range(8):
                h = b["HR"][2, 0, yt * 8 : yt * 8 + 8]
                for i in (2 * k, 2 * k + 1):
                    v, n = get0(i + 1, 2, 8 + yt * 8), get0(i + 2, 2, 8 + yt * 8)
                    for x, w in ((2 * i, v), (2 * i + 1, 0.5 * (v + n))):
                        h = h + jnp.where(half == x, pltpu.roll(w, jnp.bitwise_and(2 * x, 127), 1), 0.0)
                b["HR"][2, 0, yt * 8 : yt * 8 + 8] = h
            return 0

        lax.fori_loop(0, 16, correct0, 0)

        stencil(Af, Bf, 2, relax0, 3)
        msgs = faces(B, 3)
        tile = total_wait(2, sum_msgs)
        mean = jnp.sum(tile, keepdims=True) / cells
        mean = jnp.broadcast_to(mean, (8, 128))
        for m in msgs:
            m.wait()
        merge(3)
        stencil(Bf, None, 3, lambda c, beside, g: relax0(c, beside, g) - mean)

    return kernel, scratch


def solution(mesh):
    nx, ny, nz = (mesh.shape[a] for a in ("gx", "gy", "gz"))
    kernel, scratch = make_kernel(nx, ny, nz)

    def shards(right_side, initial_guess):
        assert right_side.shape == (64, 64, 256)
        return pl.pallas_call(
            kernel,
            out_shape=pltpu.VMEM(right_side.shape, F32),
            in_specs=[pl.BlockSpec(memory_space=pl.ANY)] * 2,
            out_specs=pl.BlockSpec(memory_space=pltpu.VMEM),
            scratch_shapes=scratch,
            compiler_params=pltpu.CompilerParams(collective_id=0, has_side_effects=True, vmem_limit_bytes=54 << 20),
        )(right_side, initial_guess)

    placed = P("gx", "gy", "gz")
    return jax.shard_map(shards, mesh=mesh, in_specs=(placed, placed), out_specs=placed, check_vma=False)
```

```python
import itertools

import jax
import jax.numpy as jnp
from jax import lax
from jax.experimental import pallas as pl
from jax.experimental.pallas import tpu as pltpu
from jax.sharding import PartitionSpec as P

F32 = jnp.float32
MESH = pl.DeviceIdType.MESH
COARSE_SWEEPS = 6
W = 0.8
C6 = W / 6.0
HIGH = lax.Precision.HIGHEST

N0, RP0 = 64, 96
PS0 = 2 * RP0
N1, H1, RP1, RO1 = 32, 4, 56, 12
PS1 = 2 * RP1
N2, H2, RP2, RO2 = 16, 8, 48, 16

XS1 = {1: (28, 5), 0: (0, 33), -1: (0, 4)}
GS1 = {1: (1, 2), 0: (0, 3), -1: (0, 1)}
XS2 = {1: (8, 8), 0: (0, 16), -1: (0, 8)}
GS2 = {1: (1, 1), 0: (0, 2), -1: (0, 1)}
PAD8 = {5: 8, 33: 40, 4: 8}
XY = [d for d in itertools.product((-1, 0, 1), repeat=2)]
XY8 = [d for d in XY if d != (0, 0)]
NEAR = [d for d in itertools.product((-1, 0, 1), repeat=3) if d != (0, 0, 0)]


def shift_weight():
    total = 0.0
    for level in range(2):
        total += 4 * W / (6.0 * 0.25**level)
    return total + COARSE_SWEEPS * W / (6.0 * 0.0625)


def make_kernel(nx, ny, nz):
    cells = float(nx * N0 * ny * N0 * nz * 256)
    peers = [d for d in NEAR if sum(map(abs, d)) == 1]
    ring = {0: [(0, 0, k) for k in range(1, nz)], 1: [(0, k, 0) for k in range(1, ny)], 2: [(k, 0, 0) for k in range(1, nx)]}
    n_sem = [0]

    scratch, names = [], []

    def vm(name, *shape):
        names.append(name)
        scratch.append(pltpu.VMEM(shape, F32))

    vm("A", 66, 2, RP0, 128)
    vm("B", 67, 2, RP0, 128)
    vm("G", 64, 2, 64, 128)
    vm("PK", 4, 64, 128)
    vm("HR", 4, 2, 64, 128)
    vm("L", 1360, 256)
    vm("G1", 41, 2, RP1, 128)
    vm("WA", 41, 2, RP1, 128)
    vm("WB", 41, 2, RP1, 128)
    vm("U", 3, 40, 128)
    vm("D", 3, 40, 128)
    vm("G2", 32, RP2, 128)
    vm("VA", 33, RP2, 128)
    vm("VB", 33, RP2, 128)
    vm("PZ2", 2, 16, 128)
    vm("RZ2", 2, 4, 32, 128)
    vm("CZ1", 21, 2, 32, 128)
    vm("F1", 21, 2, RP1, 128)
    vm("CZ0", 34, 3, 48, 128)
    vm("F0", 34, 3, 80, 128)
    vm("TS", 3, 8, 128)
    vm("TR0", max(nz - 1, 1), 8, 128)
    vm("TR1", max(ny - 1, 1), 8, 128)
    vm("TR2", max(nx - 1, 1), 8, 128)
    for dx, dy in XY8:
        vm(("RT", dx, dy), XS1[dx][1], PAD8[XS1[dy][1]], 128)
        vm(("RU0", dx, dy), GS1[dx][1], PAD8[XS1[dy][1]], 128)
    for dx, dy in XY:
        vm(("RU1", dx, dy), GS1[dx][1], PAD8[XS1[dy][1]], 128)
        vm(("RD", dx, dy), GS1[dx][1], PAD8[XS1[dy][1]], 128)
    N_MSG = 4 * 26 + 34 + 26 + (nx - 1) + (ny - 1) + (nz - 1)
    scratch += [pltpu.SemaphoreType.DMA((N_MSG,)), pltpu.SemaphoreType.DMA((N_MSG,)), pltpu.SemaphoreType.DMA((8,))]

    def kernel(g_hbm, v_hbm, out_ref, *refs):
        b = dict(zip(names, refs))
        send, recv, local = refs[len(names):]
        A, B, G = b["A"], b["B"], b["G"]
        me = (lax.axis_index("gx"), lax.axis_index("gy"), lax.axis_index("gz"))
        sizes = (nx, ny, nz)
        lane = lax.broadcasted_iota(jnp.int32, (8, 128), 1)
        l0, l127 = lane == 0, lane == 127
        zero = jnp.zeros((8, 128), F32)
        used = [26 * 4]
        refs_of = {}

        def at(d):
            return tuple(lax.rem(m + (k + n), n) if k else m for m, k, n in zip(me, d, sizes))

        def post(src, dst, d):
            k = used[0]
            used[0] += 1
            c = pltpu.make_async_remote_copy(
                src_ref=src, dst_ref=dst, send_sem=send.at[k], recv_sem=recv.at[k], device_id=at(d), device_id_type=MESH
            )
            c.start()
            return c

        def flat(ref):
            s = ref.shape
            n = 1
            for k in s[:-1]:
                n *= k
            return ref.reshape(n, s[-1])

        def row(k, m=8):
            return pl.multiple_of(k, m)

        Af, Bf, Gf = flat(A), flat(B), flat(G)
        refs_of.update({id(Af): A, id(Bf): B})
        G1f, WAf, WBf = flat(b["G1"]), flat(b["WA"]), flat(b["WB"])

        def clear(ref):
            f = flat(ref)
            n = f.shape[0] // 8
            per = 1
            for k in range(16, 0, -1):
                if n % k == 0:
                    per = k
                    break

            def step(i, _):
                for k in range(per):
                    f[pl.ds(row((i * per + k) * 8), 8)] = zero
                return 0

            lax.fori_loop(0, n // per, step, 0)

        barrier = pltpu.get_barrier_semaphore()
        for d in peers:
            pl.semaphore_signal(barrier, inc=1, device_id=at(d), device_id_type=MESH)
        loads = []
        for t in range(2):
            loads.append(pltpu.make_async_copy(v_hbm.at[:, :, t * 128 : t * 128 + 128], A.at[1:65, t, 8:72, :], local.at[t]))
            loads.append(pltpu.make_async_copy(g_hbm.at[:, :, t * 128 : t * 128 + 128], G.at[:, t, :, :], local.at[2 + t]))
        for k in (0, 2, 1, 3):
            loads[k].start()
        for name in names:
            if isinstance(name, tuple):
                clear(b[name])
        clear(b["G1"])
        for dst in (B.at[0], B.at[65], B.at[66]):
            clear(dst)

        def clear_rows(i, _):
            for t in range(2):
                Bf[pl.ds(row(i * PS0 + t * RP0), 8)] = zero
                for r in (72, 80, 88):
                    Bf[pl.ds(row(i * PS0 + t * RP0 + r), 8)] = zero
            return 0

        lax.fori_loop(1, 65, clear_rows, 0)
        loads[0].wait()
        loads[2].wait()

        half = jnp.bitwise_and(lane + 1, 127) // 2

        def pair(c):
            return (c, 7 - c)

        def chunk_msgs(V, k, c):
            first_sem = 26 * k
            out = []

            def msg(j, src, dst, d):
                out.append(
                    pltpu.make_async_remote_copy(
                        src_ref=src, dst_ref=dst, send_sem=send.at[j], recv_sem=recv.at[j], device_id=at(d), device_id_type=MESH
                    )
                )

            for m, yt in enumerate(pair(c)):
                r = pl.ds(row(8 + yt * 8), 8)
                msg(first_sem + c * 6 + m, V.at[64, :, r, :], V.at[0, :, r, :], (1, 0, 0))
                msg(first_sem + c * 6 + 2 + m, V.at[1, :, r, :], V.at[65, :, r, :], (-1, 0, 0))
            r = pl.ds(row(c * 16, 16), 16)
            pk = b["PK"].at[k, r, :]
            msg(first_sem + c * 6 + 4, pk, b["HR"].at[k, 0, r, :], (0, 0, 1))
            msg(first_sem + c * 6 + 5, pk, b["HR"].at[k, 1, r, :], (0, 0, -1))
            if isinstance(c, int) and c == 0:
                msg(first_sem + 24, V.at[1:65, :, 71:72, :], V.at[1:65, :, 7:8, :], (0, 1, 0))
                msg(first_sem + 25, V.at[1:65, :, 8:9, :], V.at[1:65, :, 72:73, :], (0, -1, 0))
            return out

        odd = jnp.bitwise_and(lane, 1) == 1

        def take_chunk(V, k, c):
            for m in chunk_msgs(V, k, c):
                m.wait()
            for m in range(2):
                r = pl.ds(row(c * 16 + 8 * m), 8)
                b["HR"][k, 0, r] = jnp.where(odd, pltpu.roll(b["HR"][k, 1, r], 127, 1), pltpu.roll(b["HR"][k, 0, r], 1, 1))

        def put_faces(Df, k, blocks, c):
            for m, yt in enumerate(pair(c)):
                r = pl.ds(row(c * 16 + 8 * m), 8)
                keep = b["PK"][k, r]
                for i in blocks:
                    for p in range(16):
                        x = i * 16 + p
                        q = row((i * 16 + 1) * PS0 + 8 + yt * 8) + p * PS0
                        both = jnp.where(l0, Df[pl.ds(row(q), 8)], Df[pl.ds(row(q + RP0), 8)])
                        both = pltpu.roll(both, jnp.bitwise_and(2 * x, 127), 1)
                        keep = jnp.where(half == x, both, keep)
                b["PK"][k, r] = keep

        def stencil(Vf, Df, k, op, faces_to=None, carry=0, taken=False):
            summed = isinstance(carry, tuple)
            V, Dst = refs_of[id(Vf)], refs_of.get(id(Df))

            def chunk(c, carry):
                if not taken:
                    take_chunk(V, k, c)

                def step(i, carry):
                    base = row((i * 16 + 1) * PS0)
                    if faces_to is not None:
                        put_faces(Df, faces_to, (jnp.maximum(i - 1, 0),), c)
                    for m, yt in enumerate(pair(c)):
                        o = 8 + yt * 8
                        h = b["HR"][k, 0, pl.ds(row(c * 16 + 8 * m), 8)]

                        def get(p, t):
                            return Vf[pl.ds(row(base + o + (p * PS0 + t * RP0)), 8)]

                        below, mid = [get(-1, t) for t in range(2)], [get(0, t) for t in range(2)]
                        for p in range(16):
                            x = i * 16 + p
                            above = [get(p + 1, t) for t in range(2)]
                            e = pltpu.roll(h, jnp.bitwise_and(128 - 2 * x, 127), 1)
                            c0, c1 = mid
                            up0, up1, dn0, dn1 = (pltpu.roll(v, n, 1) for n in (1, 127) for v in (c0, c1))
                            zs = (
                                jnp.where(l0, e, up0) + jnp.where(l127, dn1, dn0),
                                jnp.where(l0, up0, up1) + jnp.where(l127, e, dn1),
                            )
                            for t in range(2):
                                q = base + o + (p * PS0 + t * RP0)
                                ys = Vf[pl.ds(q - 1, 8)] + Vf[pl.ds(q + 1, 8)]
                                beside = (below[t] + above[t]) + ys + zs[t]
                                g = Gf[pl.ds(row(x * 128 + t * 64 + yt * 8), 8)]
                                v = op(mid[t], beside, g)
                                if Df is None:
                                    out_ref[x, pl.ds(row(yt * 8), 8), t * 128 : t * 128 + 128] = v
                                else:
                                    Df[pl.ds(row(q), 8)] = v
                                if summed:
                                    carry = (carry[0] + mid[t], carry[1] + g)
                            below, mid = mid, above
                    return carry

                carry = lax.fori_loop(0, 4, step, carry)
                if faces_to is not None:
                    put_faces(Df, faces_to, (3,), c)
                    for m in chunk_msgs(Dst, faces_to, c):
                        m.start()
                return carry

            return lax.fori_loop(1, 4, chunk, chunk(0, carry))

        def relax0(c, beside, g):
            return (1.0 - W) * c + C6 * (beside + g)

        def defect0(c, beside, g):
            return g - 6.0 * c + beside

        def total_stage(stage, tile):
            b["TS"][stage] = tile
            rec = b[f"TR{stage}"]
            return [post(b["TS"].at[stage], rec.at[j], d) for j, d in enumerate(ring[stage])]

        def total_wait(stage, msgs):
            tile = b["TS"][stage]
            for j, m in enumerate(msgs):
                m.wait()
                tile = tile + b[f"TR{stage}"][j]
            return tile

        def pack_first(n, _):
            i = jnp.bitwise_and(n, 1) * 2
            put_faces(Af, 0, (i, i + 1), n // 2)
            return 0

        lax.fori_loop(0, 8, pack_first, 0)
        pl.semaphore_wait(barrier, len(peers))
        for c in range(4):
            for m in chunk_msgs(A, 0, c):
                m.start()
        loads[1].wait()
        loads[3].wait()
        sums = stencil(Af, Bf, 0, relax0, 1, (zero, zero))
        sum_msgs = total_stage(0, sums[0] + shift_weight() * sums[1])
        stencil(Bf, Af, 1, relax0, 2)
        sum_msgs = total_stage(1, total_wait(0, sum_msgs))

        stencil(Af, Bf, 2, defect0)

        def clear_rims(i, _):
            for t in range(2):
                Bf[pl.ds(i * PS0 + t * RP0 + 7, 1)] = zero[0:1]
                Bf[pl.ds(i * PS0 + t * RP0 + 72, 1)] = zero[0:1]
            return 0

        lax.fori_loop(1, 65, clear_rims, 0)
        for dst in (B.at[0], B.at[65]):
            clear(dst)
        L = b["L"]

        def restrict_xy(Df, plane, slab, start):
            rows = []
            for dp in range(3):
                q = plane + dp * slab + start
                lo, on, up = (Df[pl.ds(q + k, 8, stride=2)] for k in range(3))
                rows.append(0.25 * (lo + up) + 0.5 * on)
            return 0.25 * (rows[0] + rows[2]) + 0.5 * rows[1]

        def restrict0(i, _):
            for t in range(2):
                for ct in range(5):
                    L[pl.ds(row(i * 40 + ct * 8), 8), t * 128 : t * 128 + 128] = restrict_xy(
                        Bf, i * 2 * PS0, PS0, t * RP0 + 7 + 16 * ct
                    )
            return 0

        lax.fori_loop(0, 33, restrict0, 0)

        def grid(rows, cols):
            return (
                lax.broadcasted_iota(jnp.int32, (rows, cols), 0),
                lax.broadcasted_iota(jnp.int32, (rows, cols), 1),
            )

        f, c = grid(256, 256)
        gap = jnp.abs(f - 2 * c)
        R0 = jnp.where(gap == 0, 0.5, jnp.where(gap == 1, 0.25, 0.0)).astype(F32)

        def rz0(i, _):
            res = jnp.dot(L[pl.ds(row(i * 440), 440), :], R0, precision=HIGH, preferred_element_type=F32)
            for p in range(11):
                for t in range(2):
                    for ct in range(5):
                        G1f[pl.ds((i * 11 + (p + H1)) * PS1 + (t * RP1 + RO1 + ct * 8), 8)] = res[
                            p * 40 + ct * 8 : p * 40 + ct * 8 + 8, t * 128 : t * 128 + 128
                        ]
            return 0

        lax.fori_loop(0, 3, rz0, 0)

        slot8 = lane // 8
        for grp in range(3):
            for ct in range(5):
                up = dn = zero
                for j in range(16 if grp < 2 else 1):
                    q = (grp * 16 + j + H1) * PS1 + RO1 + ct * 8
                    t0, e = G1f[q : q + 8], G1f[q + RP1 : q + RP1 + 8]
                    up = jnp.where(slot8 == j, pltpu.roll(jnp.where(l0, e, t0), (4 + 8 * j) % 128, 1), up)
                    dn = jnp.where(slot8 == j, pltpu.roll(t0, 8 * j, 1) if j else t0, dn)
                b["U"][grp, ct * 8 : ct * 8 + 8] = up
                b["D"][grp, ct * 8 : ct * 8 + 8] = dn
        G1 = b["G1"]
        msgs1 = []

        def along(spec, k, off=0):
            return slice(spec[k][0] + off, spec[k][0] + off + spec[k][1])

        for dx, dy in XY:
            n = XS1[dy][1]
            ys = along(XS1, dy)
            gs = along(GS1, dx)
            if (dx, dy) != (0, 0):
                msgs1.append(
                    post(G1.at[along(XS1, dx, H1), 0, along(XS1, dy, RO1), :], b["RT", dx, dy].at[:, 0:n, :], (dx, dy, 0))
                )
                msgs1.append(post(b["U"].at[gs, ys, :], b["RU0", dx, dy].at[:, 0:n, :], (dx, dy, 0)))
            msgs1.append(post(b["U"].at[gs, ys, :], b["RU1", dx, dy].at[:, 0:n, :], (dx, dy, 1)))
            msgs1.append(post(b["D"].at[gs, ys, :], b["RD", dx, dy].at[:, 0:n, :], (dx, dy, -1)))
        sum_msgs = total_stage(2, total_wait(1, sum_msgs))
        for m in msgs1:
            m.wait()

        def add1(q, v):
            G1f[pl.ds(q, 8)] = G1f[pl.ds(q, 8)] + v

        for dx, dy in XY:
            sx, n = XS1[dx]
            sy = XS1[dy][0]
            tiles = PAD8[XS1[dy][1]] // 8
            g0 = GS1[dx][0]
            per = 11 if n == 33 else n

            def unpack(i, _, dx=dx, dy=dy, sx=sx, sy=sy, tiles=tiles, g0=g0, per=per):
                for p in range(per):
                    k = i * per + p
                    s = k + sx
                    grp, j = s // 16 - g0, s % 16 if isinstance(s, int) else jnp.bitwise_and(s, 15)
                    up = (124 - 8 * j) % 128 if isinstance(s, int) else jnp.bitwise_and(124 - 8 * j, 127)
                    down = (128 - 8 * j) % 128 if isinstance(s, int) else jnp.bitwise_and(128 - 8 * j, 127)
                    for ct in range(tiles):
                        q = i * per * PS1 + ((p + (sx - N1 * dx + H1)) * PS1 + (sy - N1 * dy + RO1 + ct * 8))
                        u1 = pltpu.roll(b["RU1", dx, dy][grp, ct * 8 : ct * 8 + 8], up, 1)
                        dn = pltpu.roll(b["RD", dx, dy][grp, ct * 8 : ct * 8 + 8], down, 1)
                        e = jnp.where(lane >= 124, u1, jnp.where(lane < 4, dn, 0.0))
                        t0 = jnp.where(l0, u1, 0.0)
                        if (dx, dy) != (0, 0):
                            u0 = pltpu.roll(b["RU0", dx, dy][grp, ct * 8 : ct * 8 + 8], up, 1)
                            e = e + jnp.where(l0, u0, 0.0)
                            t0 = t0 + b["RT", dx, dy][k, ct * 8 : ct * 8 + 8]
                        add1(q, t0)
                        add1(q + RP1, e)
                return 0

            if n == 33:
                lax.fori_loop(0, 3, unpack, 0)
            else:
                unpack(0, 0)

        def ring1(Vf, op, emit, lo, hi):
            per = 3 if (hi - lo) % 3 == 0 else 2

            def step(i, _):
                for p in range(per):
                    base = i * per * PS1
                    for ct in range(5):
                        q = row(base + ((p + lo + H1) * PS1 + 8 + ct * 8))
                        c = (Vf[pl.ds(q, 8)], Vf[pl.ds(q + RP1, 8)])
                        up = [pltpu.roll(v, 1, 1) for v in c]
                        dn = [pltpu.roll(v, 127, 1) for v in c]
                        for t in range(2):
                            zs = jnp.where(l0, up[1 - t], up[t]) + jnp.where(l127, dn[1 - t], dn[t])
                            s = q + t * RP1
                            beside = (
                                (Vf[pl.ds(s - PS1, 8)] + Vf[pl.ds(s + PS1, 8)])
                                + (Vf[pl.ds(s - 1, 8)] + Vf[pl.ds(s + 1, 8)])
                                + zs
                            )
                            emit(i * per * 40 + (p + lo + 1) * 40, t, ct, s, op(c[t], beside, G1f[pl.ds(s, 8)]))
                return 0

            lax.fori_loop(0, (hi - lo) // per, step, 0)

        first = W / (6.0 * 0.25)

        def put1(Df):
            def emit(x, t, ct, s, v):
                Df[pl.ds(s, 8)] = v

            return emit

        ring1(G1f, lambda a, beside, g: ((2.0 - W) * first) * a + (C6 * first) * beside, put1(WAf), -3, 35)
        ring1(WAf, lambda a, beside, g: g - 0.25 * (6.0 * a - beside), put1(WBf), -1, 32)

        def restrict1(i, _):
            for t in range(2):
                for ct in range(2):
                    L[pl.ds(row(i * 16 + ct * 8), 8), t * 128 : t * 128 + 128] = restrict_xy(
                        WBf, (2 * i + (H1 - 1)) * PS1, PS1, t * RP1 + RO1 - 1 + 16 * ct
                    )
            return 0

        lax.fori_loop(0, 16, restrict1, 0)
        f, c = grid(256, 128)
        gap = jnp.abs(jnp.where(f < 192, f, f - 256) - 2 * c)
        R1 = jnp.where(c < 64, jnp.where(gap == 0, 0.5, jnp.where(gap == 1, 0.25, 0.0)), 0.0).astype(F32)
        G2, VA, VB = b["G2"], b["VA"], b["VB"]
        G2f, VAf, VBf = flat(G2), flat(VA), flat(VB)
        res = jnp.dot(L[0:256, :], R1, precision=HIGH, preferred_element_type=F32)
        slot16 = lane // 16
        for x in range(16):
            for ct in range(2):
                G2[x + H2, RO2 + ct * 8 : RO2 + ct * 8 + 8] = res[x * 16 + ct * 8 : x * 16 + ct * 8 + 8]
        for grp in range(2):
            for ct in range(2):
                acc = zero
                for j in range(8):
                    v = res[(grp * 8 + j) * 16 + ct * 8 : (grp * 8 + j) * 16 + ct * 8 + 8]
                    v = jnp.where(lane < 8, v, pltpu.roll(v, 128 - 48, 1))
                    acc = jnp.where(slot16 == j, pltpu.roll(v, 16 * j, 1) if j else v, acc)
                b["PZ2"][grp, ct * 8 : ct * 8 + 8] = acc
        msgs2 = []
        for dx, dy in XY:
            px, py = along(XS2, dx), along(XS2, dy)
            if (dx, dy) != (0, 0):
                msgs2.append(
                    post(
                        G2.at[along(XS2, dx, H2), along(XS2, dy, RO2), :],
                        G2.at[along(XS2, dx, H2 - N2 * dx), along(XS2, dy, RO2 - N2 * dy), :],
                        (dx, dy, 0),
                    )
                )
            gs = along(GS2, dx)
            gd = along(GS2, dx, 1 - 2 * dx)
            yd = along(XS2, dy, 8 - N2 * dy)
            for side, dz in ((0, 1), (1, -1)):
                msgs2.append(post(b["PZ2"].at[gs, py, :], b["RZ2"].at[side, gd, yd, :], (dx, dy, dz)))
        for m in msgs2:
            m.wait()

        first2 = W / (6.0 * 0.0625)

        def spread(grp, _):
            for ct in range(4):
                m = jnp.where(
                    jnp.bitwise_and(lane, 15) < 8,
                    b["RZ2"][1, grp, ct * 8 : ct * 8 + 8],
                    b["RZ2"][0, grp, ct * 8 : ct * 8 + 8],
                )
                for j in range(8):
                    hi = pltpu.roll(m, (64 - 16 * j) % 128, 1)
                    lo = pltpu.roll(m, 112 - 16 * j, 1) if j < 7 else m
                    r = pl.ds(row((grp * 8 + j) * RP2 + 8 + ct * 8), 8)
                    own = G2f[r]
                    v = jnp.where(lane < 64, own, jnp.where(lane < 72, hi, jnp.where(lane >= 120, lo, 0.0)))
                    G2f[r] = v
                    VAf[r] = first2 * v
            return 0

        lax.fori_loop(0, 4, spread, 0)

        def coarse(Sf, Tf, lo, n, per):
            def step(i, _):
                for p in range(per):
                    for ct in range(4):
                        q = row(i * per * RP2 + ((lo + p) * RP2 + 8 + ct * 8))
                        a = Sf[pl.ds(q, 8)]
                        beside = (
                            (Sf[pl.ds(q - RP2, 8)] + Sf[pl.ds(q + RP2, 8)])
                            + (Sf[pl.ds(q - 1, 8)] + Sf[pl.ds(q + 1, 8)])
                            + (pltpu.roll(a, 1, 1) + pltpu.roll(a, 127, 1))
                        )
                        Tf[pl.ds(q, 8)] = (1.0 - W) * a + (C6 * beside + first2 * G2f[pl.ds(q, 8)])
                return 0

            lax.fori_loop(0, n // per, step, 0)

        src, dst = VAf, VBf
        for lo, n, per in ((2, 28, 7), (2, 28, 7), (4, 24, 8), (4, 24, 8), (6, 20, 10)):
            coarse(src, dst, lo, n, per)
            src, dst = dst, src

        f, c = grid(128, 256)
        gap = jnp.abs(jnp.where(c < 192, c, c - 256) - 2 * jnp.where(f < 96, f, f - 128))
        P1 = jnp.where(gap == 0, 1.0, jnp.where(gap == 1, 0.5, 0.0)).astype(F32)
        CZ1f, F1f = flat(b["CZ1"]), flat(b["F1"])
        for k in range(20):
            L[k * 24 : k * 24 + 24, 0:128] = src[pl.ds((k + 6) * RP2 + 12, 24)]
        res = jnp.dot(L[0:480, 0:128], P1, precision=HIGH, preferred_element_type=F32)
        for k in range(20):
            for t in range(2):
                b["CZ1"][k, t, 0:24] = res[k * 24 : k * 24 + 24, t * 128 : t * 128 + 128]

        def widen1(k, _):
            for t in range(2):
                for ct in range(3):
                    q = k * 64 + (t * 32 + ct * 8)
                    v, n = CZ1f[pl.ds(q, 8)], CZ1f[pl.ds(q + 1, 8)]
                    o = k * PS1 + (t * RP1 + 4 + 16 * ct)
                    F1f[pl.ds(o, 8, stride=2)] = v
                    F1f[pl.ds(o + 1, 8, stride=2)] = 0.5 * (v + n)
            return 0

        lax.fori_loop(0, 20, widen1, 0)

        def correct1(k, _):
            for t in range(2):
                for ct in range(5):
                    o = t * RP1 + 8 + ct * 8
                    v = F1f[pl.ds(row(k * PS1 + o), 8)]
                    n = F1f[pl.ds(row((k + 1) * PS1 + o), 8)]
                    q = row(2 * k * PS1 + o)
                    WAf[pl.ds(q, 8)] = WAf[pl.ds(q, 8)] + v
                    q = row((2 * k + 1) * PS1 + o)
                    WAf[pl.ds(q, 8)] = WAf[pl.ds(q, 8)] + 0.5 * (v + n)
            return 0

        lax.fori_loop(0, 20, correct1, 0)

        def relax1(a, beside, g):
            return (1.0 - W) * a + (C6 * beside + first * g)

        def put_l(r, t, ct, s, v):
            L[pl.ds(row(r + ct * 8), 8), t * 128 : t * 128 + 128] = v

        ring1(WAf, relax1, put1(WBf), -2, 34)
        ring1(WBf, relax1, put_l, -1, 33)

        f, c = grid(256, 384)
        gap = jnp.abs(jnp.where(c < 256, c, jnp.where(c == 383, 256, jnp.where(c == 256, -1, 9999))) - 2 * jnp.where(f < 192, f, f - 256))
        P0 = jnp.where(gap == 0, 1.0, jnp.where(gap == 1, 0.5, 0.0)).astype(F32)
        CZ0f, F0f = flat(b["CZ0"]), flat(b["F0"])

        def pz0(i, _):
            res = jnp.dot(L[pl.ds(row(i * 680), 680), :], P0, precision=HIGH, preferred_element_type=F32)
            for p in range(17):
                for t in range(3):
                    CZ0f[pl.ds(row((i * 17 + p) * 144 + t * 48), 40)] = res[p * 40 : p * 40 + 40, t * 128 : t * 128 + 128]
            return 0

        lax.fori_loop(0, 2, pz0, 0)

        def widen0(k, _):
            for t in range(3):
                for ct in range(5):
                    q = k * 144 + (t * 48 + ct * 8)
                    v, n = CZ0f[pl.ds(q, 8)], CZ0f[pl.ds(q + 1, 8)]
                    o = k * 240 + (t * 80 + 16 * ct)
                    F0f[pl.ds(o, 8, stride=2)] = v
                    F0f[pl.ds(o + 1, 8, stride=2)] = 0.5 * (v + n)
            return 0

        lax.fori_loop(0, 34, widen0, 0)

        def add0(plane, t, r, v):
            q = pl.ds(row(plane * PS0 + t * RP0 + r), 8)
            Af[q] = Af[q] + v

        def get0(k, t, r):
            return F0f[pl.ds(row(k * 240 + t * 80 + r), 8)]

        for t in range(2):
            for r in range(8, 72, 8):
                add0(0, t, r, 0.5 * (get0(0, t, r) + get0(1, t, r)))
                add0(65, t, r, get0(33, t, r))

        def correct0(k, _):
            for i in (2 * k, 2 * k + 1):
                for t in range(2):
                    for r in range(0, 80, 8):
                        v, n = get0(i + 1, t, r), get0(i + 2, t, r)
                        add0(2 * i + 1, t, r, v)
                        add0(2 * i + 2, t, r, 0.5 * (v + n))
            for yt in range(8):
                place = 16 * yt if yt < 4 else 16 * (7 - yt) + 8
                h = b["HR"][2, 0, place : place + 8]
                for i in (2 * k, 2 * k + 1):
                    v, n = get0(i + 1, 2, 8 + yt * 8), get0(i + 2, 2, 8 + yt * 8)
                    for x, w in ((2 * i, v), (2 * i + 1, 0.5 * (v + n))):
                        h = h + jnp.where(half == x, pltpu.roll(w, jnp.bitwise_and(2 * x, 127), 1), 0.0)
                b["HR"][2, 0, place : place + 8] = h
            return 0

        lax.fori_loop(0, 16, correct0, 0)

        stencil(Af, Bf, 2, relax0, 3, taken=True)
        tile = total_wait(2, sum_msgs)
        mean = jnp.sum(tile, keepdims=True) / cells
        mean = jnp.broadcast_to(mean, (8, 128))
        stencil(Bf, None, 3, lambda c, beside, g: relax0(c, beside, g) - mean)

    return kernel, scratch


def solution(mesh):
    nx, ny, nz = (mesh.shape[a] for a in ("gx", "gy", "gz"))
    kernel, scratch = make_kernel(nx, ny, nz)

    def shards(right_side, initial_guess):
        assert right_side.shape == (64, 64, 256)
        return pl.pallas_call(
            kernel,
            out_shape=pltpu.VMEM(right_side.shape, F32),
            in_specs=[pl.BlockSpec(memory_space=pl.ANY)] * 2,
            out_specs=pl.BlockSpec(memory_space=pltpu.VMEM),
            scratch_shapes=scratch,
            compiler_params=pltpu.CompilerParams(collective_id=0, has_side_effects=True, vmem_limit_bytes=54 << 20),
        )(right_side, initial_guess)

    placed = P("gx", "gy", "gz")
    return jax.shard_map(shards, mesh=mesh, in_specs=(placed, placed), out_specs=placed, check_vma=False)
```

```python
import itertools

import jax
import jax.numpy as jnp
from jax import lax
from jax.experimental import pallas as pl
from jax.experimental.pallas import tpu as pltpu
from jax.sharding import PartitionSpec as P

F32 = jnp.float32
MESH = pl.DeviceIdType.MESH
COARSE_SWEEPS = 6
W = 0.8
C6 = W / 6.0
BF16 = jnp.bfloat16

N0, RP0 = 64, 96
PS0 = 2 * RP0
N1, H1, RP1, RO1 = 32, 4, 56, 12
PS1 = 2 * RP1
N2, H2, RP2, RO2 = 16, 8, 48, 16

XS1 = {1: (28, 5), 0: (0, 33), -1: (0, 4)}
GS1 = {1: (1, 2), 0: (0, 3), -1: (0, 1)}
XS2 = {1: (8, 8), 0: (0, 16), -1: (0, 8)}
GS2 = {1: (1, 1), 0: (0, 2), -1: (0, 1)}
PAD8 = {5: 8, 33: 40, 4: 8}
XY = [d for d in itertools.product((-1, 0, 1), repeat=2)]
XY8 = [d for d in XY if d != (0, 0)]
NEAR = [d for d in itertools.product((-1, 0, 1), repeat=3) if d != (0, 0, 0)]


def shift_weight():
    total = 0.0
    for level in range(2):
        total += 4 * W / (6.0 * 0.25**level)
    return total + COARSE_SWEEPS * W / (6.0 * 0.0625)


def make_kernel(nx, ny, nz):
    cells = float(nx * N0 * ny * N0 * nz * 256)
    peers = [d for d in NEAR if sum(map(abs, d)) == 1]
    ring = {0: [(0, 0, k) for k in range(1, nz)], 1: [(0, k, 0) for k in range(1, ny)], 2: [(k, 0, 0) for k in range(1, nx)]}
    n_sem = [0]

    scratch, names = [], []

    def vm(name, *shape):
        names.append(name)
        scratch.append(pltpu.VMEM(shape, F32))

    vm("A", 66, 2, RP0, 128)
    vm("B", 66, 2, RP0, 128)
    vm("C", 67, 2, RP0, 128)
    vm("G", 64, 2, 64, 128)
    vm("PK", 4, 64, 128)
    vm("HR", 4, 2, 64, 128)
    vm("L", 1360, 256)
    vm("G1", 42, 2, RP1, 128)
    vm("WA", 42, 2, RP1, 128)
    vm("WB", 42, 2, RP1, 128)
    vm("U", 3, 40, 128)
    vm("D", 3, 40, 128)
    vm("G2", 32, RP2, 128)
    vm("VA", 33, RP2, 128)
    vm("VB", 33, RP2, 128)
    vm("PZ2", 2, 16, 128)
    vm("RZ2", 2, 4, 32, 128)
    vm("CZ1", 21, 2, 32, 128)
    vm("F1", 21, 2, RP1, 128)
    vm("CZ0", 34, 3, 48, 128)
    vm("F0", 34, 3, 80, 128)
    vm("TS", 3, 8, 128)
    vm("TR0", max(nz - 1, 1), 8, 128)
    vm("TR1", max(ny - 1, 1), 8, 128)
    vm("TR2", max(nx - 1, 1), 8, 128)
    for dx, dy in XY8:
        vm(("RT", dx, dy), XS1[dx][1], PAD8[XS1[dy][1]], 128)
        vm(("RU0", dx, dy), GS1[dx][1], PAD8[XS1[dy][1]], 128)
    for dx, dy in XY:
        vm(("RU1", dx, dy), GS1[dx][1], PAD8[XS1[dy][1]], 128)
        vm(("RD", dx, dy), GS1[dx][1], PAD8[XS1[dy][1]], 128)
    N_MSG = 4 * 26 + 34 + 26 + (nx - 1) + (ny - 1) + (nz - 1)
    scratch += [pltpu.SemaphoreType.DMA((N_MSG,)), pltpu.SemaphoreType.DMA((N_MSG,)), pltpu.SemaphoreType.DMA((8,))]

    def kernel(g_hbm, v_hbm, out_ref, *refs):
        b = dict(zip(names, refs))
        send, recv, local = refs[len(names):]
        A, B, C, G = b["A"], b["B"], b["C"], b["G"]
        me = (lax.axis_index("gx"), lax.axis_index("gy"), lax.axis_index("gz"))
        sizes = (nx, ny, nz)
        lane = lax.broadcasted_iota(jnp.int32, (8, 128), 1)
        l0, l127 = lane == 0, lane == 127
        zero = jnp.zeros((8, 128), F32)
        used = [26 * 4]
        refs_of = {}

        def at(d):
            return tuple(lax.rem(m + (k + n), n) if k else m for m, k, n in zip(me, d, sizes))

        def post(src, dst, d):
            k = used[0]
            used[0] += 1
            c = pltpu.make_async_remote_copy(
                src_ref=src, dst_ref=dst, send_sem=send.at[k], recv_sem=recv.at[k], device_id=at(d), device_id_type=MESH
            )
            c.start()
            return c

        def flat(ref):
            s = ref.shape
            n = 1
            for k in s[:-1]:
                n *= k
            return ref.reshape(n, s[-1])

        def row(k, m=8):
            return pl.multiple_of(k, m)

        Af, Bf, Cf, Gf = flat(A), flat(B), flat(C), flat(G)
        refs_of.update({id(Af): A, id(Bf): B})
        G1f, WAf, WBf = flat(b["G1"]), flat(b["WA"]), flat(b["WB"])

        def clear(ref):
            f = flat(ref)
            n = f.shape[0] // 8
            per = 1
            for k in range(16, 0, -1):
                if n % k == 0:
                    per = k
                    break

            def step(i, _):
                for k in range(per):
                    f[pl.ds(row((i * per + k) * 8), 8)] = zero
                return 0

            lax.fori_loop(0, n // per, step, 0)

        barrier = pltpu.get_barrier_semaphore()
        for d in peers:
            pl.semaphore_signal(barrier, inc=1, device_id=at(d), device_id_type=MESH)
        loads = []
        for t in range(2):
            loads.append(pltpu.make_async_copy(v_hbm.at[:, :, t * 128 : t * 128 + 128], A.at[1:65, t, 8:72, :], local.at[t]))
            loads.append(pltpu.make_async_copy(g_hbm.at[:, :, t * 128 : t * 128 + 128], G.at[:, t, :, :], local.at[2 + t]))
        for k in (0, 2, 1, 3):
            loads[k].start()
        for name in names:
            if isinstance(name, tuple):
                clear(b[name])
        clear(b["G1"])
        for dst in (C.at[0], C.at[65], C.at[66]):
            clear(dst)

        def clear_rows(i, _):
            for t in range(2):
                for r in (0, 72, 80, 88):
                    Cf[pl.ds(row(i * PS0 + t * RP0 + r), 8)] = zero
            return 0

        lax.fori_loop(1, 65, clear_rows, 0)
        loads[0].wait()
        loads[2].wait()

        half = jnp.bitwise_and(lane + 1, 127) // 2

        def pair(c):
            return (c, 7 - c)

        def chunk_msgs(V, k, c):
            first_sem = 26 * k
            out = []

            def msg(j, src, dst, d):
                out.append(
                    pltpu.make_async_remote_copy(
                        src_ref=src, dst_ref=dst, send_sem=send.at[j], recv_sem=recv.at[j], device_id=at(d), device_id_type=MESH
                    )
                )

            for m, yt in enumerate(pair(c)):
                r = pl.ds(row(8 + yt * 8), 8)
                msg(first_sem + c * 6 + m, V.at[64, :, r, :], V.at[0, :, r, :], (1, 0, 0))
                msg(first_sem + c * 6 + 2 + m, V.at[1, :, r, :], V.at[65, :, r, :], (-1, 0, 0))
            r = pl.ds(row(c * 16, 16), 16)
            pk = b["PK"].at[k, r, :]
            msg(first_sem + c * 6 + 4, pk, b["HR"].at[k, 0, r, :], (0, 0, 1))
            msg(first_sem + c * 6 + 5, pk, b["HR"].at[k, 1, r, :], (0, 0, -1))
            if isinstance(c, int) and c == 0:
                msg(first_sem + 24, V.at[1:65, :, 71:72, :], V.at[1:65, :, 7:8, :], (0, 1, 0))
                msg(first_sem + 25, V.at[1:65, :, 8:9, :], V.at[1:65, :, 72:73, :], (0, -1, 0))
            return out

        odd = jnp.bitwise_and(lane, 1) == 1

        def take_chunk(V, k, c):
            for m in chunk_msgs(V, k, c):
                m.wait()
            for m in range(2):
                r = pl.ds(row(c * 16 + 8 * m), 8)
                b["HR"][k, 0, r] = jnp.where(odd, pltpu.roll(b["HR"][k, 1, r], 127, 1), pltpu.roll(b["HR"][k, 0, r], 1, 1))

        def put_faces(Df, k, blocks, c):
            for m, yt in enumerate(pair(c)):
                r = pl.ds(row(c * 16 + 8 * m), 8)
                keep = b["PK"][k, r]
                for i in blocks:
                    for p in range(16):
                        x = i * 16 + p
                        q = row((i * 16 + 1) * PS0 + 8 + yt * 8) + p * PS0
                        both = jnp.where(l0, Df[pl.ds(row(q), 8)], Df[pl.ds(row(q + RP0), 8)])
                        both = pltpu.roll(both, jnp.bitwise_and(2 * x, 127), 1)
                        keep = jnp.where(half == x, both, keep)
                b["PK"][k, r] = keep

        def stencil(Vf, Df, k, op, faces_to=None, carry=0, taken=False):
            summed = isinstance(carry, tuple)
            V, Dst = refs_of[id(Vf)], refs_of.get(id(Df))

            def chunk(c, carry):
                if not taken:
                    take_chunk(V, k, c)

                def step(i, carry):
                    base = row((i * 16 + 1) * PS0)
                    if faces_to is not None:
                        put_faces(Df, faces_to, (jnp.maximum(i - 1, 0),), c)
                    for m, yt in enumerate(pair(c)):
                        o = 8 + yt * 8
                        h = b["HR"][k, 0, pl.ds(row(c * 16 + 8 * m), 8)]

                        def get(p, t):
                            return Vf[pl.ds(row(base + o + (p * PS0 + t * RP0)), 8)]

                        below, mid = [get(-1, t) for t in range(2)], [get(0, t) for t in range(2)]
                        for p in range(16):
                            x = i * 16 + p
                            above = [get(p + 1, t) for t in range(2)]
                            e = pltpu.roll(h, jnp.bitwise_and(128 - 2 * x, 127), 1)
                            c0, c1 = mid
                            up0, up1, dn0, dn1 = (pltpu.roll(v, n, 1) for n in (1, 127) for v in (c0, c1))
                            zs = (
                                jnp.where(l0, e, up0) + jnp.where(l127, dn1, dn0),
                                jnp.where(l0, up0, up1) + jnp.where(l127, e, dn1),
                            )
                            for t in range(2):
                                q = base + o + (p * PS0 + t * RP0)
                                ys = Vf[pl.ds(q - 1, 8)] + Vf[pl.ds(q + 1, 8)]
                                beside = (below[t] + above[t]) + ys + zs[t]
                                g = Gf[pl.ds(row(x * 128 + t * 64 + yt * 8), 8)]
                                v = op(mid[t], beside, g)
                                if Df is None:
                                    out_ref[x, pl.ds(row(yt * 8), 8), t * 128 : t * 128 + 128] = v
                                else:
                                    Df[pl.ds(row(q), 8)] = v
                                if summed:
                                    carry = (carry[0] + mid[t], carry[1] + g)
                            below, mid = mid, above
                    return carry

                carry = lax.fori_loop(0, 4, step, carry)
                if faces_to is not None:
                    put_faces(Df, faces_to, (3,), c)
                    for m in chunk_msgs(Dst, faces_to, c):
                        m.start()
                return carry

            return lax.fori_loop(1, 4, chunk, chunk(0, carry))

        def relax0(c, beside, g):
            return (1.0 - W) * c + C6 * (beside + g)

        def defect0(c, beside, g):
            return g - 6.0 * c + beside

        def total_stage(stage, tile):
            b["TS"][stage] = tile
            rec = b[f"TR{stage}"]
            return [post(b["TS"].at[stage], rec.at[j], d) for j, d in enumerate(ring[stage])]

        def total_wait(stage, msgs):
            tile = b["TS"][stage]
            for j, m in enumerate(msgs):
                m.wait()
                tile = tile + b[f"TR{stage}"][j]
            return tile

        def pack_first(n, _):
            i = jnp.bitwise_and(n, 1) * 2
            put_faces(Af, 0, (i, i + 1), n // 2)
            return 0

        lax.fori_loop(0, 8, pack_first, 0)
        pl.semaphore_wait(barrier, len(peers))
        for c in range(4):
            for m in chunk_msgs(A, 0, c):
                m.start()
        loads[1].wait()
        loads[3].wait()
        sums = stencil(Af, Bf, 0, relax0, 1, (zero, zero))
        sum_msgs = total_stage(0, sums[0] + shift_weight() * sums[1])
        stencil(Bf, Af, 1, relax0, 2)
        sum_msgs = total_stage(1, total_wait(0, sum_msgs))

        stencil(Af, Cf, 2, defect0)

        L = b["L"]

        def restrict_xy(Df, plane, slab, start):
            rows = []
            for dp in range(3):
                q = plane + dp * slab + start
                lo, on, up = (Df[pl.ds(q + k, 8, stride=2)] for k in range(3))
                rows.append(0.25 * (lo + up) + 0.5 * on)
            return 0.25 * (rows[0] + rows[2]) + 0.5 * rows[1]

        def restrict0(i, _):
            for t in range(2):
                for ct in range(5):
                    L[pl.ds(row(i * 40 + ct * 8), 8), t * 128 : t * 128 + 128] = restrict_xy(
                        Cf, i * 2 * PS0, PS0, t * RP0 + 7 + 16 * ct
                    )
            return 0

        lax.fori_loop(0, 33, restrict0, 0)

        def exact_dot(x, weights):
            hi = x.astype(BF16)
            rest = x - hi.astype(F32)
            mid = rest.astype(BF16)
            lo = (rest - mid.astype(F32)).astype(BF16)
            return sum(jnp.dot(part, weights, preferred_element_type=F32) for part in (lo, mid, hi))

        def grid(rows, cols):
            return (
                lax.broadcasted_iota(jnp.int32, (rows, cols), 0),
                lax.broadcasted_iota(jnp.int32, (rows, cols), 1),
            )

        f, c = grid(256, 256)
        gap = jnp.abs(f - 2 * c)
        R0 = jnp.where(gap == 0, 0.5, jnp.where(gap == 1, 0.25, 0.0)).astype(BF16)

        def rz0(i, _):
            res = exact_dot(L[pl.ds(row(i * 440), 440), :], R0)
            for p in range(11):
                for t in range(2):
                    for ct in range(5):
                        G1f[pl.ds((i * 11 + (p + H1)) * PS1 + (t * RP1 + RO1 + ct * 8), 8)] = res[
                            p * 40 + ct * 8 : p * 40 + ct * 8 + 8, t * 128 : t * 128 + 128
                        ]
            return 0

        lax.fori_loop(0, 3, rz0, 0)

        slot8 = lane // 8
        for grp in range(3):
            for ct in range(5):
                up = dn = zero
                for j in range(16 if grp < 2 else 1):
                    q = (grp * 16 + j + H1) * PS1 + RO1 + ct * 8
                    t0, e = G1f[q : q + 8], G1f[q + RP1 : q + RP1 + 8]
                    up = jnp.where(slot8 == j, pltpu.roll(jnp.where(l0, e, t0), (4 + 8 * j) % 128, 1), up)
                    dn = jnp.where(slot8 == j, pltpu.roll(t0, 8 * j, 1) if j else t0, dn)
                b["U"][grp, ct * 8 : ct * 8 + 8] = up
                b["D"][grp, ct * 8 : ct * 8 + 8] = dn
        G1 = b["G1"]
        msgs1 = []

        def along(spec, k, off=0):
            return slice(spec[k][0] + off, spec[k][0] + off + spec[k][1])

        for dx, dy in sorted(XY, key=lambda d: -abs(d[0]) - abs(d[1])):
            n = XS1[dy][1]
            ys = along(XS1, dy)
            gs = along(GS1, dx)
            msgs1.append(post(b["U"].at[gs, ys, :], b["RU1", dx, dy].at[:, 0:n, :], (dx, dy, 1)))
            msgs1.append(post(b["D"].at[gs, ys, :], b["RD", dx, dy].at[:, 0:n, :], (dx, dy, -1)))
        for dx, dy in sorted(XY, key=lambda d: -abs(d[0]) - abs(d[1])):
            n = XS1[dy][1]
            ys = along(XS1, dy)
            gs = along(GS1, dx)
            if (dx, dy) != (0, 0):
                msgs1.append(
                    post(G1.at[along(XS1, dx, H1), 0, along(XS1, dy, RO1), :], b["RT", dx, dy].at[:, 0:n, :], (dx, dy, 0))
                )
                msgs1.append(post(b["U"].at[gs, ys, :], b["RU0", dx, dy].at[:, 0:n, :], (dx, dy, 0)))
        sum_msgs = total_stage(2, total_wait(1, sum_msgs))
        for m in msgs1:
            m.wait()

        def add1(q, v):
            G1f[pl.ds(q, 8)] = G1f[pl.ds(q, 8)] + v

        for dx, dy in XY:
            sx, n = XS1[dx]
            sy = XS1[dy][0]
            tiles = PAD8[XS1[dy][1]] // 8
            g0 = GS1[dx][0]
            per = 11 if n == 33 else n

            def unpack(i, _, dx=dx, dy=dy, sx=sx, sy=sy, tiles=tiles, g0=g0, per=per):
                for p in range(per):
                    k = i * per + p
                    s = k + sx
                    grp, j = s // 16 - g0, s % 16 if isinstance(s, int) else jnp.bitwise_and(s, 15)
                    up = (124 - 8 * j) % 128 if isinstance(s, int) else jnp.bitwise_and(124 - 8 * j, 127)
                    down = (128 - 8 * j) % 128 if isinstance(s, int) else jnp.bitwise_and(128 - 8 * j, 127)
                    for ct in range(tiles):
                        q = i * per * PS1 + ((p + (sx - N1 * dx + H1)) * PS1 + (sy - N1 * dy + RO1 + ct * 8))
                        u1 = pltpu.roll(b["RU1", dx, dy][grp, ct * 8 : ct * 8 + 8], up, 1)
                        dn = pltpu.roll(b["RD", dx, dy][grp, ct * 8 : ct * 8 + 8], down, 1)
                        e = jnp.where(lane >= 124, u1, jnp.where(lane < 4, dn, 0.0))
                        t0 = jnp.where(l0, u1, 0.0)
                        if (dx, dy) != (0, 0):
                            u0 = pltpu.roll(b["RU0", dx, dy][grp, ct * 8 : ct * 8 + 8], up, 1)
                            e = e + jnp.where(l0, u0, 0.0)
                            t0 = t0 + b["RT", dx, dy][k, ct * 8 : ct * 8 + 8]
                        add1(q, t0)
                        add1(q + RP1, e)
                return 0

            if n == 33:
                lax.fori_loop(0, 3, unpack, 0)
            else:
                unpack(0, 0)

        def ring1(Vf, op, emit, lo, hi, per):

            def step(i, _):
                for p in range(per):
                    base = i * per * PS1
                    for ct in range(5):
                        q = row(base + ((p + lo + H1) * PS1 + 8 + ct * 8))
                        c = (Vf[pl.ds(q, 8)], Vf[pl.ds(q + RP1, 8)])
                        up = [pltpu.roll(v, 1, 1) for v in c]
                        dn = [pltpu.roll(v, 127, 1) for v in c]
                        for t in range(2):
                            zs = jnp.where(l0, up[1 - t], up[t]) + jnp.where(l127, dn[1 - t], dn[t])
                            s = q + t * RP1
                            beside = (
                                (Vf[pl.ds(s - PS1, 8)] + Vf[pl.ds(s + PS1, 8)])
                                + (Vf[pl.ds(s - 1, 8)] + Vf[pl.ds(s + 1, 8)])
                                + zs
                            )
                            emit(i * per * 40 + (p + lo + 1) * 40, t, ct, s, op(c[t], beside, G1f[pl.ds(s, 8)]))
                return 0

            lax.fori_loop(0, (hi - lo) // per, step, 0)

        first = W / (6.0 * 0.25)

        def put1(Df):
            def emit(x, t, ct, s, v):
                Df[pl.ds(s, 8)] = v

            return emit

        ring1(G1f, lambda a, beside, g: ((2.0 - W) * first) * a + (C6 * first) * beside, put1(WAf), -3, 37, 10)
        ring1(WAf, lambda a, beside, g: g - 0.25 * (6.0 * a - beside), put1(WBf), -1, 32, 11)

        def restrict1(i, _):
            for t in range(2):
                for ct in range(2):
                    L[pl.ds(row(i * 16 + ct * 8), 8), t * 128 : t * 128 + 128] = restrict_xy(
                        WBf, (2 * i + (H1 - 1)) * PS1, PS1, t * RP1 + RO1 - 1 + 16 * ct
                    )
            return 0

        lax.fori_loop(0, 16, restrict1, 0)
        f, c = grid(256, 128)
        gap = jnp.abs(jnp.where(f < 192, f, f - 256) - 2 * c)
        R1 = jnp.where(c < 64, jnp.where(gap == 0, 0.5, jnp.where(gap == 1, 0.25, 0.0)), 0.0).astype(BF16)
        G2, VA, VB = b["G2"], b["VA"], b["VB"]
        G2f, VAf, VBf = flat(G2), flat(VA), flat(VB)
        res = exact_dot(L[0:256, :], R1)
        slot16 = lane // 16
        for x in range(16):
            for ct in range(2):
                G2[x + H2, RO2 + ct * 8 : RO2 + ct * 8 + 8] = res[x * 16 + ct * 8 : x * 16 + ct * 8 + 8]
        for grp in range(2):
            for ct in range(2):
                acc = zero
                for j in range(8):
                    v = res[(grp * 8 + j) * 16 + ct * 8 : (grp * 8 + j) * 16 + ct * 8 + 8]
                    v = jnp.where(lane < 8, v, pltpu.roll(v, 128 - 48, 1))
                    acc = jnp.where(slot16 == j, pltpu.roll(v, 16 * j, 1) if j else v, acc)
                b["PZ2"][grp, ct * 8 : ct * 8 + 8] = acc
        msgs2 = []
        for dx, dy in sorted(XY, key=lambda d: -abs(d[0]) - abs(d[1])):
            py = along(XS2, dy)
            gs = along(GS2, dx)
            gd = along(GS2, dx, 1 - 2 * dx)
            yd = along(XS2, dy, 8 - N2 * dy)
            for side, dz in ((0, 1), (1, -1)):
                msgs2.append(post(b["PZ2"].at[gs, py, :], b["RZ2"].at[side, gd, yd, :], (dx, dy, dz)))
        for dx, dy in sorted(XY8, key=lambda d: -abs(d[0]) - abs(d[1])):
            msgs2.append(
                post(
                    G2.at[along(XS2, dx, H2), along(XS2, dy, RO2), :],
                    G2.at[along(XS2, dx, H2 - N2 * dx), along(XS2, dy, RO2 - N2 * dy), :],
                    (dx, dy, 0),
                )
            )
        for m in msgs2:
            m.wait()

        first2 = W / (6.0 * 0.0625)

        def spread(grp, _):
            for ct in range(4):
                m = jnp.where(
                    jnp.bitwise_and(lane, 15) < 8,
                    b["RZ2"][1, grp, ct * 8 : ct * 8 + 8],
                    b["RZ2"][0, grp, ct * 8 : ct * 8 + 8],
                )
                for j in range(8):
                    hi = pltpu.roll(m, (64 - 16 * j) % 128, 1)
                    lo = pltpu.roll(m, 112 - 16 * j, 1) if j < 7 else m
                    r = pl.ds(row((grp * 8 + j) * RP2 + 8 + ct * 8), 8)
                    own = G2f[r]
                    v = jnp.where(lane < 64, own, jnp.where(lane < 72, hi, jnp.where(lane >= 120, lo, 0.0)))
                    G2f[r] = v
                    VAf[r] = first2 * v
            return 0

        lax.fori_loop(0, 4, spread, 0)

        def coarse(Sf, Tf, lo, n, per):
            def step(i, _):
                for p in range(per):
                    for ct in range(4):
                        q = row(i * per * RP2 + ((lo + p) * RP2 + 8 + ct * 8))
                        a = Sf[pl.ds(q, 8)]
                        beside = (
                            (Sf[pl.ds(q - RP2, 8)] + Sf[pl.ds(q + RP2, 8)])
                            + (Sf[pl.ds(q - 1, 8)] + Sf[pl.ds(q + 1, 8)])
                            + (pltpu.roll(a, 1, 1) + pltpu.roll(a, 127, 1))
                        )
                        Tf[pl.ds(q, 8)] = (1.0 - W) * a + (C6 * beside + first2 * G2f[pl.ds(q, 8)])
                return 0

            lax.fori_loop(0, n // per, step, 0)

        src, dst = VAf, VBf
        for lo, n, per in ((2, 28, 7), (2, 28, 7), (4, 24, 8), (4, 24, 8), (6, 20, 10)):
            coarse(src, dst, lo, n, per)
            src, dst = dst, src

        f, c = grid(128, 256)
        gap = jnp.abs(jnp.where(c < 192, c, c - 256) - 2 * jnp.where(f < 96, f, f - 128))
        P1 = jnp.where(gap == 0, 1.0, jnp.where(gap == 1, 0.5, 0.0)).astype(BF16)
        CZ1f, F1f = flat(b["CZ1"]), flat(b["F1"])
        for k in range(20):
            L[k * 24 : k * 24 + 24, 0:128] = src[pl.ds((k + 6) * RP2 + 12, 24)]
        res = exact_dot(L[0:480, 0:128], P1)
        for k in range(20):
            for t in range(2):
                b["CZ1"][k, t, 0:24] = res[k * 24 : k * 24 + 24, t * 128 : t * 128 + 128]

        def widen1(k, _):
            for t in range(2):
                for ct in range(3):
                    q = k * 64 + (t * 32 + ct * 8)
                    v, n = CZ1f[pl.ds(q, 8)], CZ1f[pl.ds(q + 1, 8)]
                    o = k * PS1 + (t * RP1 + 4 + 16 * ct)
                    F1f[pl.ds(o, 8, stride=2)] = v
                    F1f[pl.ds(o + 1, 8, stride=2)] = 0.5 * (v + n)
            return 0

        lax.fori_loop(0, 20, widen1, 0)

        def correct1(k, _):
            for t in range(2):
                for ct in range(5):
                    o = t * RP1 + 8 + ct * 8
                    v = F1f[pl.ds(row(k * PS1 + o), 8)]
                    n = F1f[pl.ds(row((k + 1) * PS1 + o), 8)]
                    q = row(2 * k * PS1 + o)
                    WAf[pl.ds(q, 8)] = WAf[pl.ds(q, 8)] + v
                    q = row((2 * k + 1) * PS1 + o)
                    WAf[pl.ds(q, 8)] = WAf[pl.ds(q, 8)] + 0.5 * (v + n)
            return 0

        lax.fori_loop(0, 20, correct1, 0)

        def relax1(a, beside, g):
            return (1.0 - W) * a + (C6 * beside + first * g)

        def put_l(r, t, ct, s, v):
            L[pl.ds(row(r + ct * 8), 8), t * 128 : t * 128 + 128] = v

        ring1(WAf, relax1, put1(WBf), -2, 34, 9)
        ring1(WBf, relax1, put_l, -1, 33, 17)

        f, c = grid(256, 384)
        gap = jnp.abs(jnp.where(c < 256, c, jnp.where(c == 383, 256, jnp.where(c == 256, -1, 9999))) - 2 * jnp.where(f < 192, f, f - 256))
        P0 = jnp.where(gap == 0, 1.0, jnp.where(gap == 1, 0.5, 0.0)).astype(BF16)
        CZ0f, F0f = flat(b["CZ0"]), flat(b["F0"])

        def pz0(i, _):
            res = exact_dot(L[pl.ds(row(i * 680), 680), :], P0)
            for p in range(17):
                for t in range(3):
                    CZ0f[pl.ds(row((i * 17 + p) * 144 + t * 48), 40)] = res[p * 40 : p * 40 + 40, t * 128 : t * 128 + 128]
            return 0

        lax.fori_loop(0, 2, pz0, 0)

        def widen0(k, _):
            for t in range(3):
                for ct in range(5):
                    q = k * 144 + (t * 48 + ct * 8)
                    v, n = CZ0f[pl.ds(q, 8)], CZ0f[pl.ds(q + 1, 8)]
                    o = k * 240 + (t * 80 + 16 * ct)
                    F0f[pl.ds(o, 8, stride=2)] = v
                    F0f[pl.ds(o + 1, 8, stride=2)] = 0.5 * (v + n)
            return 0

        lax.fori_loop(0, 34, widen0, 0)

        def add0(plane, t, r, v):
            q = pl.ds(row(plane * PS0 + t * RP0 + r), 8)
            Af[q] = Af[q] + v

        def get0(k, t, r):
            return F0f[pl.ds(row(k * 240 + t * 80 + r), 8)]

        for t in range(2):
            for r in range(8, 72, 8):
                add0(0, t, r, 0.5 * (get0(0, t, r) + get0(1, t, r)))
                add0(65, t, r, get0(33, t, r))

        def correct0(k, _):
            for i in (2 * k, 2 * k + 1):
                for t in range(2):
                    for r in range(0, 80, 8):
                        v, n = get0(i + 1, t, r), get0(i + 2, t, r)
                        add0(2 * i + 1, t, r, v)
                        add0(2 * i + 2, t, r, 0.5 * (v + n))
            for yt in range(8):
                place = 16 * yt if yt < 4 else 16 * (7 - yt) + 8
                h = b["HR"][2, 0, place : place + 8]
                for i in (2 * k, 2 * k + 1):
                    v, n = get0(i + 1, 2, 8 + yt * 8), get0(i + 2, 2, 8 + yt * 8)
                    for x, w in ((2 * i, v), (2 * i + 1, 0.5 * (v + n))):
                        h = h + jnp.where(half == x, pltpu.roll(w, jnp.bitwise_and(2 * x, 127), 1), 0.0)
                b["HR"][2, 0, place : place + 8] = h
            return 0

        lax.fori_loop(0, 16, correct0, 0)

        stencil(Af, Bf, 2, relax0, 3, taken=True)
        tile = total_wait(2, sum_msgs)
        mean = jnp.sum(tile, keepdims=True) / cells
        mean = jnp.broadcast_to(mean, (8, 128))
        stencil(Bf, None, 3, lambda c, beside, g: relax0(c, beside, g) - mean)

    return kernel, scratch


def solution(mesh):
    nx, ny, nz = (mesh.shape[a] for a in ("gx", "gy", "gz"))
    kernel, scratch = make_kernel(nx, ny, nz)

    def shards(right_side, initial_guess):
        assert right_side.shape == (64, 64, 256)
        return pl.pallas_call(
            kernel,
            out_shape=pltpu.VMEM(right_side.shape, F32),
            in_specs=[pl.BlockSpec(memory_space=pl.ANY)] * 2,
            out_specs=pl.BlockSpec(memory_space=pltpu.VMEM),
            scratch_shapes=scratch,
            compiler_params=pltpu.CompilerParams(collective_id=0, has_side_effects=True, vmem_limit_bytes=54 << 20),
        )(right_side, initial_guess)

    placed = P("gx", "gy", "gz")
    return jax.shard_map(shards, mesh=mesh, in_specs=(placed, placed), out_specs=placed, check_vma=False)
```

```python
import itertools

import jax
import jax.numpy as jnp
from jax import lax
from jax.experimental import pallas as pl
from jax.experimental.pallas import tpu as pltpu
from jax.sharding import PartitionSpec as P

F32 = jnp.float32
MESH = pl.DeviceIdType.MESH
COARSE_SWEEPS = 6
W = 0.8
C6 = W / 6.0
BF16 = jnp.bfloat16

N0, RP0 = 64, 96
PS0 = 2 * RP0
N1, H1, RP1, RO1 = 32, 4, 56, 12
PS1 = 2 * RP1
N2, H2, RP2, RO2 = 16, 8, 48, 16

XS1 = {1: (28, 5), 0: (0, 33), -1: (0, 4)}
GS1 = {1: (1, 2), 0: (0, 3), -1: (0, 1)}
XS2 = {1: (8, 8), 0: (0, 16), -1: (0, 8)}
GS2 = {1: (1, 1), 0: (0, 2), -1: (0, 1)}
PAD8 = {5: 8, 33: 40, 4: 8}
XY = [d for d in itertools.product((-1, 0, 1), repeat=2)]
XY8 = [d for d in XY if d != (0, 0)]
NEAR = [d for d in itertools.product((-1, 0, 1), repeat=3) if d != (0, 0, 0)]


def shift_weight():
    total = 0.0
    for level in range(2):
        total += 4 * W / (6.0 * 0.25**level)
    return total + COARSE_SWEEPS * W / (6.0 * 0.0625)


def make_kernel(nx, ny, nz):
    cells = float(nx * N0 * ny * N0 * nz * 256)
    peers = [d for d in NEAR if sum(map(abs, d)) == 1]
    ring = {0: [(0, 0, k) for k in range(1, nz)], 1: [(0, k, 0) for k in range(1, ny)], 2: [(k, 0, 0) for k in range(1, nx)]}
    n_sem = [0]

    scratch, names = [], []

    def vm(name, *shape):
        names.append(name)
        scratch.append(pltpu.VMEM(shape, F32))

    vm("A", 66, 2, RP0, 128)
    vm("B", 66, 2, RP0, 128)
    vm("C", 67, 2, RP0, 128)
    vm("G", 64, 2, 64, 128)
    vm("PK", 4, 64, 128)
    vm("HR", 4, 2, 64, 128)
    vm("L", 1360, 256)
    vm("G1", 42, 2, RP1, 128)
    vm("WA", 42, 2, RP1, 128)
    vm("WB", 42, 2, RP1, 128)
    vm("U", 3, 40, 128)
    vm("D", 3, 40, 128)
    vm("G2", 32, RP2, 128)
    vm("VA", 33, RP2, 128)
    vm("VB", 33, RP2, 128)
    vm("PZ2", 2, 16, 128)
    vm("RZ2", 2, 4, 32, 128)
    vm("CZ1", 21, 2, 32, 128)
    vm("F1", 21, 2, RP1, 128)
    vm("CZ0", 34, 3, 48, 128)
    vm("F0", 34, 3, 80, 128)
    vm("TS", 3, 8, 128)
    vm("TR0", max(nz - 1, 1), 8, 128)
    vm("TR1", max(ny - 1, 1), 8, 128)
    vm("TR2", max(nx - 1, 1), 8, 128)
    for dx, dy in XY8:
        vm(("RT", dx, dy), XS1[dx][1], PAD8[XS1[dy][1]], 128)
        vm(("RU0", dx, dy), GS1[dx][1], PAD8[XS1[dy][1]], 128)
    for dx, dy in XY:
        vm(("RU1", dx, dy), GS1[dx][1], PAD8[XS1[dy][1]], 128)
        vm(("RD", dx, dy), GS1[dx][1], PAD8[XS1[dy][1]], 128)
    N_MSG = 4 * 28 + 34 + 26 + (nx - 1) + (ny - 1) + (nz - 1)
    scratch += [pltpu.SemaphoreType.DMA((N_MSG,)), pltpu.SemaphoreType.DMA((N_MSG,)), pltpu.SemaphoreType.DMA((8,))]

    def kernel(g_hbm, v_hbm, out_ref, *refs):
        b = dict(zip(names, refs))
        send, recv, local = refs[len(names):]
        A, B, C, G = b["A"], b["B"], b["C"], b["G"]
        me = (lax.axis_index("gx"), lax.axis_index("gy"), lax.axis_index("gz"))
        sizes = (nx, ny, nz)
        lane = lax.broadcasted_iota(jnp.int32, (8, 128), 1)
        l0, l127 = lane == 0, lane == 127
        zero = jnp.zeros((8, 128), F32)
        used = [28 * 4]
        refs_of = {}

        def at(d):
            return tuple(lax.rem(m + (k + n), n) if k else m for m, k, n in zip(me, d, sizes))

        def post(src, dst, d):
            k = used[0]
            used[0] += 1
            c = pltpu.make_async_remote_copy(
                src_ref=src, dst_ref=dst, send_sem=send.at[k], recv_sem=recv.at[k], device_id=at(d), device_id_type=MESH
            )
            c.start()
            return c

        def flat(ref):
            s = ref.shape
            n = 1
            for k in s[:-1]:
                n *= k
            return ref.reshape(n, s[-1])

        def row(k, m=8):
            return pl.multiple_of(k, m)

        Af, Bf, Cf, Gf = flat(A), flat(B), flat(C), flat(G)
        refs_of.update({id(Af): A, id(Bf): B})
        G1f, WAf, WBf = flat(b["G1"]), flat(b["WA"]), flat(b["WB"])

        def clear(ref):
            f = flat(ref)
            n = f.shape[0] // 8
            per = 1
            for k in range(16, 0, -1):
                if n % k == 0:
                    per = k
                    break

            def step(i, _):
                for k in range(per):
                    f[pl.ds(row((i * per + k) * 8), 8)] = zero
                return 0

            lax.fori_loop(0, n // per, step, 0)

        barrier = pltpu.get_barrier_semaphore()
        for d in peers:
            pl.semaphore_signal(barrier, inc=1, device_id=at(d), device_id_type=MESH)
        loads = []
        for t in range(2):
            loads.append(pltpu.make_async_copy(v_hbm.at[:, :, t * 128 : t * 128 + 128], A.at[1:65, t, 8:72, :], local.at[t]))
            loads.append(pltpu.make_async_copy(g_hbm.at[:, :, t * 128 : t * 128 + 128], G.at[:, t, :, :], local.at[2 + t]))
        for k in (0, 2, 1, 3):
            loads[k].start()
        for name in names:
            if isinstance(name, tuple):
                clear(b[name])
        clear(b["G1"])
        for dst in (C.at[0], C.at[65], C.at[66]):
            clear(dst)

        def clear_rows(i, _):
            for t in range(2):
                for r in (0, 72, 80, 88):
                    Cf[pl.ds(row(i * PS0 + t * RP0 + r), 8)] = zero
            return 0

        lax.fori_loop(1, 65, clear_rows, 0)
        loads[0].wait()
        loads[2].wait()

        half = jnp.bitwise_and(lane + 1, 127) // 2

        def pair(c):
            return (c, 7 - c)

        def message(j, src, dst, d):
            return pltpu.make_async_remote_copy(
                src_ref=src, dst_ref=dst, send_sem=send.at[j], recv_sem=recv.at[j], device_id=at(d), device_id_type=MESH
            )

        def row_msgs(V, k, h):
            ps = slice(1 + 32 * h, 33 + 32 * h)
            return [
                message(28 * k + 24 + 2 * h, V.at[ps, :, 71:72, :], V.at[ps, :, 7:8, :], (0, 1, 0)),
                message(28 * k + 25 + 2 * h, V.at[ps, :, 8:9, :], V.at[ps, :, 72:73, :], (0, -1, 0)),
            ]

        def chunk_msgs(V, k, c):
            first_sem = 28 * k
            out = []

            def msg(j, src, dst, d):
                out.append(message(j, src, dst, d))

            for m, yt in enumerate(pair(c)):
                r = pl.ds(row(8 + yt * 8), 8)
                msg(first_sem + c * 6 + m, V.at[64, :, r, :], V.at[0, :, r, :], (1, 0, 0))
                msg(first_sem + c * 6 + 2 + m, V.at[1, :, r, :], V.at[65, :, r, :], (-1, 0, 0))
            r = pl.ds(row(c * 16, 16), 16)
            pk = b["PK"].at[k, r, :]
            msg(first_sem + c * 6 + 4, pk, b["HR"].at[k, 0, r, :], (0, 0, 1))
            msg(first_sem + c * 6 + 5, pk, b["HR"].at[k, 1, r, :], (0, 0, -1))
            return out

        odd = jnp.bitwise_and(lane, 1) == 1

        def take_chunk(V, k, c):
            for m in chunk_msgs(V, k, c):
                m.wait()
            for m in range(2):
                r = pl.ds(row(c * 16 + 8 * m), 8)
                b["HR"][k, 0, r] = jnp.where(odd, pltpu.roll(b["HR"][k, 1, r], 127, 1), pltpu.roll(b["HR"][k, 0, r], 1, 1))

        def put_faces(Df, k, blocks, c):
            for m, yt in enumerate(pair(c)):
                r = pl.ds(row(c * 16 + 8 * m), 8)
                keep = b["PK"][k, r]
                for i in blocks:
                    for p in range(16):
                        x = i * 16 + p
                        q = row((i * 16 + 1) * PS0 + 8 + yt * 8) + p * PS0
                        both = jnp.where(l0, Df[pl.ds(row(q), 8)], Df[pl.ds(row(q + RP0), 8)])
                        both = pltpu.roll(both, jnp.bitwise_and(2 * x, 127), 1)
                        keep = jnp.where(half == x, both, keep)
                b["PK"][k, r] = keep

        def stencil(Vf, Df, k, op, faces_to=None, carry=0, taken=False):
            summed = isinstance(carry, tuple)
            V, Dst = refs_of[id(Vf)], refs_of.get(id(Df))

            def chunk(c, carry):
                if not taken:
                    take_chunk(V, k, c)

                def step(i, carry):
                    base = row((i * 16 + 1) * PS0)
                    if faces_to is not None:
                        put_faces(Df, faces_to, (jnp.maximum(i - 1, 0),), c)
                    for m, yt in enumerate(pair(c)):
                        o = 8 + yt * 8
                        h = b["HR"][k, 0, pl.ds(row(c * 16 + 8 * m), 8)]

                        def get(p, t):
                            return Vf[pl.ds(row(base + o + (p * PS0 + t * RP0)), 8)]

                        below, mid = [get(-1, t) for t in range(2)], [get(0, t) for t in range(2)]
                        for p in range(16):
                            x = i * 16 + p
                            above = [get(p + 1, t) for t in range(2)]
                            e = pltpu.roll(h, jnp.bitwise_and(128 - 2 * x, 127), 1)
                            c0, c1 = mid
                            up0, up1, dn0, dn1 = (pltpu.roll(v, n, 1) for n in (1, 127) for v in (c0, c1))
                            zs = (
                                jnp.where(l0, e, up0) + jnp.where(l127, dn1, dn0),
                                jnp.where(l0, up0, up1) + jnp.where(l127, e, dn1),
                            )
                            for t in range(2):
                                q = base + o + (p * PS0 + t * RP0)
                                ys = Vf[pl.ds(q - 1, 8)] + Vf[pl.ds(q + 1, 8)]
                                beside = (below[t] + above[t]) + ys + zs[t]
                                g = Gf[pl.ds(row(x * 128 + t * 64 + yt * 8), 8)]
                                v = op(mid[t], beside, g)
                                if Df is None:
                                    out_ref[x, pl.ds(row(yt * 8), 8), t * 128 : t * 128 + 128] = v
                                else:
                                    Df[pl.ds(row(q), 8)] = v
                                if summed:
                                    carry = (carry[0] + mid[t], carry[1] + g)
                            below, mid = mid, above
                    return carry

                if isinstance(c, int):
                    for h in range(2):
                        if not taken:
                            for m in row_msgs(V, k, h):
                                m.wait()
                        carry = lax.fori_loop(2 * h, 2 * h + 2, step, carry)
                        if faces_to is not None:
                            for m in row_msgs(Dst, faces_to, h):
                                m.start()
                else:
                    carry = lax.fori_loop(0, 4, step, carry)
                if faces_to is not None:
                    put_faces(Df, faces_to, (3,), c)
                    for m in chunk_msgs(Dst, faces_to, c):
                        m.start()
                return carry

            return lax.fori_loop(1, 4, chunk, chunk(0, carry))

        def relax0(c, beside, g):
            return (1.0 - W) * c + C6 * (beside + g)

        def defect0(c, beside, g):
            return g - 6.0 * c + beside

        def total_stage(stage, tile):
            b["TS"][stage] = tile
            rec = b[f"TR{stage}"]
            return [post(b["TS"].at[stage], rec.at[j], d) for j, d in enumerate(ring[stage])]

        def total_wait(stage, msgs):
            tile = b["TS"][stage]
            for j, m in enumerate(msgs):
                m.wait()
                tile = tile + b[f"TR{stage}"][j]
            return tile

        def pack_first(n, _):
            i = jnp.bitwise_and(n, 1) * 2
            put_faces(Af, 0, (i, i + 1), n // 2)
            return 0

        lax.fori_loop(0, 8, pack_first, 0)
        pl.semaphore_wait(barrier, len(peers))
        for c in range(4):
            for m in chunk_msgs(A, 0, c):
                m.start()
            if c == 0:
                for m in row_msgs(A, 0, 0) + row_msgs(A, 0, 1):
                    m.start()
        loads[1].wait()
        loads[3].wait()
        sums = stencil(Af, Bf, 0, relax0, 1, (zero, zero))
        sum_msgs = total_stage(0, sums[0] + shift_weight() * sums[1])
        stencil(Bf, Af, 1, relax0, 2)
        sum_msgs = total_stage(1, total_wait(0, sum_msgs))

        stencil(Af, Cf, 2, defect0)

        L = b["L"]

        def restrict_xy(Df, plane, slab, start):
            rows = []
            for dp in range(3):
                q = plane + dp * slab + start
                lo, on, up = (Df[pl.ds(q + k, 8, stride=2)] for k in range(3))
                rows.append(0.25 * (lo + up) + 0.5 * on)
            return 0.25 * (rows[0] + rows[2]) + 0.5 * rows[1]

        def restrict0(i, _):
            for t in range(2):
                for ct in range(5):
                    L[pl.ds(row(i * 40 + ct * 8), 8), t * 128 : t * 128 + 128] = restrict_xy(
                        Cf, i * 2 * PS0, PS0, t * RP0 + 7 + 16 * ct
                    )
            return 0

        lax.fori_loop(0, 33, restrict0, 0)

        def exact_dot(x, weights):
            hi = x.astype(BF16)
            rest = x - hi.astype(F32)
            mid = rest.astype(BF16)
            lo = (rest - mid.astype(F32)).astype(BF16)
            return sum(jnp.dot(part, weights, preferred_element_type=F32) for part in (lo, mid, hi))

        def grid(rows, cols):
            return (
                lax.broadcasted_iota(jnp.int32, (rows, cols), 0),
                lax.broadcasted_iota(jnp.int32, (rows, cols), 1),
            )

        f, c = grid(256, 256)
        gap = jnp.abs(f - 2 * c)
        R0 = jnp.where(gap == 0, 0.5, jnp.where(gap == 1, 0.25, 0.0)).astype(BF16)

        def rz0(i, _):
            res = exact_dot(L[pl.ds(row(i * 440), 440), :], R0)
            for p in range(11):
                for t in range(2):
                    for ct in range(5):
                        G1f[pl.ds((i * 11 + (p + H1)) * PS1 + (t * RP1 + RO1 + ct * 8), 8)] = res[
                            p * 40 + ct * 8 : p * 40 + ct * 8 + 8, t * 128 : t * 128 + 128
                        ]
            return 0

        lax.fori_loop(0, 3, rz0, 0)

        slot8 = lane // 8
        for grp in range(3):
            for ct in range(5):
                up = dn = zero
                for j in range(16 if grp < 2 else 1):
                    q = (grp * 16 + j + H1) * PS1 + RO1 + ct * 8
                    t0, e = G1f[q : q + 8], G1f[q + RP1 : q + RP1 + 8]
                    up = jnp.where(slot8 == j, pltpu.roll(jnp.where(l0, e, t0), (4 + 8 * j) % 128, 1), up)
                    dn = jnp.where(slot8 == j, pltpu.roll(t0, 8 * j, 1) if j else t0, dn)
                b["U"][grp, ct * 8 : ct * 8 + 8] = up
                b["D"][grp, ct * 8 : ct * 8 + 8] = dn
        G1 = b["G1"]
        msgs1 = []

        def along(spec, k, off=0):
            return slice(spec[k][0] + off, spec[k][0] + off + spec[k][1])

        def packed1(dx, dy):
            n = XS1[dy][1]
            ys, gs = along(XS1, dy), along(GS1, dx)
            msgs1.append(post(b["U"].at[gs, ys, :], b["RU1", dx, dy].at[:, 0:n, :], (dx, dy, 1)))
            msgs1.append(post(b["D"].at[gs, ys, :], b["RD", dx, dy].at[:, 0:n, :], (dx, dy, -1)))

        corners = [d for d in XY if d[0] and d[1]]
        for dx, dy in corners:
            packed1(dx, dy)
        for dx, dy in [d for d in XY8 if d not in corners] + corners:
            n = XS1[dy][1]
            msgs1.append(
                post(G1.at[along(XS1, dx, H1), 0, along(XS1, dy, RO1), :], b["RT", dx, dy].at[:, 0:n, :], (dx, dy, 0))
            )
        for dx, dy in [d for d in XY if d not in corners]:
            packed1(dx, dy)
        for dx, dy in XY8:
            n = XS1[dy][1]
            msgs1.append(post(b["U"].at[along(GS1, dx), along(XS1, dy), :], b["RU0", dx, dy].at[:, 0:n, :], (dx, dy, 0)))
        sum_msgs = total_stage(2, total_wait(1, sum_msgs))
        for m in msgs1:
            m.wait()

        def add1(q, v):
            G1f[pl.ds(q, 8)] = G1f[pl.ds(q, 8)] + v

        for dx, dy in XY:
            sx, n = XS1[dx]
            sy = XS1[dy][0]
            tiles = PAD8[XS1[dy][1]] // 8
            g0 = GS1[dx][0]
            per = 11 if n == 33 else n

            def unpack(i, _, dx=dx, dy=dy, sx=sx, sy=sy, tiles=tiles, g0=g0, per=per):
                for p in range(per):
                    k = i * per + p
                    s = k + sx
                    grp, j = s // 16 - g0, s % 16 if isinstance(s, int) else jnp.bitwise_and(s, 15)
                    up = (124 - 8 * j) % 128 if isinstance(s, int) else jnp.bitwise_and(124 - 8 * j, 127)
                    down = (128 - 8 * j) % 128 if isinstance(s, int) else jnp.bitwise_and(128 - 8 * j, 127)
                    for ct in range(tiles):
                        q = i * per * PS1 + ((p + (sx - N1 * dx + H1)) * PS1 + (sy - N1 * dy + RO1 + ct * 8))
                        u1 = pltpu.roll(b["RU1", dx, dy][grp, ct * 8 : ct * 8 + 8], up, 1)
                        dn = pltpu.roll(b["RD", dx, dy][grp, ct * 8 : ct * 8 + 8], down, 1)
                        e = jnp.where(lane >= 124, u1, jnp.where(lane < 4, dn, 0.0))
                        t0 = jnp.where(l0, u1, 0.0)
                        if (dx, dy) != (0, 0):
                            u0 = pltpu.roll(b["RU0", dx, dy][grp, ct * 8 : ct * 8 + 8], up, 1)
                            e = e + jnp.where(l0, u0, 0.0)
                            t0 = t0 + b["RT", dx, dy][k, ct * 8 : ct * 8 + 8]
                        add1(q, t0)
                        add1(q + RP1, e)
                return 0

            if n == 33:
                lax.fori_loop(0, 3, unpack, 0)
            else:
                unpack(0, 0)

        def ring1(Vf, op, emit, lo, hi, per):

            def step(i, _):
                for p in range(per):
                    base = i * per * PS1
                    for ct in range(5):
                        q = row(base + ((p + lo + H1) * PS1 + 8 + ct * 8))
                        c = (Vf[pl.ds(q, 8)], Vf[pl.ds(q + RP1, 8)])
                        up = [pltpu.roll(v, 1, 1) for v in c]
                        dn = [pltpu.roll(v, 127, 1) for v in c]
                        for t in range(2):
                            zs = jnp.where(l0, up[1 - t], up[t]) + jnp.where(l127, dn[1 - t], dn[t])
                            s = q + t * RP1
                            beside = (
                                (Vf[pl.ds(s - PS1, 8)] + Vf[pl.ds(s + PS1, 8)])
                                + (Vf[pl.ds(s - 1, 8)] + Vf[pl.ds(s + 1, 8)])
                                + zs
                            )
                            emit(i * per * 40 + (p + lo + 1) * 40, t, ct, s, op(c[t], beside, G1f[pl.ds(s, 8)]))
                return 0

            lax.fori_loop(0, (hi - lo) // per, step, 0)

        first = W / (6.0 * 0.25)

        def put1(Df):
            def emit(x, t, ct, s, v):
                Df[pl.ds(s, 8)] = v

            return emit

        ring1(G1f, lambda a, beside, g: ((2.0 - W) * first) * a + (C6 * first) * beside, put1(WAf), -3, 37, 10)
        ring1(WAf, lambda a, beside, g: g - 0.25 * (6.0 * a - beside), put1(WBf), -1, 32, 11)

        def restrict1(i, _):
            for t in range(2):
                for ct in range(2):
                    L[pl.ds(row(i * 16 + ct * 8), 8), t * 128 : t * 128 + 128] = restrict_xy(
                        WBf, (2 * i + (H1 - 1)) * PS1, PS1, t * RP1 + RO1 - 1 + 16 * ct
                    )
            return 0

        lax.fori_loop(0, 16, restrict1, 0)
        f, c = grid(256, 128)
        gap = jnp.abs(jnp.where(f < 192, f, f - 256) - 2 * c)
        R1 = jnp.where(c < 64, jnp.where(gap == 0, 0.5, jnp.where(gap == 1, 0.25, 0.0)), 0.0).astype(BF16)
        G2, VA, VB = b["G2"], b["VA"], b["VB"]
        G2f, VAf, VBf = flat(G2), flat(VA), flat(VB)
        res = exact_dot(L[0:256, :], R1)
        slot16 = lane // 16
        for x in range(16):
            for ct in range(2):
                G2[x + H2, RO2 + ct * 8 : RO2 + ct * 8 + 8] = res[x * 16 + ct * 8 : x * 16 + ct * 8 + 8]
        for grp in range(2):
            for ct in range(2):
                acc = zero
                for j in range(8):
                    v = res[(grp * 8 + j) * 16 + ct * 8 : (grp * 8 + j) * 16 + ct * 8 + 8]
                    v = jnp.where(lane < 8, v, pltpu.roll(v, 128 - 48, 1))
                    acc = jnp.where(slot16 == j, pltpu.roll(v, 16 * j, 1) if j else v, acc)
                b["PZ2"][grp, ct * 8 : ct * 8 + 8] = acc
        msgs2 = []
        def packed2(dx, dy):
            gs = along(GS2, dx)
            gd = along(GS2, dx, 1 - 2 * dx)
            yd = along(XS2, dy, 8 - N2 * dy)
            for side, dz in ((0, 1), (1, -1)):
                msgs2.append(post(b["PZ2"].at[gs, along(XS2, dy), :], b["RZ2"].at[side, gd, yd, :], (dx, dy, dz)))

        corners = [d for d in XY if d[0] and d[1]]
        for dx, dy in corners:
            packed2(dx, dy)
        for dx, dy in [d for d in XY8 if d not in corners] + corners:
            msgs2.append(
                post(
                    G2.at[along(XS2, dx, H2), along(XS2, dy, RO2), :],
                    G2.at[along(XS2, dx, H2 - N2 * dx), along(XS2, dy, RO2 - N2 * dy), :],
                    (dx, dy, 0),
                )
            )
        for dx, dy in [d for d in XY if d not in corners]:
            packed2(dx, dy)
        for m in msgs2:
            m.wait()

        first2 = W / (6.0 * 0.0625)

        def spread(grp, _):
            for ct in range(4):
                m = jnp.where(
                    jnp.bitwise_and(lane, 15) < 8,
                    b["RZ2"][1, grp, ct * 8 : ct * 8 + 8],
                    b["RZ2"][0, grp, ct * 8 : ct * 8 + 8],
                )
                for j in range(8):
                    hi = pltpu.roll(m, (64 - 16 * j) % 128, 1)
                    lo = pltpu.roll(m, 112 - 16 * j, 1) if j < 7 else m
                    r = pl.ds(row((grp * 8 + j) * RP2 + 8 + ct * 8), 8)
                    own = G2f[r]
                    v = jnp.where(lane < 64, own, jnp.where(lane < 72, hi, jnp.where(lane >= 120, lo, 0.0)))
                    G2f[r] = v
                    VAf[r] = first2 * v
            return 0

        lax.fori_loop(0, 4, spread, 0)

        def coarse(Sf, Tf, lo, n, per):
            def step(i, _):
                for p in range(per):
                    for ct in range(4):
                        q = row(i * per * RP2 + ((lo + p) * RP2 + 8 + ct * 8))
                        a = Sf[pl.ds(q, 8)]
                        beside = (
                            (Sf[pl.ds(q - RP2, 8)] + Sf[pl.ds(q + RP2, 8)])
                            + (Sf[pl.ds(q - 1, 8)] + Sf[pl.ds(q + 1, 8)])
                            + (pltpu.roll(a, 1, 1) + pltpu.roll(a, 127, 1))
                        )
                        Tf[pl.ds(q, 8)] = (1.0 - W) * a + (C6 * beside + first2 * G2f[pl.ds(q, 8)])
                return 0

            lax.fori_loop(0, n // per, step, 0)

        src, dst = VAf, VBf
        for lo, n, per in ((2, 28, 7), (2, 28, 7), (4, 24, 8), (4, 24, 8), (6, 20, 10)):
            coarse(src, dst, lo, n, per)
            src, dst = dst, src

        f, c = grid(128, 256)
        gap = jnp.abs(jnp.where(c < 192, c, c - 256) - 2 * jnp.where(f < 96, f, f - 128))
        P1 = jnp.where(gap == 0, 1.0, jnp.where(gap == 1, 0.5, 0.0)).astype(BF16)
        CZ1f, F1f = flat(b["CZ1"]), flat(b["F1"])
        for k in range(20):
            L[k * 24 : k * 24 + 24, 0:128] = src[pl.ds((k + 6) * RP2 + 12, 24)]
        res = exact_dot(L[0:480, 0:128], P1)
        for k in range(20):
            for t in range(2):
                b["CZ1"][k, t, 0:24] = res[k * 24 : k * 24 + 24, t * 128 : t * 128 + 128]

        def widen1(k, _):
            for t in range(2):
                for ct in range(3):
                    q = k * 64 + (t * 32 + ct * 8)
                    v, n = CZ1f[pl.ds(q, 8)], CZ1f[pl.ds(q + 1, 8)]
                    o = k * PS1 + (t * RP1 + 4 + 16 * ct)
                    F1f[pl.ds(o, 8, stride=2)] = v
                    F1f[pl.ds(o + 1, 8, stride=2)] = 0.5 * (v + n)
            return 0

        lax.fori_loop(0, 20, widen1, 0)

        def correct1(k, _):
            for t in range(2):
                for ct in range(5):
                    o = t * RP1 + 8 + ct * 8
                    v = F1f[pl.ds(row(k * PS1 + o), 8)]
                    n = F1f[pl.ds(row((k + 1) * PS1 + o), 8)]
                    q = row(2 * k * PS1 + o)
                    WAf[pl.ds(q, 8)] = WAf[pl.ds(q, 8)] + v
                    q = row((2 * k + 1) * PS1 + o)
                    WAf[pl.ds(q, 8)] = WAf[pl.ds(q, 8)] + 0.5 * (v + n)
            return 0

        lax.fori_loop(0, 20, correct1, 0)

        def relax1(a, beside, g):
            return (1.0 - W) * a + (C6 * beside + first * g)

        def put_l(r, t, ct, s, v):
            L[pl.ds(row(r + ct * 8), 8), t * 128 : t * 128 + 128] = v

        ring1(WAf, relax1, put1(WBf), -2, 34, 9)
        ring1(WBf, relax1, put_l, -1, 33, 17)

        f, c = grid(256, 384)
        gap = jnp.abs(jnp.where(c < 256, c, jnp.where(c == 383, 256, jnp.where(c == 256, -1, 9999))) - 2 * jnp.where(f < 192, f, f - 256))
        P0 = jnp.where(gap == 0, 1.0, jnp.where(gap == 1, 0.5, 0.0)).astype(BF16)
        CZ0f, F0f = flat(b["CZ0"]), flat(b["F0"])

        def pz0(i, _):
            res = exact_dot(L[pl.ds(row(i * 680), 680), :], P0)
            for p in range(17):
                for t in range(3):
                    CZ0f[pl.ds(row((i * 17 + p) * 144 + t * 48), 40)] = res[p * 40 : p * 40 + 40, t * 128 : t * 128 + 128]
            return 0

        lax.fori_loop(0, 2, pz0, 0)

        def widen0(k, _):
            for t in range(3):
                for ct in range(5):
                    q = k * 144 + (t * 48 + ct * 8)
                    v, n = CZ0f[pl.ds(q, 8)], CZ0f[pl.ds(q + 1, 8)]
                    o = k * 240 + (t * 80 + 16 * ct)
                    F0f[pl.ds(o, 8, stride=2)] = v
                    F0f[pl.ds(o + 1, 8, stride=2)] = 0.5 * (v + n)
            return 0

        lax.fori_loop(0, 34, widen0, 0)

        def add0(plane, t, r, v):
            q = pl.ds(row(plane * PS0 + t * RP0 + r), 8)
            Af[q] = Af[q] + v

        def get0(k, t, r):
            return F0f[pl.ds(row(k * 240 + t * 80 + r), 8)]

        for t in range(2):
            for r in range(8, 72, 8):
                add0(0, t, r, 0.5 * (get0(0, t, r) + get0(1, t, r)))
                add0(65, t, r, get0(33, t, r))

        def correct0(k, _):
            for i in (2 * k, 2 * k + 1):
                for t in range(2):
                    for r in range(0, 80, 8):
                        v, n = get0(i + 1, t, r), get0(i + 2, t, r)
                        add0(2 * i + 1, t, r, v)
                        add0(2 * i + 2, t, r, 0.5 * (v + n))
            for yt in range(8):
                place = 16 * yt if yt < 4 else 16 * (7 - yt) + 8
                h = b["HR"][2, 0, place : place + 8]
                for i in (2 * k, 2 * k + 1):
                    v, n = get0(i + 1, 2, 8 + yt * 8), get0(i + 2, 2, 8 + yt * 8)
                    for x, w in ((2 * i, v), (2 * i + 1, 0.5 * (v + n))):
                        h = h + jnp.where(half == x, pltpu.roll(w, jnp.bitwise_and(2 * x, 127), 1), 0.0)
                b["HR"][2, 0, place : place + 8] = h
            return 0

        lax.fori_loop(0, 16, correct0, 0)

        stencil(Af, Bf, 2, relax0, 3, taken=True)
        tile = total_wait(2, sum_msgs)
        mean = jnp.sum(tile, keepdims=True) / cells
        mean = jnp.broadcast_to(mean, (8, 128))
        stencil(Bf, None, 3, lambda c, beside, g: relax0(c, beside, g) - mean)

    return kernel, scratch


def solution(mesh):
    nx, ny, nz = (mesh.shape[a] for a in ("gx", "gy", "gz"))
    kernel, scratch = make_kernel(nx, ny, nz)

    def shards(right_side, initial_guess):
        assert right_side.shape == (64, 64, 256)
        return pl.pallas_call(
            kernel,
            out_shape=pltpu.VMEM(right_side.shape, F32),
            in_specs=[pl.BlockSpec(memory_space=pl.ANY)] * 2,
            out_specs=pl.BlockSpec(memory_space=pltpu.VMEM),
            scratch_shapes=scratch,
            compiler_params=pltpu.CompilerParams(collective_id=0, has_side_effects=True, vmem_limit_bytes=54 << 20),
        )(right_side, initial_guess)

    placed = P("gx", "gy", "gz")
    return jax.shard_map(shards, mesh=mesh, in_specs=(placed, placed), out_specs=placed, check_vma=False)
```

```python
import itertools

import jax
import jax.numpy as jnp
from jax import lax
from jax.experimental import pallas as pl
from jax.experimental.pallas import tpu as pltpu
from jax.sharding import PartitionSpec as P

F32 = jnp.float32
MESH = pl.DeviceIdType.MESH
COARSE_SWEEPS = 6
W = 0.8
C6 = W / 6.0
BF16 = jnp.bfloat16

N0, RP0 = 64, 96
PS0 = 2 * RP0
N1, H1, RP1, RO1 = 32, 4, 56, 12
PS1 = 2 * RP1
N2, H2, RP2, RO2 = 16, 8, 48, 16

XS1 = {1: (28, 5), 0: (0, 33), -1: (0, 4)}
GS1 = {1: (1, 2), 0: (0, 3), -1: (0, 1)}
XS2 = {1: (8, 8), 0: (0, 16), -1: (0, 8)}
GS2 = {1: (1, 1), 0: (0, 2), -1: (0, 1)}
PAD8 = {5: 8, 33: 40, 4: 8}
XY = [d for d in itertools.product((-1, 0, 1), repeat=2)]
XY8 = [d for d in XY if d != (0, 0)]
NEAR = [d for d in itertools.product((-1, 0, 1), repeat=3) if d != (0, 0, 0)]


def shift_weight():
    total = 0.0
    for level in range(2):
        total += 4 * W / (6.0 * 0.25**level)
    return total + COARSE_SWEEPS * W / (6.0 * 0.0625)


def make_kernel(nx, ny, nz):
    cells = float(nx * N0 * ny * N0 * nz * 256)
    peers = [d for d in NEAR if sum(map(abs, d)) == 1]
    ring = {0: [(0, 0, k) for k in range(1, nz)], 1: [(0, k, 0) for k in range(1, ny)], 2: [(k, 0, 0) for k in range(1, nx)]}
    n_sem = [0]

    scratch, names = [], []

    def vm(name, *shape):
        names.append(name)
        scratch.append(pltpu.VMEM(shape, F32))

    vm("A", 66, 2, RP0, 128)
    vm("B", 66, 2, RP0, 128)
    vm("C", 67, 2, RP0, 128)
    vm("G", 64, 2, 64, 128)
    vm("PK", 4, 64, 128)
    vm("HR", 4, 2, 64, 128)
    vm("L", 1360, 256)
    vm("G1", 42, 2, RP1, 128)
    vm("WA", 42, 2, RP1, 128)
    vm("WB", 42, 2, RP1, 128)
    vm("U", 3, 40, 128)
    vm("D", 3, 40, 128)
    vm("G2", 32, RP2, 128)
    vm("VA", 33, RP2, 128)
    vm("VB", 33, RP2, 128)
    vm("PZ2", 2, 16, 128)
    vm("RZ2", 2, 4, 32, 128)
    vm("CZ1", 21, 2, 32, 128)
    vm("F1", 21, 2, RP1, 128)
    vm("CZ0", 34, 3, 48, 128)
    vm("F0", 34, 3, 80, 128)
    vm("TS", 3, 8, 128)
    vm("TR0", max(nz - 1, 1), 8, 128)
    vm("TR1", max(ny - 1, 1), 8, 128)
    vm("TR2", max(nx - 1, 1), 8, 128)
    for dx, dy in XY8:
        vm(("RT", dx, dy), XS1[dx][1], PAD8[XS1[dy][1]], 128)
        vm(("RU0", dx, dy), GS1[dx][1], PAD8[XS1[dy][1]], 128)
    for dx, dy in XY:
        vm(("RU1", dx, dy), GS1[dx][1], PAD8[XS1[dy][1]], 128)
        vm(("RD", dx, dy), GS1[dx][1], PAD8[XS1[dy][1]], 128)
    N_MSG = 4 * 28 + 34 + 26 + (nx - 1) + (ny - 1) + (nz - 1)
    scratch += [pltpu.SemaphoreType.DMA((N_MSG,)), pltpu.SemaphoreType.DMA((N_MSG,)), pltpu.SemaphoreType.DMA((8,))]

    def kernel(g_hbm, v_hbm, out_ref, *refs):
        b = dict(zip(names, refs))
        send, recv, local = refs[len(names):]
        A, B, C, G = b["A"], b["B"], b["C"], b["G"]
        me = (lax.axis_index("gx"), lax.axis_index("gy"), lax.axis_index("gz"))
        sizes = (nx, ny, nz)
        lane = lax.broadcasted_iota(jnp.int32, (8, 128), 1)
        l0, l127 = lane == 0, lane == 127
        zero = jnp.zeros((8, 128), F32)
        used = [28 * 4]
        refs_of = {}

        def at(d):
            return tuple(lax.rem(m + (k + n), n) if k else m for m, k, n in zip(me, d, sizes))

        def post(src, dst, d):
            k = used[0]
            used[0] += 1
            c = pltpu.make_async_remote_copy(
                src_ref=src, dst_ref=dst, send_sem=send.at[k], recv_sem=recv.at[k], device_id=at(d), device_id_type=MESH
            )
            c.start()
            return c

        def flat(ref):
            s = ref.shape
            n = 1
            for k in s[:-1]:
                n *= k
            return ref.reshape(n, s[-1])

        def row(k, m=8):
            return pl.multiple_of(k, m)

        Af, Bf, Cf, Gf = flat(A), flat(B), flat(C), flat(G)
        refs_of.update({id(Af): A, id(Bf): B})
        G1f, WAf, WBf = flat(b["G1"]), flat(b["WA"]), flat(b["WB"])

        def clear(ref):
            f = flat(ref)
            n = f.shape[0] // 8
            per = 1
            for k in range(16, 0, -1):
                if n % k == 0:
                    per = k
                    break

            def step(i, _):
                for k in range(per):
                    f[pl.ds(row((i * per + k) * 8), 8)] = zero
                return 0

            lax.fori_loop(0, n // per, step, 0)

        barrier = pltpu.get_barrier_semaphore()
        for d in peers:
            pl.semaphore_signal(barrier, inc=1, device_id=at(d), device_id_type=MESH)
        loads = []
        for t in range(2):
            loads.append(pltpu.make_async_copy(v_hbm.at[:, :, t * 128 : t * 128 + 128], A.at[1:65, t, 8:72, :], local.at[t]))
            loads.append(pltpu.make_async_copy(g_hbm.at[:, :, t * 128 : t * 128 + 128], G.at[:, t, :, :], local.at[2 + t]))
        for k in (0, 2, 1, 3):
            loads[k].start()
        for name in names:
            if isinstance(name, tuple):
                clear(b[name])
        clear(b["G1"])
        for dst in (C.at[0], C.at[65], C.at[66]):
            clear(dst)

        def clear_rows(i, _):
            for t in range(2):
                for r in (0, 72, 80, 88):
                    Cf[pl.ds(row(i * PS0 + t * RP0 + r), 8)] = zero
            return 0

        lax.fori_loop(1, 65, clear_rows, 0)
        loads[0].wait()
        loads[2].wait()

        half = jnp.bitwise_and(lane + 1, 127) // 2

        def pair(c):
            return (c, 7 - c)

        def message(j, src, dst, d):
            return pltpu.make_async_remote_copy(
                src_ref=src, dst_ref=dst, send_sem=send.at[j], recv_sem=recv.at[j], device_id=at(d), device_id_type=MESH
            )

        def row_msgs(V, k, h):
            ps = slice(1 + 32 * h, 33 + 32 * h)
            return [
                message(28 * k + 24 + 2 * h, V.at[ps, :, 71:72, :], V.at[ps, :, 7:8, :], (0, 1, 0)),
                message(28 * k + 25 + 2 * h, V.at[ps, :, 8:9, :], V.at[ps, :, 72:73, :], (0, -1, 0)),
            ]

        def chunk_msgs(V, k, c):
            first_sem = 28 * k
            out = []

            def msg(j, src, dst, d):
                out.append(message(j, src, dst, d))

            for m, yt in enumerate(pair(c)):
                r = pl.ds(row(8 + yt * 8), 8)
                msg(first_sem + c * 6 + m, V.at[64, :, r, :], V.at[0, :, r, :], (1, 0, 0))
                msg(first_sem + c * 6 + 2 + m, V.at[1, :, r, :], V.at[65, :, r, :], (-1, 0, 0))
            r = pl.ds(row(c * 16, 16), 16)
            pk = b["PK"].at[k, r, :]
            msg(first_sem + c * 6 + 4, pk, b["HR"].at[k, 0, r, :], (0, 0, 1))
            msg(first_sem + c * 6 + 5, pk, b["HR"].at[k, 1, r, :], (0, 0, -1))
            return out

        odd = jnp.bitwise_and(lane, 1) == 1

        def take_chunk(V, k, c):
            for m in chunk_msgs(V, k, c):
                m.wait()
            for m in range(2):
                r = pl.ds(row(c * 16 + 8 * m), 8)
                b["HR"][k, 0, r] = jnp.where(odd, pltpu.roll(b["HR"][k, 1, r], 127, 1), pltpu.roll(b["HR"][k, 0, r], 1, 1))

        def put_faces(Df, k, blocks, c):
            for m, yt in enumerate(pair(c)):
                r = pl.ds(row(c * 16 + 8 * m), 8)
                keep = b["PK"][k, r]
                for i in blocks:
                    for p in range(16):
                        x = i * 16 + p
                        q = row((i * 16 + 1) * PS0 + 8 + yt * 8) + p * PS0
                        both = jnp.where(l0, Df[pl.ds(row(q), 8)], Df[pl.ds(row(q + RP0), 8)])
                        both = pltpu.roll(both, jnp.bitwise_and(2 * x, 127), 1)
                        keep = jnp.where(half == x, both, keep)
                b["PK"][k, r] = keep

        def stencil(Vf, Df, k, op, faces_to=None, carry=0, taken=False):
            summed = isinstance(carry, tuple)
            V, Dst = refs_of[id(Vf)], refs_of.get(id(Df))

            def chunk(c, carry):
                if not taken:
                    take_chunk(V, k, c)

                def step(i, carry):
                    base = row((i * 16 + 1) * PS0)
                    if faces_to is not None:
                        put_faces(Df, faces_to, (jnp.maximum(i - 1, 0),), c)
                    for m, yt in enumerate(pair(c)):
                        o = 8 + yt * 8
                        h = b["HR"][k, 0, pl.ds(row(c * 16 + 8 * m), 8)]

                        def get(p, t):
                            return Vf[pl.ds(row(base + o + (p * PS0 + t * RP0)), 8)]

                        below, mid = [get(-1, t) for t in range(2)], [get(0, t) for t in range(2)]
                        for p in range(16):
                            x = i * 16 + p
                            above = [get(p + 1, t) for t in range(2)]
                            e = pltpu.roll(h, jnp.bitwise_and(128 - 2 * x, 127), 1)
                            c0, c1 = mid
                            up0, up1, dn0, dn1 = (pltpu.roll(v, n, 1) for n in (1, 127) for v in (c0, c1))
                            zs = (
                                jnp.where(l0, e, up0) + jnp.where(l127, dn1, dn0),
                                jnp.where(l0, up0, up1) + jnp.where(l127, e, dn1),
                            )
                            for t in range(2):
                                q = base + o + (p * PS0 + t * RP0)
                                ys = Vf[pl.ds(q - 1, 8)] + Vf[pl.ds(q + 1, 8)]
                                beside = (below[t] + above[t]) + ys + zs[t]
                                g = Gf[pl.ds(row(x * 128 + t * 64 + yt * 8), 8)]
                                v = op(mid[t], beside, g)
                                if Df is None:
                                    out_ref[x, pl.ds(row(yt * 8), 8), t * 128 : t * 128 + 128] = v
                                else:
                                    Df[pl.ds(row(q), 8)] = v
                                if summed:
                                    carry = (carry[0] + mid[t], carry[1] + g)
                            below, mid = mid, above
                    return carry

                if isinstance(c, int):
                    for h in range(2):
                        if not taken:
                            for m in row_msgs(V, k, h):
                                m.wait()
                        carry = lax.fori_loop(2 * h, 2 * h + 2, step, carry)
                        if faces_to is not None:
                            for m in row_msgs(Dst, faces_to, h):
                                m.start()
                else:
                    carry = lax.fori_loop(0, 4, step, carry)
                if faces_to is not None:
                    put_faces(Df, faces_to, (3,), c)
                    for m in chunk_msgs(Dst, faces_to, c):
                        m.start()
                return carry

            return lax.fori_loop(1, 4, chunk, chunk(0, carry))

        def relax0(c, beside, g):
            return (1.0 - W) * c + C6 * (beside + g)

        def defect0(c, beside, g):
            return g - 6.0 * c + beside

        def total_stage(stage, tile):
            b["TS"][stage] = tile
            rec = b[f"TR{stage}"]
            return [post(b["TS"].at[stage], rec.at[j], d) for j, d in enumerate(ring[stage])]

        def total_wait(stage, msgs):
            tile = b["TS"][stage]
            for j, m in enumerate(msgs):
                m.wait()
                tile = tile + b[f"TR{stage}"][j]
            return tile

        def pack_first(n, _):
            i = jnp.bitwise_and(n, 1) * 2
            put_faces(Af, 0, (i, i + 1), n // 2)
            return 0

        lax.fori_loop(0, 8, pack_first, 0)
        pl.semaphore_wait(barrier, len(peers))
        for c in range(4):
            for m in chunk_msgs(A, 0, c):
                m.start()
            if c == 0:
                for m in row_msgs(A, 0, 0) + row_msgs(A, 0, 1):
                    m.start()
        loads[1].wait()
        loads[3].wait()
        sums = stencil(Af, Bf, 0, relax0, 1, (zero, zero))
        sum_msgs = total_stage(0, sums[0] + shift_weight() * sums[1])
        stencil(Bf, Af, 1, relax0, 2)
        sum_msgs = total_stage(1, total_wait(0, sum_msgs))

        stencil(Af, Cf, 2, defect0)

        L = b["L"]

        def restrict_xy(Df, plane, slab, start):
            rows = []
            for dp in range(3):
                q = plane + dp * slab + start
                lo, on, up = (Df[pl.ds(q + k, 8, stride=2)] for k in range(3))
                rows.append(0.25 * (lo + up) + 0.5 * on)
            return 0.25 * (rows[0] + rows[2]) + 0.5 * rows[1]

        def restrict0(i, _):
            for t in range(2):
                for ct in range(5):
                    L[pl.ds(row(i * 40 + ct * 8), 8), t * 128 : t * 128 + 128] = restrict_xy(
                        Cf, i * 2 * PS0, PS0, t * RP0 + 7 + 16 * ct
                    )
            return 0

        lax.fori_loop(0, 33, restrict0, 0)

        def exact_dot(x, weights):
            hi = x.astype(BF16)
            rest = x - hi.astype(F32)
            mid = rest.astype(BF16)
            lo = (rest - mid.astype(F32)).astype(BF16)
            return sum(jnp.dot(part, weights, preferred_element_type=F32) for part in (lo, mid, hi))

        def grid(rows, cols):
            return (
                lax.broadcasted_iota(jnp.int32, (rows, cols), 0),
                lax.broadcasted_iota(jnp.int32, (rows, cols), 1),
            )

        f, c = grid(256, 256)
        gap = jnp.abs(f - 2 * c)
        R0 = jnp.where(gap == 0, 0.5, jnp.where(gap == 1, 0.25, 0.0)).astype(BF16)

        def rz0(i, _):
            res = exact_dot(L[pl.ds(row(i * 440), 440), :], R0)
            for p in range(11):
                for t in range(2):
                    for ct in range(5):
                        G1f[pl.ds((i * 11 + (p + H1)) * PS1 + (t * RP1 + RO1 + ct * 8), 8)] = res[
                            p * 40 + ct * 8 : p * 40 + ct * 8 + 8, t * 128 : t * 128 + 128
                        ]
            return 0

        lax.fori_loop(0, 3, rz0, 0)

        slot8 = lane // 8
        for grp in range(3):
            for ct in range(5):
                up = dn = zero
                for j in range(16 if grp < 2 else 1):
                    q = (grp * 16 + j + H1) * PS1 + RO1 + ct * 8
                    t0, e = G1f[q : q + 8], G1f[q + RP1 : q + RP1 + 8]
                    up = jnp.where(slot8 == j, pltpu.roll(jnp.where(l0, e, t0), (4 + 8 * j) % 128, 1), up)
                    dn = jnp.where(slot8 == j, pltpu.roll(t0, 8 * j, 1) if j else t0, dn)
                b["U"][grp, ct * 8 : ct * 8 + 8] = up
                b["D"][grp, ct * 8 : ct * 8 + 8] = dn
        G1 = b["G1"]
        msgs1 = []
        near1, side1 = [], []

        def along(spec, k, off=0):
            return slice(spec[k][0] + off, spec[k][0] + off + spec[k][1])

        def packed1(dx, dy):
            n = XS1[dy][1]
            ys, gs = along(XS1, dy), along(GS1, dx)
            to = side1 if dx else near1
            to.append(post(b["U"].at[gs, ys, :], b["RU1", dx, dy].at[:, 0:n, :], (dx, dy, 1)))
            to.append(post(b["D"].at[gs, ys, :], b["RD", dx, dy].at[:, 0:n, :], (dx, dy, -1)))

        corners = [d for d in XY if d[0] and d[1]]
        for dx, dy in corners:
            packed1(dx, dy)
        for dx, dy in [d for d in XY8 if d not in corners] + corners:
            n = XS1[dy][1]
            msgs1.append((dx,
                post(G1.at[along(XS1, dx, H1), 0, along(XS1, dy, RO1), :], b["RT", dx, dy].at[:, 0:n, :], (dx, dy, 0))
            ))
        for dx, dy in [d for d in XY if d not in corners]:
            packed1(dx, dy)
        for dx, dy in XY8:
            n = XS1[dy][1]
            (side1 if dx else near1).append(
                post(b["U"].at[along(GS1, dx), along(XS1, dy), :], b["RU0", dx, dy].at[:, 0:n, :], (dx, dy, 0))
            )
        sum_msgs = total_stage(2, total_wait(1, sum_msgs))
        for dx, m in msgs1:
            m.wait_send()

        def add1(q, v):
            G1f[pl.ds(q, 8)] = G1f[pl.ds(q, 8)] + v

        def add_from(dx, dy):
            sx, n = XS1[dx]
            sy = XS1[dy][0]
            tiles = PAD8[XS1[dy][1]] // 8
            g0 = GS1[dx][0]
            per = 11 if n == 33 else n

            def unpack(i, _, dx=dx, dy=dy, sx=sx, sy=sy, tiles=tiles, g0=g0, per=per):
                for p in range(per):
                    k = i * per + p
                    s = k + sx
                    grp, j = s // 16 - g0, s % 16 if isinstance(s, int) else jnp.bitwise_and(s, 15)
                    up = (124 - 8 * j) % 128 if isinstance(s, int) else jnp.bitwise_and(124 - 8 * j, 127)
                    down = (128 - 8 * j) % 128 if isinstance(s, int) else jnp.bitwise_and(128 - 8 * j, 127)
                    for ct in range(tiles):
                        q = i * per * PS1 + ((p + (sx - N1 * dx + H1)) * PS1 + (sy - N1 * dy + RO1 + ct * 8))
                        u1 = pltpu.roll(b["RU1", dx, dy][grp, ct * 8 : ct * 8 + 8], up, 1)
                        dn = pltpu.roll(b["RD", dx, dy][grp, ct * 8 : ct * 8 + 8], down, 1)
                        e = jnp.where(lane >= 124, u1, jnp.where(lane < 4, dn, 0.0))
                        t0 = jnp.where(l0, u1, 0.0)
                        if (dx, dy) != (0, 0):
                            u0 = pltpu.roll(b["RU0", dx, dy][grp, ct * 8 : ct * 8 + 8], up, 1)
                            e = e + jnp.where(l0, u0, 0.0)
                            t0 = t0 + b["RT", dx, dy][k, ct * 8 : ct * 8 + 8]
                        add1(q, t0)
                        add1(q + RP1, e)
                return 0

            if n == 33:
                lax.fori_loop(0, 3, unpack, 0)
            else:
                unpack(0, 0)

        def ring1(Vf, op, emit, lo, hi, per):

            def step(i, _):
                for p in range(per):
                    base = i * per * PS1
                    for ct in range(5):
                        q = row(base + ((p + lo + H1) * PS1 + 8 + ct * 8))
                        c = (Vf[pl.ds(q, 8)], Vf[pl.ds(q + RP1, 8)])
                        up = [pltpu.roll(v, 1, 1) for v in c]
                        dn = [pltpu.roll(v, 127, 1) for v in c]
                        for t in range(2):
                            zs = jnp.where(l0, up[1 - t], up[t]) + jnp.where(l127, dn[1 - t], dn[t])
                            s = q + t * RP1
                            beside = (
                                (Vf[pl.ds(s - PS1, 8)] + Vf[pl.ds(s + PS1, 8)])
                                + (Vf[pl.ds(s - 1, 8)] + Vf[pl.ds(s + 1, 8)])
                                + zs
                            )
                            emit(i * per * 40 + (p + lo + 1) * 40, t, ct, s, op(c[t], beside, G1f[pl.ds(s, 8)]))
                return 0

            lax.fori_loop(0, (hi - lo) // per, step, 0)

        first = W / (6.0 * 0.25)

        def put1(Df):
            def emit(x, t, ct, s, v):
                Df[pl.ds(s, 8)] = v

            return emit

        def two_relaxed(lo, hi, per):
            ring1(G1f, lambda a, beside, g: ((2.0 - W) * first) * a + (C6 * first) * beside, put1(WAf), lo, hi, per)

        def defect1(lo, hi, per):
            ring1(WAf, lambda a, beside, g: g - 0.25 * (6.0 * a - beside), put1(WBf), lo, hi, per)

        for m in near1:
            m.wait()
        for dx, m in msgs1:
            if dx == 0:
                m.wait_recv()
        for dy in (0, -1, 1):
            add_from(0, dy)
        two_relaxed(2, 30, 7)
        defect1(3, 29, 13)
        for m in side1:
            m.wait()
        for dx, m in msgs1:
            if dx:
                m.wait_recv()
        for dx, dy in XY:
            if dx:
                add_from(dx, dy)
        two_relaxed(-3, 2, 5)
        two_relaxed(30, 37, 7)
        defect1(-1, 3, 4)
        defect1(29, 32, 3)

        def restrict1(i, _):
            for t in range(2):
                for ct in range(2):
                    L[pl.ds(row(i * 16 + ct * 8), 8), t * 128 : t * 128 + 128] = restrict_xy(
                        WBf, (2 * i + (H1 - 1)) * PS1, PS1, t * RP1 + RO1 - 1 + 16 * ct
                    )
            return 0

        lax.fori_loop(0, 16, restrict1, 0)
        f, c = grid(256, 128)
        gap = jnp.abs(jnp.where(f < 192, f, f - 256) - 2 * c)
        R1 = jnp.where(c < 64, jnp.where(gap == 0, 0.5, jnp.where(gap == 1, 0.25, 0.0)), 0.0).astype(BF16)
        G2, VA, VB = b["G2"], b["VA"], b["VB"]
        G2f, VAf, VBf = flat(G2), flat(VA), flat(VB)
        res = exact_dot(L[0:256, :], R1)
        slot16 = lane // 16
        for x in range(16):
            for ct in range(2):
                G2[x + H2, RO2 + ct * 8 : RO2 + ct * 8 + 8] = res[x * 16 + ct * 8 : x * 16 + ct * 8 + 8]
        for grp in range(2):
            for ct in range(2):
                acc = zero
                for j in range(8):
                    v = res[(grp * 8 + j) * 16 + ct * 8 : (grp * 8 + j) * 16 + ct * 8 + 8]
                    v = jnp.where(lane < 8, v, pltpu.roll(v, 128 - 48, 1))
                    acc = jnp.where(slot16 == j, pltpu.roll(v, 16 * j, 1) if j else v, acc)
                b["PZ2"][grp, ct * 8 : ct * 8 + 8] = acc
        msgs2 = []
        def packed2(dx, dy):
            gs = along(GS2, dx)
            gd = along(GS2, dx, 1 - 2 * dx)
            yd = along(XS2, dy, 8 - N2 * dy)
            for side, dz in ((0, 1), (1, -1)):
                msgs2.append(post(b["PZ2"].at[gs, along(XS2, dy), :], b["RZ2"].at[side, gd, yd, :], (dx, dy, dz)))

        corners = [d for d in XY if d[0] and d[1]]
        for dx, dy in corners:
            packed2(dx, dy)
        for dx, dy in [d for d in XY8 if d not in corners] + corners:
            msgs2.append(
                post(
                    G2.at[along(XS2, dx, H2), along(XS2, dy, RO2), :],
                    G2.at[along(XS2, dx, H2 - N2 * dx), along(XS2, dy, RO2 - N2 * dy), :],
                    (dx, dy, 0),
                )
            )
        for dx, dy in [d for d in XY if d not in corners]:
            packed2(dx, dy)
        for m in msgs2:
            m.wait()

        first2 = W / (6.0 * 0.0625)

        def spread(grp, _):
            for ct in range(4):
                m = jnp.where(
                    jnp.bitwise_and(lane, 15) < 8,
                    b["RZ2"][1, grp, ct * 8 : ct * 8 + 8],
                    b["RZ2"][0, grp, ct * 8 : ct * 8 + 8],
                )
                for j in range(8):
                    hi = pltpu.roll(m, (64 - 16 * j) % 128, 1)
                    lo = pltpu.roll(m, 112 - 16 * j, 1) if j < 7 else m
                    r = pl.ds(row((grp * 8 + j) * RP2 + 8 + ct * 8), 8)
                    own = G2f[r]
                    v = jnp.where(lane < 64, own, jnp.where(lane < 72, hi, jnp.where(lane >= 120, lo, 0.0)))
                    G2f[r] = v
                    VAf[r] = first2 * v
            return 0

        lax.fori_loop(0, 4, spread, 0)

        def coarse(Sf, Tf, lo, n, per):
            def step(i, _):
                for p in range(per):
                    for ct in range(4):
                        q = row(i * per * RP2 + ((lo + p) * RP2 + 8 + ct * 8))
                        a = Sf[pl.ds(q, 8)]
                        beside = (
                            (Sf[pl.ds(q - RP2, 8)] + Sf[pl.ds(q + RP2, 8)])
                            + (Sf[pl.ds(q - 1, 8)] + Sf[pl.ds(q + 1, 8)])
                            + (pltpu.roll(a, 1, 1) + pltpu.roll(a, 127, 1))
                        )
                        Tf[pl.ds(q, 8)] = (1.0 - W) * a + (C6 * beside + first2 * G2f[pl.ds(q, 8)])
                return 0

            lax.fori_loop(0, n // per, step, 0)

        src, dst = VAf, VBf
        for lo, n, per in ((2, 28, 7), (2, 28, 7), (4, 24, 8), (4, 24, 8), (6, 20, 10)):
            coarse(src, dst, lo, n, per)
            src, dst = dst, src

        f, c = grid(128, 256)
        gap = jnp.abs(jnp.where(c < 192, c, c - 256) - 2 * jnp.where(f < 96, f, f - 128))
        P1 = jnp.where(gap == 0, 1.0, jnp.where(gap == 1, 0.5, 0.0)).astype(BF16)
        CZ1f, F1f = flat(b["CZ1"]), flat(b["F1"])
        for k in range(20):
            L[k * 24 : k * 24 + 24, 0:128] = src[pl.ds((k + 6) * RP2 + 12, 24)]
        res = exact_dot(L[0:480, 0:128], P1)
        for k in range(20):
            for t in range(2):
                b["CZ1"][k, t, 0:24] = res[k * 24 : k * 24 + 24, t * 128 : t * 128 + 128]

        def widen1(k, _):
            for t in range(2):
                for ct in range(3):
                    q = k * 64 + (t * 32 + ct * 8)
                    v, n = CZ1f[pl.ds(q, 8)], CZ1f[pl.ds(q + 1, 8)]
                    o = k * PS1 + (t * RP1 + 4 + 16 * ct)
                    F1f[pl.ds(o, 8, stride=2)] = v
                    F1f[pl.ds(o + 1, 8, stride=2)] = 0.5 * (v + n)
            return 0

        lax.fori_loop(0, 20, widen1, 0)

        def correct1(k, _):
            for t in range(2):
                for ct in range(5):
                    o = t * RP1 + 8 + ct * 8
                    v = F1f[pl.ds(row(k * PS1 + o), 8)]
                    n = F1f[pl.ds(row((k + 1) * PS1 + o), 8)]
                    q = row(2 * k * PS1 + o)
                    WAf[pl.ds(q, 8)] = WAf[pl.ds(q, 8)] + v
                    q = row((2 * k + 1) * PS1 + o)
                    WAf[pl.ds(q, 8)] = WAf[pl.ds(q, 8)] + 0.5 * (v + n)
            return 0

        lax.fori_loop(0, 20, correct1, 0)

        def relax1(a, beside, g):
            return (1.0 - W) * a + (C6 * beside + first * g)

        def put_l(r, t, ct, s, v):
            L[pl.ds(row(r + ct * 8), 8), t * 128 : t * 128 + 128] = v

        ring1(WAf, relax1, put1(WBf), -2, 34, 9)
        ring1(WBf, relax1, put_l, -1, 33, 17)

        f, c = grid(256, 384)
        gap = jnp.abs(jnp.where(c < 256, c, jnp.where(c == 383, 256, jnp.where(c == 256, -1, 9999))) - 2 * jnp.where(f < 192, f, f - 256))
        P0 = jnp.where(gap == 0, 1.0, jnp.where(gap == 1, 0.5, 0.0)).astype(BF16)
        CZ0f, F0f = flat(b["CZ0"]), flat(b["F0"])

        def pz0(i, _):
            res = exact_dot(L[pl.ds(row(i * 680), 680), :], P0)
            for p in range(17):
                for t in range(3):
                    CZ0f[pl.ds(row((i * 17 + p) * 144 + t * 48), 40)] = res[p * 40 : p * 40 + 40, t * 128 : t * 128 + 128]
            return 0

        lax.fori_loop(0, 2, pz0, 0)

        def widen0(k, _):
            for t in range(3):
                for ct in range(5):
                    q = k * 144 + (t * 48 + ct * 8)
                    v, n = CZ0f[pl.ds(q, 8)], CZ0f[pl.ds(q + 1, 8)]
                    o = k * 240 + (t * 80 + 16 * ct)
                    F0f[pl.ds(o, 8, stride=2)] = v
                    F0f[pl.ds(o + 1, 8, stride=2)] = 0.5 * (v + n)
            return 0

        lax.fori_loop(0, 34, widen0, 0)

        def add0(plane, t, r, v):
            q = pl.ds(row(plane * PS0 + t * RP0 + r), 8)
            Af[q] = Af[q] + v

        def get0(k, t, r):
            return F0f[pl.ds(row(k * 240 + t * 80 + r), 8)]

        for t in range(2):
            for r in range(8, 72, 8):
                add0(0, t, r, 0.5 * (get0(0, t, r) + get0(1, t, r)))
                add0(65, t, r, get0(33, t, r))

        def correct0(k, _):
            for i in (2 * k, 2 * k + 1):
                for t in range(2):
                    for r in range(0, 80, 8):
                        v, n = get0(i + 1, t, r), get0(i + 2, t, r)
                        add0(2 * i + 1, t, r, v)
                        add0(2 * i + 2, t, r, 0.5 * (v + n))
            for yt in range(8):
                place = 16 * yt if yt < 4 else 16 * (7 - yt) + 8
                h = b["HR"][2, 0, place : place + 8]
                for i in (2 * k, 2 * k + 1):
                    v, n = get0(i + 1, 2, 8 + yt * 8), get0(i + 2, 2, 8 + yt * 8)
                    for x, w in ((2 * i, v), (2 * i + 1, 0.5 * (v + n))):
                        h = h + jnp.where(half == x, pltpu.roll(w, jnp.bitwise_and(2 * x, 127), 1), 0.0)
                b["HR"][2, 0, place : place + 8] = h
            return 0

        lax.fori_loop(0, 16, correct0, 0)

        stencil(Af, Bf, 2, relax0, 3, taken=True)
        tile = total_wait(2, sum_msgs)
        mean = jnp.sum(tile, keepdims=True) / cells
        mean = jnp.broadcast_to(mean, (8, 128))
        stencil(Bf, None, 3, lambda c, beside, g: relax0(c, beside, g) - mean)

    return kernel, scratch


def solution(mesh):
    nx, ny, nz = (mesh.shape[a] for a in ("gx", "gy", "gz"))
    kernel, scratch = make_kernel(nx, ny, nz)

    def shards(right_side, initial_guess):
        assert right_side.shape == (64, 64, 256)
        return pl.pallas_call(
            kernel,
            out_shape=pltpu.VMEM(right_side.shape, F32),
            in_specs=[pl.BlockSpec(memory_space=pl.ANY)] * 2,
            out_specs=pl.BlockSpec(memory_space=pltpu.VMEM),
            scratch_shapes=scratch,
            compiler_params=pltpu.CompilerParams(collective_id=0, has_side_effects=True, vmem_limit_bytes=54 << 20),
        )(right_side, initial_guess)

    placed = P("gx", "gy", "gz")
    return jax.shard_map(shards, mesh=mesh, in_specs=(placed, placed), out_specs=placed, check_vma=False)
```

```python
import itertools

import jax
import jax.numpy as jnp
from jax import lax
from jax.experimental import pallas as pl
from jax.experimental.pallas import tpu as pltpu
from jax.sharding import PartitionSpec as P

F32 = jnp.float32
MESH = pl.DeviceIdType.MESH
COARSE_SWEEPS = 6
W = 0.8
C6 = W / 6.0
BF16 = jnp.bfloat16

N0, RP0 = 64, 96
PS0 = 2 * RP0
N1, H1, RP1, RO1 = 32, 4, 56, 12
PS1 = 2 * RP1
N2, H2, RP2, RO2 = 16, 8, 48, 16

XS1 = {1: (28, 5), 0: (0, 33), -1: (0, 4)}
GS1 = {1: (1, 2), 0: (0, 3), -1: (0, 1)}
XS2 = {1: (8, 8), 0: (0, 16), -1: (0, 8)}
GS2 = {1: (1, 1), 0: (0, 2), -1: (0, 1)}
PAD8 = {5: 8, 33: 40, 4: 8}
XY = [d for d in itertools.product((-1, 0, 1), repeat=2)]
XY8 = [d for d in XY if d != (0, 0)]
NEAR = [d for d in itertools.product((-1, 0, 1), repeat=3) if d != (0, 0, 0)]


def shift_weight():
    total = 0.0
    for level in range(2):
        total += 4 * W / (6.0 * 0.25**level)
    return total + COARSE_SWEEPS * W / (6.0 * 0.0625)


def make_kernel(nx, ny, nz):
    cells = float(nx * N0 * ny * N0 * nz * 256)
    peers = [d for d in NEAR if sum(map(abs, d)) == 1]
    ring = {0: [(0, 0, k) for k in range(1, nz)], 1: [(0, k, 0) for k in range(1, ny)], 2: [(k, 0, 0) for k in range(1, nx)]}
    n_sem = [0]

    scratch, names = [], []

    def vm(name, *shape):
        names.append(name)
        scratch.append(pltpu.VMEM(shape, F32))

    vm("A", 66, 2, RP0, 128)
    vm("B", 66, 2, RP0, 128)
    vm("C", 67, 2, RP0, 128)
    vm("G", 64, 2, 64, 128)
    vm("PK", 4, 64, 128)
    vm("HR", 4, 2, 64, 128)
    vm("L", 1360, 256)
    vm("G1", 42, 2, RP1, 128)
    vm("WA", 42, 2, RP1, 128)
    vm("WB", 42, 2, RP1, 128)
    vm("U", 3, 40, 128)
    vm("D", 3, 40, 128)
    vm("G2", 32, RP2, 128)
    vm("VA", 33, RP2, 128)
    vm("VB", 33, RP2, 128)
    vm("PZ2", 2, 16, 128)
    vm("RZ2", 2, 4, 32, 128)
    vm("CZ1", 21, 2, 32, 128)
    vm("F1", 21, 2, RP1, 128)
    vm("CZ0", 34, 3, 48, 128)
    vm("F0", 34, 3, 80, 128)
    vm("TS", 3, 8, 128)
    vm("TR0", max(nz - 1, 1), 8, 128)
    vm("TR1", max(ny - 1, 1), 8, 128)
    vm("TR2", max(nx - 1, 1), 8, 128)
    for dx, dy in XY8:
        vm(("RT", dx, dy), XS1[dx][1], PAD8[XS1[dy][1]], 128)
        vm(("RU0", dx, dy), GS1[dx][1], PAD8[XS1[dy][1]], 128)
    for dx, dy in XY:
        vm(("RU1", dx, dy), GS1[dx][1], PAD8[XS1[dy][1]], 128)
        vm(("RD", dx, dy), GS1[dx][1], PAD8[XS1[dy][1]], 128)
    N_MSG = 4 * 28 + 34 + 26 + (nx - 1) + (ny - 1) + (nz - 1)
    scratch += [pltpu.SemaphoreType.DMA((N_MSG,)), pltpu.SemaphoreType.DMA((N_MSG,)), pltpu.SemaphoreType.DMA((8,))]

    def kernel(g_hbm, v_hbm, out_ref, *refs):
        b = dict(zip(names, refs))
        send, recv, local = refs[len(names):]
        A, B, C, G = b["A"], b["B"], b["C"], b["G"]
        me = (lax.axis_index("gx"), lax.axis_index("gy"), lax.axis_index("gz"))
        sizes = (nx, ny, nz)
        lane = lax.broadcasted_iota(jnp.int32, (8, 128), 1)
        l0, l127 = lane == 0, lane == 127
        zero = jnp.zeros((8, 128), F32)
        used = [28 * 4]
        refs_of = {}

        def at(d):
            return tuple(lax.rem(m + (k + n), n) if k else m for m, k, n in zip(me, d, sizes))

        def post(src, dst, d):
            k = used[0]
            used[0] += 1
            c = pltpu.make_async_remote_copy(
                src_ref=src, dst_ref=dst, send_sem=send.at[k], recv_sem=recv.at[k], device_id=at(d), device_id_type=MESH
            )
            c.start()
            return c

        def flat(ref):
            s = ref.shape
            n = 1
            for k in s[:-1]:
                n *= k
            return ref.reshape(n, s[-1])

        def row(k, m=8):
            return pl.multiple_of(k, m)

        Af, Bf, Cf, Gf = flat(A), flat(B), flat(C), flat(G)
        refs_of.update({id(Af): A, id(Bf): B})
        G1f, WAf, WBf = flat(b["G1"]), flat(b["WA"]), flat(b["WB"])

        def clear(ref):
            f = flat(ref)
            n = f.shape[0] // 8
            per = 1
            for k in range(16, 0, -1):
                if n % k == 0:
                    per = k
                    break

            def step(i, _):
                for k in range(per):
                    f[pl.ds(row((i * per + k) * 8), 8)] = zero
                return 0

            lax.fori_loop(0, n // per, step, 0)

        barrier = pltpu.get_barrier_semaphore()
        for d in peers:
            pl.semaphore_signal(barrier, inc=1, device_id=at(d), device_id_type=MESH)
        loads = []
        for t in range(2):
            loads.append(pltpu.make_async_copy(v_hbm.at[:, :, t * 128 : t * 128 + 128], A.at[1:65, t, 8:72, :], local.at[t]))
            loads.append(pltpu.make_async_copy(g_hbm.at[:, :, t * 128 : t * 128 + 128], G.at[:, t, :, :], local.at[2 + t]))
        for k in (0, 2, 1, 3):
            loads[k].start()
        for name in names:
            if isinstance(name, tuple):
                clear(b[name])
        clear(b["G1"])
        for dst in (C.at[0], C.at[65], C.at[66]):
            clear(dst)

        def clear_rows(i, _):
            for t in range(2):
                for r in (0, 72, 80, 88):
                    Cf[pl.ds(row(i * PS0 + t * RP0 + r), 8)] = zero
            return 0

        lax.fori_loop(1, 65, clear_rows, 0)
        loads[0].wait()
        loads[2].wait()

        half = jnp.bitwise_and(lane + 1, 127) // 2

        def pair(c):
            return (c, 7 - c)

        def message(j, src, dst, d):
            return pltpu.make_async_remote_copy(
                src_ref=src, dst_ref=dst, send_sem=send.at[j], recv_sem=recv.at[j], device_id=at(d), device_id_type=MESH
            )

        def row_msgs(V, k, h):
            ps = slice(1 + 32 * h, 33 + 32 * h)
            return [
                message(28 * k + 24 + 2 * h, V.at[ps, :, 71:72, :], V.at[ps, :, 7:8, :], (0, 1, 0)),
                message(28 * k + 25 + 2 * h, V.at[ps, :, 8:9, :], V.at[ps, :, 72:73, :], (0, -1, 0)),
            ]

        def chunk_msgs(V, k, c):
            first_sem = 28 * k
            out = []

            def msg(j, src, dst, d):
                out.append(message(j, src, dst, d))

            for m, yt in enumerate(pair(c)):
                r = pl.ds(row(8 + yt * 8), 8)
                msg(first_sem + c * 6 + m, V.at[64, :, r, :], V.at[0, :, r, :], (1, 0, 0))
                msg(first_sem + c * 6 + 2 + m, V.at[1, :, r, :], V.at[65, :, r, :], (-1, 0, 0))
            r = pl.ds(row(c * 16, 16), 16)
            pk = b["PK"].at[k, r, :]
            msg(first_sem + c * 6 + 4, pk, b["HR"].at[k, 0, r, :], (0, 0, 1))
            msg(first_sem + c * 6 + 5, pk, b["HR"].at[k, 1, r, :], (0, 0, -1))
            return out

        odd = jnp.bitwise_and(lane, 1) == 1

        def take_chunk(V, k, c):
            for m in chunk_msgs(V, k, c):
                m.wait()
            for m in range(2):
                r = pl.ds(row(c * 16 + 8 * m), 8)
                b["HR"][k, 0, r] = jnp.where(odd, pltpu.roll(b["HR"][k, 1, r], 127, 1), pltpu.roll(b["HR"][k, 0, r], 1, 1))

        def put_faces(Df, k, blocks, c):
            for m, yt in enumerate(pair(c)):
                r = pl.ds(row(c * 16 + 8 * m), 8)
                keep = b["PK"][k, r]
                for i in blocks:
                    for p in range(16):
                        x = i * 16 + p
                        q = row((i * 16 + 1) * PS0 + 8 + yt * 8) + p * PS0
                        both = jnp.where(l0, Df[pl.ds(row(q), 8)], Df[pl.ds(row(q + RP0), 8)])
                        both = pltpu.roll(both, jnp.bitwise_and(2 * x, 127), 1)
                        keep = jnp.where(half == x, both, keep)
                b["PK"][k, r] = keep

        def stencil(Vf, Df, k, op, faces_to=None, carry=0, taken=False):
            summed = isinstance(carry, tuple)
            V, Dst = refs_of[id(Vf)], refs_of.get(id(Df))

            def chunk(c, carry):
                if not taken:
                    take_chunk(V, k, c)

                def step(i, carry):
                    base = row((i * 16 + 1) * PS0)
                    if faces_to is not None:
                        put_faces(Df, faces_to, (jnp.maximum(i - 1, 0),), c)
                    for m, yt in enumerate(pair(c)):
                        o = 8 + yt * 8
                        h = b["HR"][k, 0, pl.ds(row(c * 16 + 8 * m), 8)]

                        def get(p, t):
                            return Vf[pl.ds(row(base + o + (p * PS0 + t * RP0)), 8)]

                        below, mid = [get(-1, t) for t in range(2)], [get(0, t) for t in range(2)]
                        for p in range(16):
                            x = i * 16 + p
                            above = [get(p + 1, t) for t in range(2)]
                            e = pltpu.roll(h, jnp.bitwise_and(128 - 2 * x, 127), 1)
                            c0, c1 = mid
                            up0, up1, dn0, dn1 = (pltpu.roll(v, n, 1) for n in (1, 127) for v in (c0, c1))
                            zs = (
                                jnp.where(l0, e, up0) + jnp.where(l127, dn1, dn0),
                                jnp.where(l0, up0, up1) + jnp.where(l127, e, dn1),
                            )
                            for t in range(2):
                                q = base + o + (p * PS0 + t * RP0)
                                ys = Vf[pl.ds(q - 1, 8)] + Vf[pl.ds(q + 1, 8)]
                                beside = (below[t] + above[t]) + ys + zs[t]
                                g = Gf[pl.ds(row(x * 128 + t * 64 + yt * 8), 8)]
                                v = op(mid[t], beside, g)
                                if Df is None:
                                    out_ref[x, pl.ds(row(yt * 8), 8), t * 128 : t * 128 + 128] = v
                                else:
                                    Df[pl.ds(row(q), 8)] = v
                                if summed:
                                    carry = (carry[0] + mid[t], carry[1] + g)
                            below, mid = mid, above
                    return carry

                if isinstance(c, int):
                    for h in range(2):
                        if not taken:
                            for m in row_msgs(V, k, h):
                                m.wait()
                        carry = lax.fori_loop(2 * h, 2 * h + 2, step, carry)
                        if faces_to is not None:
                            for m in row_msgs(Dst, faces_to, h):
                                m.start()
                else:
                    carry = lax.fori_loop(0, 4, step, carry)
                if faces_to is not None:
                    put_faces(Df, faces_to, (3,), c)
                    for m in chunk_msgs(Dst, faces_to, c):
                        m.start()
                return carry

            return lax.fori_loop(1, 4, chunk, chunk(0, carry))

        def relax0(c, beside, g):
            return (1.0 - W) * c + C6 * (beside + g)

        def defect0(c, beside, g):
            return g - 6.0 * c + beside

        def total_stage(stage, tile):
            b["TS"][stage] = tile
            rec = b[f"TR{stage}"]
            return [post(b["TS"].at[stage], rec.at[j], d) for j, d in enumerate(ring[stage])]

        def total_wait(stage, msgs):
            tile = b["TS"][stage]
            for j, m in enumerate(msgs):
                m.wait()
                tile = tile + b[f"TR{stage}"][j]
            return tile

        def pack_first(n, _):
            i = jnp.bitwise_and(n, 1) * 2
            put_faces(Af, 0, (i, i + 1), n // 2)
            return 0

        lax.fori_loop(0, 8, pack_first, 0)
        pl.semaphore_wait(barrier, len(peers))
        for c in range(4):
            for m in chunk_msgs(A, 0, c):
                m.start()
            if c == 0:
                for m in row_msgs(A, 0, 0) + row_msgs(A, 0, 1):
                    m.start()
        loads[1].wait()
        loads[3].wait()
        sums = stencil(Af, Bf, 0, relax0, 1, (zero, zero))
        sum_msgs = total_stage(0, sums[0] + shift_weight() * sums[1])
        stencil(Bf, Af, 1, relax0, 2)
        sum_msgs = total_stage(1, total_wait(0, sum_msgs))

        stencil(Af, Cf, 2, defect0)

        L = b["L"]

        def restrict_xy(Df, plane, slab, start):
            rows = []
            for dp in range(3):
                q = plane + dp * slab + start
                lo, on, up = (Df[pl.ds(q + k, 8, stride=2)] for k in range(3))
                rows.append(0.25 * (lo + up) + 0.5 * on)
            return 0.25 * (rows[0] + rows[2]) + 0.5 * rows[1]

        def restrict0(i, _):
            for t in range(2):
                for ct in range(5):
                    L[pl.ds(row(i * 40 + ct * 8), 8), t * 128 : t * 128 + 128] = restrict_xy(
                        Cf, i * 2 * PS0, PS0, t * RP0 + 7 + 16 * ct
                    )
            return 0

        lax.fori_loop(0, 33, restrict0, 0)

        def exact_dot(x, weights):
            hi = x.astype(BF16)
            rest = x - hi.astype(F32)
            mid = rest.astype(BF16)
            lo = (rest - mid.astype(F32)).astype(BF16)
            return sum(jnp.dot(part, weights, preferred_element_type=F32) for part in (lo, mid, hi))

        def grid(rows, cols):
            return (
                lax.broadcasted_iota(jnp.int32, (rows, cols), 0),
                lax.broadcasted_iota(jnp.int32, (rows, cols), 1),
            )

        f, c = grid(256, 256)
        gap = jnp.abs(f - 2 * c)
        R0 = jnp.where(gap == 0, 0.5, jnp.where(gap == 1, 0.25, 0.0)).astype(BF16)

        def rz0(i, _):
            res = exact_dot(L[pl.ds(row(i * 440), 440), :], R0)
            for p in range(11):
                for t in range(2):
                    for ct in range(5):
                        G1f[pl.ds((i * 11 + (p + H1)) * PS1 + (t * RP1 + RO1 + ct * 8), 8)] = res[
                            p * 40 + ct * 8 : p * 40 + ct * 8 + 8, t * 128 : t * 128 + 128
                        ]
            return 0

        lax.fori_loop(0, 3, rz0, 0)

        slot8 = lane // 8
        for grp in range(3):
            for ct in range(5):
                up = dn = zero
                for j in range(16 if grp < 2 else 1):
                    q = (grp * 16 + j + H1) * PS1 + RO1 + ct * 8
                    t0, e = G1f[q : q + 8], G1f[q + RP1 : q + RP1 + 8]
                    up = jnp.where(slot8 == j, pltpu.roll(jnp.where(l0, e, t0), (4 + 8 * j) % 128, 1), up)
                    dn = jnp.where(slot8 == j, pltpu.roll(t0, 8 * j, 1) if j else t0, dn)
                b["U"][grp, ct * 8 : ct * 8 + 8] = up
                b["D"][grp, ct * 8 : ct * 8 + 8] = dn
        G1 = b["G1"]
        msgs1 = []
        near1, side1 = [], []

        def along(spec, k, off=0):
            return slice(spec[k][0] + off, spec[k][0] + off + spec[k][1])

        def packed1(dx, dy):
            n = XS1[dy][1]
            ys, gs = along(XS1, dy), along(GS1, dx)
            to = side1 if dx else near1
            to.append(post(b["U"].at[gs, ys, :], b["RU1", dx, dy].at[:, 0:n, :], (dx, dy, 1)))
            to.append(post(b["D"].at[gs, ys, :], b["RD", dx, dy].at[:, 0:n, :], (dx, dy, -1)))

        corners = [d for d in XY if d[0] and d[1]]
        for dx, dy in corners:
            packed1(dx, dy)
        for dx, dy in [d for d in XY8 if d not in corners] + corners:
            n = XS1[dy][1]
            msgs1.append((dx,
                post(G1.at[along(XS1, dx, H1), 0, along(XS1, dy, RO1), :], b["RT", dx, dy].at[:, 0:n, :], (dx, dy, 0))
            ))
        for dx, dy in [d for d in XY if d not in corners]:
            packed1(dx, dy)
        for dx, dy in XY8:
            n = XS1[dy][1]
            (side1 if dx else near1).append(
                post(b["U"].at[along(GS1, dx), along(XS1, dy), :], b["RU0", dx, dy].at[:, 0:n, :], (dx, dy, 0))
            )
        sum_msgs = total_stage(2, total_wait(1, sum_msgs))
        for dx, m in msgs1:
            m.wait_send()

        def add1(q, v):
            G1f[pl.ds(q, 8)] = G1f[pl.ds(q, 8)] + v

        def add_from(dx, dy):
            sx, n = XS1[dx]
            sy = XS1[dy][0]
            tiles = PAD8[XS1[dy][1]] // 8
            g0 = GS1[dx][0]
            per = 11 if n == 33 else n

            def unpack(i, _, dx=dx, dy=dy, sx=sx, sy=sy, tiles=tiles, g0=g0, per=per):
                for p in range(per):
                    k = i * per + p
                    s = k + sx
                    grp, j = s // 16 - g0, s % 16 if isinstance(s, int) else jnp.bitwise_and(s, 15)
                    up = (124 - 8 * j) % 128 if isinstance(s, int) else jnp.bitwise_and(124 - 8 * j, 127)
                    down = (128 - 8 * j) % 128 if isinstance(s, int) else jnp.bitwise_and(128 - 8 * j, 127)
                    for ct in range(tiles):
                        q = i * per * PS1 + ((p + (sx - N1 * dx + H1)) * PS1 + (sy - N1 * dy + RO1 + ct * 8))
                        u1 = pltpu.roll(b["RU1", dx, dy][grp, ct * 8 : ct * 8 + 8], up, 1)
                        dn = pltpu.roll(b["RD", dx, dy][grp, ct * 8 : ct * 8 + 8], down, 1)
                        e = jnp.where(lane >= 124, u1, jnp.where(lane < 4, dn, 0.0))
                        t0 = jnp.where(l0, u1, 0.0)
                        if (dx, dy) != (0, 0):
                            u0 = pltpu.roll(b["RU0", dx, dy][grp, ct * 8 : ct * 8 + 8], up, 1)
                            e = e + jnp.where(l0, u0, 0.0)
                            t0 = t0 + b["RT", dx, dy][k, ct * 8 : ct * 8 + 8]
                        add1(q, t0)
                        add1(q + RP1, e)
                return 0

            if n == 33:
                lax.fori_loop(0, 3, unpack, 0)
            else:
                unpack(0, 0)

        def ring1(Vf, op, emit, lo, hi, per):

            def step(i, _):
                for p in range(per):
                    base = i * per * PS1
                    for ct in range(5):
                        q = row(base + ((p + lo + H1) * PS1 + 8 + ct * 8))
                        c = (Vf[pl.ds(q, 8)], Vf[pl.ds(q + RP1, 8)])
                        up = [pltpu.roll(v, 1, 1) for v in c]
                        dn = [pltpu.roll(v, 127, 1) for v in c]
                        for t in range(2):
                            zs = jnp.where(l0, up[1 - t], up[t]) + jnp.where(l127, dn[1 - t], dn[t])
                            s = q + t * RP1
                            beside = (
                                (Vf[pl.ds(s - PS1, 8)] + Vf[pl.ds(s + PS1, 8)])
                                + (Vf[pl.ds(s - 1, 8)] + Vf[pl.ds(s + 1, 8)])
                                + zs
                            )
                            emit(i * per * 40 + (p + lo + 1) * 40, t, ct, s, op(c[t], beside, G1f[pl.ds(s, 8)]))
                return 0

            lax.fori_loop(0, (hi - lo) // per, step, 0)

        first = W / (6.0 * 0.25)

        def put1(Df):
            def emit(x, t, ct, s, v):
                Df[pl.ds(s, 8)] = v

            return emit

        def two_relaxed(lo, hi, per):
            ring1(G1f, lambda a, beside, g: ((2.0 - W) * first) * a + (C6 * first) * beside, put1(WAf), lo, hi, per)

        def defect1(lo, hi, per):
            ring1(WAf, lambda a, beside, g: g - 0.25 * (6.0 * a - beside), put1(WBf), lo, hi, per)

        for m in near1:
            m.wait()
        for dx, m in msgs1:
            if dx == 0:
                m.wait_recv()
        for dy in (0, -1, 1):
            add_from(0, dy)
        two_relaxed(2, 30, 7)
        defect1(3, 29, 13)
        for m in side1:
            m.wait()
        for dx, m in msgs1:
            if dx:
                m.wait_recv()
        for dx, dy in XY:
            if dx:
                add_from(dx, dy)
        two_relaxed(-3, 2, 5)
        two_relaxed(30, 37, 7)
        defect1(-1, 3, 4)
        defect1(29, 32, 3)

        def restrict1(i, _):
            for t in range(2):
                for ct in range(2):
                    L[pl.ds(row(i * 16 + ct * 8), 8), t * 128 : t * 128 + 128] = restrict_xy(
                        WBf, (2 * i + (H1 - 1)) * PS1, PS1, t * RP1 + RO1 - 1 + 16 * ct
                    )
            return 0

        lax.fori_loop(0, 16, restrict1, 0)
        f, c = grid(256, 128)
        gap = jnp.abs(jnp.where(f < 192, f, f - 256) - 2 * c)
        R1 = jnp.where(c < 64, jnp.where(gap == 0, 0.5, jnp.where(gap == 1, 0.25, 0.0)), 0.0).astype(BF16)
        G2, VA, VB = b["G2"], b["VA"], b["VB"]
        G2f, VAf, VBf = flat(G2), flat(VA), flat(VB)
        res = exact_dot(L[0:256, :], R1)
        slot16 = lane // 16
        for x in range(16):
            for ct in range(2):
                G2[x + H2, RO2 + ct * 8 : RO2 + ct * 8 + 8] = res[x * 16 + ct * 8 : x * 16 + ct * 8 + 8]
        for grp in range(2):
            for ct in range(2):
                acc = zero
                for j in range(8):
                    v = res[(grp * 8 + j) * 16 + ct * 8 : (grp * 8 + j) * 16 + ct * 8 + 8]
                    v = jnp.where(lane < 8, v, pltpu.roll(v, 128 - 48, 1))
                    acc = jnp.where(slot16 == j, pltpu.roll(v, 16 * j, 1) if j else v, acc)
                b["PZ2"][grp, ct * 8 : ct * 8 + 8] = acc
        msgs2 = []
        def packed2(dx, dy):
            gs = along(GS2, dx)
            gd = along(GS2, dx, 1 - 2 * dx)
            yd = along(XS2, dy, 8 - N2 * dy)
            for side, dz in ((0, 1), (1, -1)):
                msgs2.append((dx, post(b["PZ2"].at[gs, along(XS2, dy), :], b["RZ2"].at[side, gd, yd, :], (dx, dy, dz))))

        corners = [d for d in XY if d[0] and d[1]]
        for dx, dy in corners:
            packed2(dx, dy)
        for dx, dy in [d for d in XY8 if d not in corners] + corners:
            msgs2.append((dx,
                post(
                    G2.at[along(XS2, dx, H2), along(XS2, dy, RO2), :],
                    G2.at[along(XS2, dx, H2 - N2 * dx), along(XS2, dy, RO2 - N2 * dy), :],
                    (dx, dy, 0),
                )
            ))
        for dx, dy in [d for d in XY if d not in corners]:
            packed2(dx, dy)
        for dx, m in msgs2:
            m.wait_send()
        for dx, m in msgs2:
            if dx == 0:
                m.wait_recv()

        first2 = W / (6.0 * 0.0625)

        def spread(grp, _):
            for ct in range(4):
                m = jnp.where(
                    jnp.bitwise_and(lane, 15) < 8,
                    b["RZ2"][1, grp, ct * 8 : ct * 8 + 8],
                    b["RZ2"][0, grp, ct * 8 : ct * 8 + 8],
                )
                for j in range(8):
                    hi = pltpu.roll(m, (64 - 16 * j) % 128, 1)
                    lo = pltpu.roll(m, 112 - 16 * j, 1) if j < 7 else m
                    r = pl.ds(row((grp * 8 + j) * RP2 + 8 + ct * 8), 8)
                    own = G2f[r]
                    v = jnp.where(lane < 64, own, jnp.where(lane < 72, hi, jnp.where(lane >= 120, lo, 0.0)))
                    G2f[r] = v
                    VAf[r] = first2 * v
            return 0

        lax.fori_loop(1, 3, spread, 0)

        def coarse(Sf, Tf, lo, n, per):
            def step(i, _):
                for p in range(per):
                    for ct in range(4):
                        q = row(i * per * RP2 + ((lo + p) * RP2 + 8 + ct * 8))
                        a = Sf[pl.ds(q, 8)]
                        beside = (
                            (Sf[pl.ds(q - RP2, 8)] + Sf[pl.ds(q + RP2, 8)])
                            + (Sf[pl.ds(q - 1, 8)] + Sf[pl.ds(q + 1, 8)])
                            + (pltpu.roll(a, 1, 1) + pltpu.roll(a, 127, 1))
                        )
                        Tf[pl.ds(q, 8)] = (1.0 - W) * a + (C6 * beside + first2 * G2f[pl.ds(q, 8)])
                return 0

            lax.fori_loop(0, n // per, step, 0)

        src, dst = VAf, VBf
        coarse(src, dst, 9, 14, 14)
        for dx, m in msgs2:
            if dx:
                m.wait_recv()
        spread(0, 0)
        spread(3, 0)
        coarse(src, dst, 2, 7, 7)
        coarse(src, dst, 23, 7, 7)
        src, dst = dst, src
        for lo, n, per in ((2, 28, 7), (4, 24, 8), (4, 24, 8), (6, 20, 10)):
            coarse(src, dst, lo, n, per)
            src, dst = dst, src

        f, c = grid(128, 256)
        gap = jnp.abs(jnp.where(c < 192, c, c - 256) - 2 * jnp.where(f < 96, f, f - 128))
        P1 = jnp.where(gap == 0, 1.0, jnp.where(gap == 1, 0.5, 0.0)).astype(BF16)
        CZ1f, F1f = flat(b["CZ1"]), flat(b["F1"])
        for k in range(20):
            L[k * 24 : k * 24 + 24, 0:128] = src[pl.ds((k + 6) * RP2 + 12, 24)]
        res = exact_dot(L[0:480, 0:128], P1)
        for k in range(20):
            for t in range(2):
                b["CZ1"][k, t, 0:24] = res[k * 24 : k * 24 + 24, t * 128 : t * 128 + 128]

        def widen1(k, _):
            for t in range(2):
                for ct in range(3):
                    q = k * 64 + (t * 32 + ct * 8)
                    v, n = CZ1f[pl.ds(q, 8)], CZ1f[pl.ds(q + 1, 8)]
                    o = k * PS1 + (t * RP1 + 4 + 16 * ct)
                    F1f[pl.ds(o, 8, stride=2)] = v
                    F1f[pl.ds(o + 1, 8, stride=2)] = 0.5 * (v + n)
            return 0

        lax.fori_loop(0, 20, widen1, 0)

        def correct1(k, _):
            for t in range(2):
                for ct in range(5):
                    o = t * RP1 + 8 + ct * 8
                    v = F1f[pl.ds(row(k * PS1 + o), 8)]
                    n = F1f[pl.ds(row((k + 1) * PS1 + o), 8)]
                    q = row(2 * k * PS1 + o)
                    WAf[pl.ds(q, 8)] = WAf[pl.ds(q, 8)] + v
                    q = row((2 * k + 1) * PS1 + o)
                    WAf[pl.ds(q, 8)] = WAf[pl.ds(q, 8)] + 0.5 * (v + n)
            return 0

        lax.fori_loop(0, 20, correct1, 0)

        def relax1(a, beside, g):
            return (1.0 - W) * a + (C6 * beside + first * g)

        def put_l(r, t, ct, s, v):
            L[pl.ds(row(r + ct * 8), 8), t * 128 : t * 128 + 128] = v

        ring1(WAf, relax1, put1(WBf), -2, 34, 9)
        ring1(WBf, relax1, put_l, -1, 33, 17)

        f, c = grid(256, 384)
        gap = jnp.abs(jnp.where(c < 256, c, jnp.where(c == 383, 256, jnp.where(c == 256, -1, 9999))) - 2 * jnp.where(f < 192, f, f - 256))
        P0 = jnp.where(gap == 0, 1.0, jnp.where(gap == 1, 0.5, 0.0)).astype(BF16)
        CZ0f, F0f = flat(b["CZ0"]), flat(b["F0"])

        def pz0(i, _):
            res = exact_dot(L[pl.ds(row(i * 680), 680), :], P0)
            for p in range(17):
                for t in range(3):
                    CZ0f[pl.ds(row((i * 17 + p) * 144 + t * 48), 40)] = res[p * 40 : p * 40 + 40, t * 128 : t * 128 + 128]
            return 0

        lax.fori_loop(0, 2, pz0, 0)

        def widen0(k, _):
            for t in range(3):
                for ct in range(5):
                    q = k * 144 + (t * 48 + ct * 8)
                    v, n = CZ0f[pl.ds(q, 8)], CZ0f[pl.ds(q + 1, 8)]
                    o = k * 240 + (t * 80 + 16 * ct)
                    F0f[pl.ds(o, 8, stride=2)] = v
                    F0f[pl.ds(o + 1, 8, stride=2)] = 0.5 * (v + n)
            return 0

        lax.fori_loop(0, 34, widen0, 0)

        def add0(plane, t, r, v):
            q = pl.ds(row(plane * PS0 + t * RP0 + r), 8)
            Af[q] = Af[q] + v

        def get0(k, t, r):
            return F0f[pl.ds(row(k * 240 + t * 80 + r), 8)]

        for t in range(2):
            for r in range(8, 72, 8):
                add0(0, t, r, 0.5 * (get0(0, t, r) + get0(1, t, r)))
                add0(65, t, r, get0(33, t, r))

        def correct0(k, _):
            for i in (2 * k, 2 * k + 1):
                for t in range(2):
                    for r in range(0, 80, 8):
                        v, n = get0(i + 1, t, r), get0(i + 2, t, r)
                        add0(2 * i + 1, t, r, v)
                        add0(2 * i + 2, t, r, 0.5 * (v + n))
            for yt in range(8):
                place = 16 * yt if yt < 4 else 16 * (7 - yt) + 8
                h = b["HR"][2, 0, place : place + 8]
                for i in (2 * k, 2 * k + 1):
                    v, n = get0(i + 1, 2, 8 + yt * 8), get0(i + 2, 2, 8 + yt * 8)
                    for x, w in ((2 * i, v), (2 * i + 1, 0.5 * (v + n))):
                        h = h + jnp.where(half == x, pltpu.roll(w, jnp.bitwise_and(2 * x, 127), 1), 0.0)
                b["HR"][2, 0, place : place + 8] = h
            return 0

        lax.fori_loop(0, 16, correct0, 0)

        stencil(Af, Bf, 2, relax0, 3, taken=True)
        tile = total_wait(2, sum_msgs)
        mean = jnp.sum(tile, keepdims=True) / cells
        mean = jnp.broadcast_to(mean, (8, 128))
        stencil(Bf, None, 3, lambda c, beside, g: relax0(c, beside, g) - mean)

    return kernel, scratch


def solution(mesh):
    nx, ny, nz = (mesh.shape[a] for a in ("gx", "gy", "gz"))
    kernel, scratch = make_kernel(nx, ny, nz)

    def shards(right_side, initial_guess):
        assert right_side.shape == (64, 64, 256)
        return pl.pallas_call(
            kernel,
            out_shape=pltpu.VMEM(right_side.shape, F32),
            in_specs=[pl.BlockSpec(memory_space=pl.ANY)] * 2,
            out_specs=pl.BlockSpec(memory_space=pltpu.VMEM),
            scratch_shapes=scratch,
            compiler_params=pltpu.CompilerParams(collective_id=0, has_side_effects=True, vmem_limit_bytes=54 << 20),
        )(right_side, initial_guess)

    placed = P("gx", "gy", "gz")
    return jax.shard_map(shards, mesh=mesh, in_specs=(placed, placed), out_specs=placed, check_vma=False)
```
